32 devices in a mesh: wide: 8 (over z, x), narrow: 4 (over y, core).
Axes of the slice: x: 2, y: 2, z: 4, core: 2. Of those that a mesh axis runs over, the one named last changes fastest.
Arguments:
- stream_one: bfloat16 [12288, 1024], P(('wide', 'narrow')), may hold values from -6 to 6
- stream_two: bfloat16 [12288, 1024], P(('wide', 'narrow')), may hold values from -6 to 6
- attention_gain: float32 [1024], replicated, may hold values from 0.5 to 1.5
- attention_shift: float32 [1024], replicated, may hold values from -1.8 to 1.8
- query_proj: bfloat16 [1024, 1024], P(None, 'narrow'), may hold values from -3.59375 to 3.59375
- value_proj: bfloat16 [1024, 1024], P(None, 'narrow'), may hold values from -0.1875 to 0.1875
- output_proj: bfloat16 [1024, 1024], P('narrow'), may hold values from -0.375 to 0.375
- forward_gain: float32 [1024], replicated, may hold values from 0.5 to 1.5
- forward_shift: float32 [1024], replicated, may hold values from -1.8 to 1.8
- up_proj: bfloat16 [1024, 4096], P(None, 'narrow'), may hold values from -0.1875 to 0.1875
- up_bias: float32 [4096], P('narrow'), may hold values from -1.8 to 1.8
- down_proj: bfloat16 [4096, 1024], P('narrow'), may hold values from -0.125 to 0.125
- down_bias: float32 [1024], replicated, may hold values from -1.8 to 1.8
- bucket_ids: int32 [12288, 4], P(('wide', 'narrow')), may hold values from 0 to 23
- sort_orders: int32 [8, 4, 1536], P('wide'), may hold values from 0 to 1535, as said below
- doc_lengths: int32 [8, 8], P('wide'), may hold values from 1 to 768, 1536 in all within a row
- cotan_one: bfloat16 [12288, 1024], P(('wide', 'narrow'))
- cotan_two: bfloat16 [12288, 1024], P(('wide', 'narrow'))
Outputs:
- output_one: bfloat16 [12288, 1024], P(('wide', 'narrow'))
- output_two: bfloat16 [12288, 1024], P(('wide', 'narrow'))
- grad_one: bfloat16 [12288, 1024], P(('wide', 'narrow'))
- grad_two: bfloat16 [12288, 1024], P(('wide', 'narrow'))
- grad_attention_gain: float32 [1024], replicated
- grad_attention_shift: float32 [1024], replicated
- grad_query_proj: float32 [1024, 1024], P(None, 'narrow')
- grad_value_proj: float32 [1024, 1024], P(None, 'narrow')
- grad_output_proj: float32 [1024, 1024], P('narrow')
- grad_forward_gain: float32 [1024], replicated
- grad_forward_shift: float32 [1024], replicated
- grad_up_proj: float32 [1024, 4096], P(None, 'narrow')
- grad_up_bias: float32 [4096], P('narrow')
- grad_down_proj: float32 [4096, 1024], P('narrow')
- grad_down_bias: float32 [1024], replicated
- bucket_counts: int32 [4, 24], replicated
The draws below stay inside these ranges and needn't reach their ends.
Inputs may be any that keep to these rules, and one draw needn't show every extreme that they name: sort_orders[s, r] lists the 1536 positions of sequence s by increasing bucket of round r, ties by position. `doc_lengths`: the 8 documents of a sequence fill its 1536 positions in order.
All inputs are finite; a program needn't handle non-finite values.
Results may differ from the reference program's by a relative error of at most 0.019.
Values may be sent and summed in bfloat16 or wider, within the bound.
A program may use at most 256 MiB of HBM per device.

```python
import math
import jax
import jax.numpy as jnp
import numpy as np
from jax import lax

D = 1024
FF = 4096
HD = 128
ROUNDS = 4
GROUP = 64
DOCS = 8
SEQ = 1536
SEQS = 8
TOKENS = 12288
NB = 24
MOST = 768


def bucket_table(key):
    return jax.random.randint(jax.random.fold_in(key, 11), (TOKENS, ROUNDS), 0, NB, dtype=jnp.int32)


def draw_bucket_ids(key, part):
    return bucket_table(key)


def draw_sort_orders(key, part):
    table = bucket_table(key).reshape(SEQS, SEQ, ROUNDS)
    ranking = jnp.transpose(table, (0, 2, 1)) * SEQ + jnp.arange(SEQ, dtype=jnp.int32)
    return jnp.argsort(ranking, axis=-1).astype(jnp.int32)


def ramp_rows(key):
    rows = jnp.arange(TOKENS, dtype=jnp.float32)[:, None] / TOKENS
    base = jax.random.normal(key, (TOKENS, D), jnp.float32)
    return base * (1.0 + rows)


def draw_cotan_one(key, part):
    return ramp_rows(jax.random.fold_in(key, 21)).astype(jnp.bfloat16)


def draw_cotan_two(key, part):
    return ramp_rows(jax.random.fold_in(key, 22)).astype(jnp.bfloat16)


def steps_of(stream_key, dims, shards, low, largest):
    def one(axis_at, parts):
        steps = jax.random.uniform(jax.random.fold_in(jax.random.fold_in(stream_key, 6), axis_at), (parts,), jnp.float32, low / len(shards), largest / len(shards))
        return jnp.repeat(jnp.exp(steps), dims[axis_at] // parts).reshape((-1,) + (1,) * (len(dims) - axis_at - 1))

    factor_of = one(*shards[0])
    for cut in shards[1:]:
        factor_of = factor_of * one(*cut)
    return factor_of


def profile(number_of, total, bound, lean):
    weights = [(1 << 20) // math.isqrt(standing ** lean) + 1 for standing in range(2, number_of + 1)]
    rest, given = total - bound - (number_of - 1), [1] * (number_of - 1)
    while rest > 0:
        candidates = [i for i in range(number_of - 1) if given[i] < bound]
        whole, remaining = sum([weights[i] for i in candidates]), rest
        for i in candidates:
            addition = min(bound - given[i], max(1, remaining * weights[i] // whole), rest)
            given[i] = given[i] + addition
            rest = rest - addition
    return np.array([bound] + given)


def ragged_sizes(own_key, amount, total, most, lean):
    if amount == 2:
        one = jax.random.randint(own_key, (), max(1, total - most), min(most, total - 1) + 1)
        return jnp.stack([one, total - one])
    lengths = jnp.asarray(profile(amount, total, most, lean), jnp.int32)
    pairs = (amount - 1) // 2
    giver, sink = lengths[1:1 + 2 * pairs:2], lengths[2:2 + 2 * pairs:2]
    slack = jnp.minimum(giver - 1, most - sink)
    moved = jax.random.randint(jax.random.fold_in(own_key, 1), (pairs,), 0, 1 << 20) % (slack + 1)
    lengths = lengths.at[1:1 + 2 * pairs:2].set(giver - moved).at[2:2 + 2 * pairs:2].set(sink + moved)
    return lengths[jax.random.permutation(jax.random.fold_in(own_key, 2), amount)]


def centred(stream_key, shape, spread, limit, cuts=(), kind=jnp.bfloat16):
    result = jax.random.normal(stream_key, shape, jnp.float32) * spread
    if len(cuts) > 0:
        result = steps_of(stream_key, shape, cuts, -0.22, 0.18) * result
    return jnp.clip(result, min=-limit, max=limit).astype(kind)


def setup_inputs(seed: int = 0) -> dict:
    key_list = jax.random.split(jax.random.key(seed), 19)
    return {
        "stream_one": centred(key_list[0], (TOKENS, D), 1.0, 6.0, ((0, 32),)),
        "stream_two": centred(key_list[1], (TOKENS, D), 1.0, 6.0, ((0, 32),)),
        "attention_gain": jnp.clip(1.0 + 0.1 * jax.random.normal(key_list[2], (D,), jnp.float32), 0.5, 1.5),
        "attention_shift": centred(key_list[3], (D,), 0.3, 1.8, (), jnp.float32),
        "query_proj": centred(key_list[4], (D, D), 0.6, 3.59375, ((1, 4),)),
        "value_proj": centred(key_list[5], (D, D), D ** -0.5, 0.1875, ((1, 4),)),
        "output_proj": centred(key_list[6], (D, D), (D // 4) ** -0.5, 0.375, ((0, 4),)),
        "forward_gain": jnp.clip(1.0 + 0.1 * jax.random.normal(key_list[7], (D,), jnp.float32), 0.5, 1.5),
        "forward_shift": centred(key_list[8], (D,), 0.3, 1.8, (), jnp.float32),
        "up_proj": centred(key_list[9], (D, FF), D ** -0.5, 0.1875, ((1, 4),)),
        "up_bias": centred(key_list[10], (FF,), 0.3, 1.8, ((0, 4),), jnp.float32),
        "down_proj": centred(key_list[11], (FF, D), (FF // 2) ** -0.5, 0.125, ((0, 4),)),
        "down_bias": centred(key_list[12], (D,), 0.3, 1.8, (), jnp.float32),
        "bucket_ids": draw_bucket_ids(jax.random.fold_in(key_list[18], 71), 0),
        "sort_orders": draw_sort_orders(jax.random.fold_in(key_list[18], 71), 0),
        "doc_lengths": jax.vmap(lambda own: ragged_sizes(own, DOCS, SEQ, MOST, 2))(jax.random.split(key_list[15], SEQS)).reshape((SEQS, DOCS)).astype(jnp.int32),
        "cotan_one": draw_cotan_one(jax.random.fold_in(key_list[18], 71), 0),
        "cotan_two": draw_cotan_two(jax.random.fold_in(key_list[18], 71), 0),
    }


HIGHEST = lax.Precision.HIGHEST

@jax.custom_vjp
def low(v):
    return lax.optimization_barrier(v.astype(jnp.bfloat16)).astype(jnp.float32)

@jax.custom_vjp
def low_back(v):
    return v

def low_keep(v):
    return (low(v), None)

def low_pass(kept, grad):
    return (grad,)

def back_keep(v):
    return (v, None)

def back_low(kept, grad):
    return (low(grad),)
low.defvjp(low_keep, low_pass)
low_back.defvjp(back_keep, back_low)

def both_ways(value):
    return low(low_back(value))

def layer_norm(inputs, gain, offset):
    center = inputs - lax.optimization_barrier(jnp.mean(inputs, axis=-1, keepdims=True))
    scaled = center * lax.rsqrt(lax.optimization_barrier(jnp.mean(center * center, axis=-1, keepdims=True)) + 1e-05)
    return scaled * gain + offset

def window_of(blocks):
    return jnp.concatenate([jnp.roll(blocks, 1, axis=0), blocks], axis=1)

def one_round(queries, key_rows, value_rows, ordering, segment):
    length = queries.shape[0]
    blocks = length // GROUP
    head_count = queries.shape[1]
    factor = 1.0 / math.sqrt(HD)
    query_sorted = queries[ordering].reshape(blocks, GROUP, head_count, HD)
    key_window = window_of(key_rows[ordering].reshape(blocks, GROUP, head_count, HD))
    value_window = window_of(value_rows[ordering].reshape(blocks, GROUP, head_count, HD))
    pos_rows = ordering.reshape(blocks, GROUP)
    pos_window = window_of(pos_rows)
    seg_rows = segment[ordering].reshape(blocks, GROUP)
    seg_window = window_of(seg_rows)
    allowed = (seg_window[:, None, :] == seg_rows[:, :, None]) & (pos_window[:, None, :] <= pos_rows[:, :, None])
    itself = pos_window[:, None, :] == pos_rows[:, :, None]
    scores = jnp.einsum('cihd,cjhd->chij', query_sorted, key_window, precision=HIGHEST) * factor
    scores = low_back(scores)
    scores = jnp.where(itself[:, None], -100000.0, scores)
    scores = jnp.where(allowed[:, None], scores, -1000000000.0)
    row_max = lax.optimization_barrier(jnp.max(scores, axis=-1, keepdims=True))
    powers = jnp.exp(scores - row_max)
    row_total = lax.optimization_barrier(jnp.sum(powers, axis=-1, keepdims=True))
    log_total = row_max + jnp.log(row_total)
    probabilities = low(powers / row_total)
    mixture = jnp.einsum('chij,cjhd->cihd', probabilities, value_window, precision=HIGHEST)
    mixture = mixture.reshape(length, head_count, HD)
    log_sums = jnp.transpose(log_total[..., 0], (0, 2, 1)).reshape(length, head_count)
    inverse = jnp.zeros((length,), jnp.int32).at[ordering].set(jnp.arange(length, dtype=jnp.int32))
    return (mixture[inverse], log_sums[inverse])

def attention(inputs, gain, offset, query_proj, value_proj, output_proj, orderings, segment):
    length = inputs.shape[0]
    head_count = query_proj.shape[1] // HD
    normed = low(layer_norm(inputs, gain, offset))
    queries = both_ways(jnp.dot(normed, query_proj, precision=HIGHEST)).reshape(length, head_count, HD)
    unit_keys = low(queries * lax.rsqrt(lax.optimization_barrier(jnp.sum(queries * queries, axis=-1, keepdims=True)) + 1e-06))
    value_rows = both_ways(jnp.dot(normed, value_proj, precision=HIGHEST)).reshape(length, head_count, HD)
    outputs = []
    sums_list = []
    for hashing in range(ROUNDS):
        mixture, log_sums = jax.checkpoint(one_round)(queries, unit_keys, value_rows, orderings[hashing], segment)
        outputs.append(low_back(mixture))
        sums_list.append(log_sums)
    stacked = jnp.stack(sums_list)
    round_peak = lax.optimization_barrier(jnp.max(stacked, axis=0, keepdims=True))
    shares = jnp.exp(stacked - round_peak)
    shares = shares / lax.optimization_barrier(jnp.sum(shares, axis=0, keepdims=True))
    merged = lax.optimization_barrier(jnp.sum(shares[..., None] * jnp.stack(outputs), axis=0)).reshape(length, head_count * HD)
    return low_back(jnp.dot(both_ways(merged), output_proj, precision=HIGHEST))

def feed_forward(inputs, gain, offset, up_proj, up_bias, down_proj, down_bias):
    normed = low(layer_norm(inputs, gain, offset))
    hidden = low_back(jnp.dot(normed, up_proj, precision=HIGHEST) + up_bias)
    active = low(jax.nn.gelu(hidden, approximate=True))
    return low_back(jnp.dot(active, down_proj, precision=HIGHEST) + down_bias)

def block_layer(first_rows, second_rows, weights, orderings, segment):
    middle = first_rows + attention(second_rows, weights[0], weights[1], weights[2], weights[3], weights[4], orderings, segment)
    result_two = second_rows + feed_forward(middle, weights[5], weights[6], weights[7], weights[8], weights[9], weights[10])
    return (middle, result_two)

def reference(stream_one, stream_two, attention_gain, attention_shift, query_proj, value_proj, output_proj, forward_gain, forward_shift, up_proj, up_bias, down_proj, down_bias, bucket_ids, sort_orders, doc_lengths, cotan_one, cotan_two):
    weights = tuple((weight.astype(jnp.float32) for weight in (attention_gain, attention_shift, query_proj, value_proj, output_proj, forward_gain, forward_shift, up_proj, up_bias, down_proj, down_bias)))
    first_rows = stream_one.astype(jnp.float32).reshape(SEQS, SEQ, D)
    second_rows = stream_two.astype(jnp.float32).reshape(SEQS, SEQ, D)
    doc_ends = jnp.cumsum(doc_lengths, axis=-1).astype(jnp.int32)
    places = jnp.arange(SEQ, dtype=jnp.int32)
    segments = lax.optimization_barrier(jnp.sum((places[None, :, None] >= doc_ends[:, None, :]).astype(jnp.int32), axis=-1, dtype=jnp.int32))

    def whole(first_in, second_in, params):

        def one_sequence(item):
            return jax.checkpoint(block_layer)(item[0], item[1], params, item[2], item[3])
        return lax.map(one_sequence, (first_in, second_in, sort_orders, segments))
    (out_one, out_two), pullback = jax.vjp(whole, first_rows, second_rows, weights)
    cotangents = (cotan_one.astype(jnp.float32).reshape(SEQS, SEQ, D), cotan_two.astype(jnp.float32).reshape(SEQS, SEQ, D))
    grad_first, grad_second, grad_params = pullback(cotangents)
    levels = jnp.arange(NB, dtype=jnp.int32)
    counts = lax.optimization_barrier(jnp.sum((bucket_ids[:, :, None] == levels).astype(jnp.int32), axis=0, dtype=jnp.int32))
    return (out_one.reshape(TOKENS, D).astype(jnp.bfloat16), out_two.reshape(TOKENS, D).astype(jnp.bfloat16), grad_first.reshape(TOKENS, D).astype(jnp.bfloat16), grad_second.reshape(TOKENS, D).astype(jnp.bfloat16), grad_params[0], grad_params[1], grad_params[2], grad_params[3], grad_params[4], grad_params[5], grad_params[6], grad_params[7], grad_params[8], grad_params[9], grad_params[10], counts)
```

```python
from functools import partial
import math

import jax
import jax.numpy as jnp
from jax import lax
from jax.experimental import pallas as pl
from jax.experimental.pallas import tpu as pltpu
from jax.sharding import PartitionSpec as P

HD = 128
GROUP = 64
NB = 24
MOST = 768
BLOCK = 256
LANES = 128

FLOAT = jnp.float32
HALF = jnp.bfloat16
NEG = -1e30
EXP_SCALE = math.log2(math.e) / math.sqrt(HD)
FACTOR = 1.0 / math.sqrt(HD)


def normalize(inputs):
    center = inputs - jnp.mean(inputs, axis=-1, keepdims=True)
    inverse = lax.rsqrt(jnp.mean(center * center, axis=-1, keepdims=True) + 1e-05)
    return (center * inverse, inverse)


def norm_back(grad_out, scaled, inverse, gain):
    spread = grad_out * gain
    return inverse * (
        spread
        - jnp.mean(spread, axis=-1, keepdims=True)
        - scaled * jnp.mean(spread * scaled, axis=-1, keepdims=True)
    )


def contract_rows(left, right):
    return lax.dot_general(left, right, (((0,), (0,)), ((), ())), preferred_element_type=FLOAT)


def times_transpose(left, right):
    return lax.dot_general(left, right, (((1,), (1,)), ((), ())), preferred_element_type=FLOAT)


def one_hot(values, depth):
    return values[..., None] == jnp.arange(depth, dtype=jnp.int32)


def pair_features(orderings, doc_lengths):
    rounds, length = orderings.shape
    blocks = length // GROUP
    docs = doc_lengths.shape[0]
    places = jnp.arange(length, dtype=jnp.int32)
    high = one_hot(orderings // LANES, length // LANES).astype(HALF)
    low = jnp.where(one_hot(orderings % LANES, LANES), (places // GROUP)[None, :, None], 0).astype(HALF)
    group = jnp.einsum("rpa,rpb->rab", high, low, preferred_element_type=FLOAT)
    group = group.reshape(rounds, length).astype(jnp.int32).T
    ends = jnp.sum(
        jnp.where(jnp.arange(docs)[None, :] <= jnp.arange(docs)[:, None], doc_lengths[None, :], 0), axis=1
    )
    segment = jnp.sum((places[:, None] >= ends[None, :]).astype(jnp.int32), axis=-1)
    begins = jnp.sum(jnp.where(one_hot(segment, docs), (ends - doc_lengths)[None, :], 0), axis=-1)
    own = one_hot(group, blocks)
    before = one_hot((group + 1) % blocks, blocks)
    same = one_hot(segment, docs)
    width = rounds * blocks + docs
    pad = -width % LANES
    query = jnp.concatenate(
        [own.reshape(length, -1).astype(HALF), same.astype(HALF) * (2 * rounds), jnp.zeros((length, pad), HALF)], axis=1
    )
    key = jnp.concatenate(
        [(own | before).reshape(length, -1).astype(HALF), same.astype(HALF), jnp.zeros((length, pad), HALF)], axis=1
    )
    first = begins.reshape(length // BLOCK, BLOCK)[:, 0] // BLOCK
    return query, key, first.astype(jnp.int32)


def pair_counts(query, key, rounds, diagonal):
    total = times_transpose(query, key)
    counts = jnp.maximum(total - 2.0 * rounds, 0.0)
    if diagonal:
        rows = lax.broadcasted_iota(jnp.int32, counts.shape, 0)
        columns = lax.broadcasted_iota(jnp.int32, counts.shape, 1)
        counts = jnp.where(columns < rows, counts, 0.0)
    return counts


def attention_kernel(rounds, heads, steps, first, q_ref, k_ref, v_ref, fq_ref, fk_ref, merged_ref, logs_ref, counts, scores, peak, total, mixed):
    block = pl.program_id(0)
    size = q_ref.shape[0]

    def active(step):
        return (block - step) >= first[block]

    def rows(step):
        return pl.ds(pl.multiple_of((block - step) * size, size), size)

    for step in range(steps):

        @pl.when(active(step))
        def _():
            counts[step] = pair_counts(fq_ref[...], fk_ref[rows(step), :], rounds, step == 0)

    lane = lax.broadcasted_iota(jnp.int32, logs_ref.shape, 1)
    logs = jnp.zeros(logs_ref.shape, FLOAT)
    for head in range(heads):
        span = slice(head * HD, (head + 1) * HD)
        for step in range(steps):

            @pl.when(active(step))
            def _():
                raw = times_transpose(q_ref[:, span], k_ref[rows(step), span])
                raw = jnp.where(counts[step] > 0.0, raw, NEG)
                scores[step] = raw
                if step == 0:
                    peak[...] = raw
                else:
                    peak[...] = jnp.maximum(peak[...], raw)

        largest = jnp.max(peak[...], axis=-1, keepdims=True)
        for step in range(steps):

            @pl.when(active(step))
            def _():
                powers = counts[step] * jnp.exp2((scores[step] - largest) * EXP_SCALE)
                part = jnp.dot(powers.astype(HALF), v_ref[rows(step), span], preferred_element_type=FLOAT)
                if step == 0:
                    total[...] = powers
                    mixed[...] = part
                else:
                    total[...] += powers
                    mixed[...] += part

        sums = jnp.sum(total[...], axis=-1, keepdims=True)
        alone = sums == 0.0
        own = v_ref[rows(0), span].astype(FLOAT)
        result = jnp.where(alone, own, mixed[...] / jnp.where(alone, 1.0, sums))
        merged_ref[:, span] = result.astype(HALF)
        log_sum = jnp.where(alone, -NEG, largest * EXP_SCALE + jnp.log2(jnp.where(alone, 1.0, sums)))
        logs = jnp.where(lane == head, log_sum, logs)
    logs_ref[...] = logs


def attention(queries, keys, values, features, rounds):
    length, width = queries.shape
    heads = width // HD
    query_features, key_features, first = features
    depth = query_features.shape[1]
    steps = min(-(-(MOST - 1) // BLOCK), length // BLOCK - 1) + 1
    whole = lambda i, first: (0, 0)
    by_block = lambda i, first: (i, 0)
    return pl.pallas_call(
        partial(attention_kernel, rounds, heads, steps),
        grid_spec=pltpu.PrefetchScalarGridSpec(
            num_scalar_prefetch=1,
            grid=(length // BLOCK,),
            in_specs=[
                pl.BlockSpec((BLOCK, width), by_block),
                pl.BlockSpec((length, width), whole),
                pl.BlockSpec((length, width), whole),
                pl.BlockSpec((BLOCK, depth), by_block),
                pl.BlockSpec((length, depth), whole),
            ],
            out_specs=[
                pl.BlockSpec((BLOCK, width), by_block),
                pl.BlockSpec((BLOCK, LANES), by_block),
            ],
            scratch_shapes=[
                pltpu.VMEM((steps, BLOCK, BLOCK), FLOAT),
                pltpu.VMEM((steps, BLOCK, BLOCK), FLOAT),
                pltpu.VMEM((BLOCK, BLOCK), FLOAT),
                pltpu.VMEM((BLOCK, BLOCK), FLOAT),
                pltpu.VMEM((BLOCK, HD), FLOAT),
            ],
        ),
        out_shape=[
            jax.ShapeDtypeStruct((length, width), HALF),
            jax.ShapeDtypeStruct((length, LANES), FLOAT),
        ],
        compiler_params=pltpu.CompilerParams(vmem_limit_bytes=32 << 20),
        cost_estimate=pl.CostEstimate(flops=3 * 10**9, bytes_accessed=6 * 2**20, transcendentals=2 * 10**6),
        name="attention_forward",
    )(first, queries, keys, values, query_features, key_features)


def attention_back_kernel(
    rounds, heads, steps, first, q_ref, g_ref, merged_ref, logs_ref, fq_ref, fk_ref, k_ref, v_ref, all_q_ref, all_g_ref, all_logs_ref,
    grad_q_ref, grad_v_ref, counts, dq, dk, dv,
):
    block = pl.program_id(0)
    size = q_ref.shape[0]
    length = k_ref.shape[0]

    @pl.when(block == 0)
    def _():
        dk[...] = jnp.zeros_like(dk)
        dv[...] = jnp.zeros_like(dv)

    def active(step):
        return (block - step) >= first[block]

    def rows(step):
        return pl.ds(pl.multiple_of((block - step) * size, size), size)

    for step in range(steps):

        @pl.when(active(step))
        def _():
            counts[step] = pair_counts(fq_ref[...], fk_ref[rows(step), :], rounds, step == 0)

    for head in range(heads):
        span = slice(head * HD, (head + 1) * HD)
        log_sum = logs_ref[:, head : head + 1]
        along = jnp.sum(
            g_ref[:, span].astype(FLOAT) * merged_ref[:, span].astype(FLOAT), axis=-1, keepdims=True
        )
        for step in range(steps):

            @pl.when(active(step))
            def _():
                at = rows(step)
                raw = times_transpose(q_ref[:, span], k_ref[at, span])
                count = counts[step]
                weights = count * jnp.exp2(jnp.where(count > 0.0, raw * EXP_SCALE - log_sum, NEG))
                grad_probs = times_transpose(g_ref[:, span], v_ref[at, span])
                grad_scores = (weights * (grad_probs - along)).astype(HALF)
                dv[at, span] += contract_rows(weights.astype(HALF), g_ref[:, span])
                dk[at, span] += contract_rows(grad_scores, q_ref[:, span])
                part = jnp.dot(grad_scores, k_ref[at, span], preferred_element_type=FLOAT)
                here = rows(0)
                if step == 0:
                    dq[here, span] = part
                else:
                    dq[here, span] += part

    @pl.when(block == pl.num_programs(0) - 1)
    def _():
        @pl.loop(0, length // size)
        def _(index):
            at = pl.ds(pl.multiple_of(index * size, size), size)
            for head in range(heads):
                span = slice(head * HD, (head + 1) * HD)
                alone = all_logs_ref[at, head : head + 1] == -NEG
                grad_v_ref[at, span] = (
                    dv[at, span] + jnp.where(alone, all_g_ref[at, span].astype(FLOAT), 0.0)
                ).astype(HALF)
                query = all_q_ref[at, span].astype(FLOAT)
                key_scale = lax.rsqrt(jnp.sum(query * query, axis=-1, keepdims=True) + 1e-06)
                unit = query * key_scale
                grad_key = dk[at, span] * FACTOR
                key_along = jnp.sum(grad_key * unit, axis=-1, keepdims=True)
                grad_q_ref[at, span] = (
                    dq[at, span] * FACTOR + key_scale * (grad_key - unit * key_along)
                ).astype(HALF)


def attention_back(queries, keys, values, grads, merged, logs, features, rounds):
    length, width = queries.shape
    heads = width // HD
    query_features, key_features, first = features
    depth = query_features.shape[1]
    steps = min(-(-(MOST - 1) // BLOCK), length // BLOCK - 1) + 1
    whole = lambda i, first: (0, 0)
    by_block = lambda i, first: (i, 0)
    return pl.pallas_call(
        partial(attention_back_kernel, rounds, heads, steps),
        grid_spec=pltpu.PrefetchScalarGridSpec(
            num_scalar_prefetch=1,
            grid=(length // BLOCK,),
            in_specs=[
                pl.BlockSpec((BLOCK, width), by_block),
                pl.BlockSpec((BLOCK, width), by_block),
                pl.BlockSpec((BLOCK, width), by_block),
                pl.BlockSpec((BLOCK, LANES), by_block),
                pl.BlockSpec((BLOCK, depth), by_block),
                pl.BlockSpec((length, depth), whole),
                pl.BlockSpec((length, width), whole),
                pl.BlockSpec((length, width), whole),
                pl.BlockSpec((length, width), whole),
                pl.BlockSpec((length, width), whole),
                pl.BlockSpec((length, LANES), whole),
            ],
            out_specs=[pl.BlockSpec((length, width), whole), pl.BlockSpec((length, width), whole)],
            scratch_shapes=[
                pltpu.VMEM((steps, BLOCK, BLOCK), FLOAT),
                pltpu.VMEM((length, width), FLOAT),
                pltpu.VMEM((length, width), FLOAT),
                pltpu.VMEM((length, width), FLOAT),
            ],
        ),
        out_shape=[jax.ShapeDtypeStruct((length, width), HALF), jax.ShapeDtypeStruct((length, width), HALF)],
        compiler_params=pltpu.CompilerParams(vmem_limit_bytes=40 << 20),
        cost_estimate=pl.CostEstimate(flops=6 * 10**9, bytes_accessed=8 * 2**20, transcendentals=2 * 10**6),
        name="attention_backward",
    )(first, queries, grads, merged, logs, query_features, key_features, keys, values, queries, grads, logs)


def per_device(
    stream_one,
    stream_two,
    attention_gain,
    attention_shift,
    query_proj,
    value_proj,
    output_proj,
    forward_gain,
    forward_shift,
    up_proj,
    up_bias,
    down_proj,
    down_bias,
    bucket_ids,
    sort_orders,
    doc_lengths,
    cotan_one,
    cotan_two,
):
    gather = partial(lax.all_gather, axis_name="narrow", axis=0, tiled=True)
    scatter = partial(lax.psum_scatter, axis_name="narrow", scatter_dimension=0, tiled=True)
    first_rows = stream_one.astype(FLOAT)
    second_rows = stream_two.astype(FLOAT)
    orderings = sort_orders[0]
    rounds, length = orderings.shape
    heads = query_proj.shape[1] // HD

    scaled_one, inverse_one = normalize(second_rows)
    normed_one = (scaled_one * attention_gain + attention_shift).astype(HALF)
    gathered_one = gather(normed_one)
    grad_out_two = gather(cotan_two)
    features = pair_features(orderings, doc_lengths[0])
    queries = jnp.dot(gathered_one, query_proj, preferred_element_type=FLOAT).astype(HALF)
    by_head = queries.astype(FLOAT).reshape(length, heads, HD)
    key_scale = lax.rsqrt(jnp.sum(by_head * by_head, axis=-1, keepdims=True) + 1e-06)
    keys = (by_head * key_scale).astype(HALF).reshape(length, heads * HD)
    values = jnp.dot(gathered_one, value_proj, preferred_element_type=FLOAT).astype(HALF)
    merged, logs = attention(queries, keys, values, features, rounds)
    attended = scatter(jnp.dot(merged, output_proj, preferred_element_type=FLOAT).astype(HALF)).astype(FLOAT)
    middle = first_rows + attended
    scaled_two, inverse_two = normalize(middle)
    normed_two = (scaled_two * forward_gain + forward_shift).astype(HALF)
    gathered_two = gather(normed_two)
    hidden = jnp.dot(gathered_two, up_proj, preferred_element_type=FLOAT) + up_bias
    active_float, gelu_back = jax.vjp(partial(jax.nn.gelu, approximate=True), hidden)
    active = active_float.astype(HALF)
    grad_hidden = gelu_back(times_transpose(grad_out_two, down_proj))[0].astype(HALF)
    grad_normed_two = scatter(times_transpose(grad_hidden, up_proj).astype(HALF)).astype(FLOAT)
    grad_middle = cotan_one.astype(FLOAT) + norm_back(grad_normed_two, scaled_two, inverse_two, forward_gain)
    grad_first_low = grad_middle.astype(HALF)
    grad_rows = gather(grad_first_low)
    grad_down = contract_rows(active, grad_out_two)
    grad_down_bias = jnp.sum(grad_out_two, axis=0, dtype=FLOAT)
    grad_up = contract_rows(gathered_two, grad_hidden)
    grad_up_bias = jnp.sum(grad_hidden, axis=0, dtype=FLOAT)
    forward_sums = lax.psum((grad_up.astype(HALF), grad_down.astype(HALF)), "wide")
    fed_rows = scatter(jnp.dot(active, down_proj, preferred_element_type=FLOAT).astype(HALF)).astype(FLOAT)
    result_two = second_rows + (fed_rows + down_bias)
    grad_output = contract_rows(merged, grad_rows)
    grad_merged = times_transpose(grad_rows, output_proj).astype(HALF)
    grad_query, grad_value = attention_back(queries, keys, values, grad_merged, merged, logs, features, rounds)
    grad_query_weights = contract_rows(gathered_one, grad_query)
    grad_value_weights = contract_rows(gathered_one, grad_value)
    grad_normed_one = scatter(
        (times_transpose(grad_query, query_proj) + times_transpose(grad_value, value_proj)).astype(HALF)
    ).astype(FLOAT)
    grad_second = cotan_two.astype(FLOAT) + norm_back(grad_normed_one, scaled_one, inverse_one, attention_gain)
    attention_sums = lax.psum(
        (grad_query_weights.astype(HALF), grad_value_weights.astype(HALF), grad_output.astype(HALF)), "wide"
    )
    levels = jnp.arange(NB, dtype=jnp.int32)
    counts = jnp.sum((bucket_ids[:, :, None] == levels).astype(FLOAT), axis=0)
    norm_totals = lax.psum(
        (
            jnp.sum(grad_normed_one * scaled_one, axis=0),
            jnp.sum(grad_normed_one, axis=0),
            jnp.sum(grad_normed_two * scaled_two, axis=0),
            jnp.sum(grad_normed_two, axis=0),
            counts,
        ),
        ("wide", "narrow"),
    )
    bias_sums = lax.psum((grad_up_bias, grad_down_bias), "wide")
    return (
        middle.astype(HALF),
        result_two.astype(HALF),
        grad_first_low,
        grad_second.astype(HALF),
        norm_totals[0],
        norm_totals[1],
        attention_sums[0].astype(FLOAT),
        attention_sums[1].astype(FLOAT),
        attention_sums[2].astype(FLOAT),
        norm_totals[2],
        norm_totals[3],
        forward_sums[0].astype(FLOAT),
        bias_sums[0],
        forward_sums[1].astype(FLOAT),
        bias_sums[1],
        norm_totals[4].astype(jnp.int32),
    )


def solution(mesh):
    rows = P(("wide", "narrow"), None)
    columns = P(None, "narrow")
    return jax.shard_map(
        per_device,
        mesh=mesh,
        in_specs=(
            rows,
            rows,
            P(),
            P(),
            columns,
            columns,
            P("narrow", None),
            P(),
            P(),
            columns,
            P("narrow"),
            P("narrow", None),
            P(),
            rows,
            P("wide", None, None),
            P("wide", None),
            rows,
            rows,
        ),
        out_specs=(
            rows,
            rows,
            rows,
            rows,
            P(),
            P(),
            columns,
            columns,
            P("narrow", None),
            P(),
            P(),
            columns,
            P("narrow"),
            P("narrow", None),
            P(),
            P(),
        ),
        check_vma=False,
    )
```

```python
from functools import partial
import math

import jax
import jax.numpy as jnp
from jax import lax
from jax.experimental import pallas as pl
from jax.experimental.pallas import tpu as pltpu
from jax.sharding import PartitionSpec as P

HD = 128
GROUP = 64
NB = 24
MOST = 768
BLOCK = 256
LANES = 128
CHUNK = 128
NARROW = 4

FLOAT = jnp.float32
HALF = jnp.bfloat16
NEG = -1e30
EXP_SCALE = math.log2(math.e) / math.sqrt(HD)
FACTOR = 1.0 / math.sqrt(HD)
MESH = pl.DeviceIdType.MESH
IN_VMEM = pl.BlockSpec(memory_space=pltpu.VMEM)
IN_SMEM = pl.BlockSpec(memory_space=pltpu.SMEM)
ANYWHERE = pl.BlockSpec(memory_space=pl.ANY)
DMA = pltpu.SemaphoreType.DMA


def normalize(inputs):
    center = inputs - jnp.mean(inputs, axis=-1, keepdims=True)
    inverse = lax.rsqrt(jnp.mean(center * center, axis=-1, keepdims=True) + 1e-05)
    return (center * inverse, inverse)


def norm_back(grad_out, scaled, inverse, gain):
    spread = grad_out * gain
    return inverse * (
        spread
        - jnp.mean(spread, axis=-1, keepdims=True)
        - scaled * jnp.mean(spread * scaled, axis=-1, keepdims=True)
    )


def contract_rows(left, right):
    return lax.dot_general(left, right, (((0,), (0,)), ((), ())), preferred_element_type=FLOAT)


def times_transpose(left, right):
    return lax.dot_general(left, right, (((1,), (1,)), ((), ())), preferred_element_type=FLOAT)


def times(left, right):
    return jnp.dot(left, right, preferred_element_type=FLOAT)


def column_sums(rows):
    return times(jnp.ones((8, rows.shape[0]), rows.dtype), rows)[0:1]


class Place:
    def __init__(self):
        index = lax.axis_index("narrow")
        core, chip = lax.rem(index, 2), lax.div(index, 2)
        self.me = index
        self.near = 2 * chip + 1 - core
        self.far = 2 * (1 - chip) + core
        self.cross = 2 * (1 - chip) + 1 - core


def span(start, size):
    return pl.ds(pl.multiple_of(start, size), size)


def meet(place):
    barrier = pltpu.get_barrier_semaphore()
    for other in (place.near, place.far):
        pl.semaphore_signal(barrier, inc=1, device_id={"narrow": other}, device_id_type=MESH)
    pl.semaphore_wait(barrier, 2)


def remote(source, target, sent, arrived, other):
    return pltpu.make_async_remote_copy(
        src_ref=source,
        dst_ref=target,
        send_sem=sent,
        recv_sem=arrived,
        device_id={"narrow": other},
        device_id_type=MESH,
    )


class Gather:
    def __init__(self, place, whole, rows, sems):
        self.place, self.whole, self.rows = place, whole, rows
        self.sent, self.arrived = sems
        self.chunks = rows // CHUNK

    def at(self, owner, chunk):
        return self.whole.at[span(owner * self.rows + chunk * CHUNK, CHUNK), :]

    def copy(self, lane, owner, chunk, other):
        index = lane * self.chunks + chunk
        piece = self.at(owner, chunk)
        return remote(piece, piece, self.sent.at[index], self.arrived.at[index], other)

    def to_far(self, chunk):
        return self.copy(0, self.place.me, chunk, self.place.far)

    def to_near(self, chunk):
        return self.copy(1, self.place.me, chunk, self.place.near)

    def onward(self, chunk):
        return self.copy(2, self.place.far, chunk, self.place.near)

    def send(self, chunk):
        self.to_far(chunk).start()
        self.to_near(chunk).start()

    def take_near(self, chunk):
        self.to_near(chunk).wait_recv()

    def take_far(self, chunk):
        self.to_far(chunk).wait_recv()
        self.onward(chunk).start()

    def take_cross(self, chunk):
        self.onward(chunk).wait_recv()

    def finish(self):
        @pl.loop(0, self.chunks)
        def _(chunk):
            self.to_far(chunk).wait_send()
            self.to_near(chunk).wait_send()
            self.onward(chunk).wait_send()


def gather_sems(rows):
    return [DMA((3 * (rows // CHUNK),)), DMA((3 * (rows // CHUNK),))]


class Scatter:
    def __init__(self, place, term, rows, buffers, sems):
        self.place, self.term, self.rows = place, term, rows
        self.near_out, self.near_in, self.far_out, self.far_in = buffers
        self.sent, self.arrived = sems
        self.chunks = rows // CHUNK

    def to_near(self, part, chunk):
        index = part * self.chunks + chunk
        at = span(chunk * CHUNK, CHUNK)
        return remote(
            self.near_out.at[part, at, :],
            self.near_in.at[part, at, :],
            self.sent.at[index],
            self.arrived.at[index],
            self.place.near,
        )

    def to_far(self, chunk):
        index = 2 * self.chunks + chunk
        at = span(chunk * CHUNK, CHUNK)
        return remote(
            self.far_out.at[at, :], self.far_in.at[at, :], self.sent.at[index], self.arrived.at[index], self.place.far
        )

    def part(self, owner, chunk):
        return self.term(span(owner * self.rows + chunk * CHUNK, CHUNK))

    def start(self):
        @pl.loop(0, self.chunks)
        def _(chunk):
            self.near_out[0, span(chunk * CHUNK, CHUNK), :] = self.part(self.place.cross, chunk).astype(HALF)
            self.to_near(0, chunk).start()

        @pl.loop(0, self.chunks)
        def _(chunk):
            at = span(chunk * CHUNK, CHUNK)
            own = self.part(self.place.far, chunk)
            self.to_near(0, chunk).wait_recv()
            self.far_out[at, :] = (own + self.near_in[0, at, :].astype(FLOAT)).astype(HALF)
            self.to_far(chunk).start()

        @pl.loop(0, self.chunks)
        def _(chunk):
            self.near_out[1, span(chunk * CHUNK, CHUNK), :] = self.part(self.place.near, chunk).astype(HALF)
            self.to_near(1, chunk).start()

    def chip_sum(self, chunk):
        own = self.part(self.place.me, chunk)
        self.to_near(1, chunk).wait_recv()
        return own + self.near_in[1, span(chunk * CHUNK, CHUNK), :].astype(FLOAT)

    def take_far(self, chunk):
        self.to_far(chunk).wait_recv()
        return self.far_in[span(chunk * CHUNK, CHUNK), :].astype(FLOAT)

    def finish(self):
        @pl.loop(0, self.chunks)
        def _(chunk):
            self.to_near(0, chunk).wait_send()
            self.to_near(1, chunk).wait_send()
            self.to_far(chunk).wait_send()


def scatter_buffers(rows, width):
    return [
        pltpu.VMEM((2, rows, width), HALF),
        pltpu.VMEM((2, rows, width), HALF),
        pltpu.VMEM((rows, width), HALF),
        pltpu.VMEM((rows, width), HALF),
    ]


def scatter_sems(rows):
    return [DMA((3 * (rows // CHUNK),)), DMA((3 * (rows // CHUNK),))]


def fetch(copies, sems):
    handles = [pltpu.make_async_copy(source, target, sems.at[i]) for i, (source, target) in enumerate(copies)]
    for handle in handles:
        handle.start()
    return handles


def call(kernel, outs, ins, args, scratch, collective, flops, moved):
    return pl.pallas_call(
        kernel,
        out_shape=[jax.ShapeDtypeStruct(*o) for o in outs],
        in_specs=ins,
        out_specs=[IN_VMEM] * len(outs),
        scratch_shapes=scratch,
        compiler_params=pltpu.CompilerParams(
            collective_id=collective, has_side_effects=True, vmem_limit_bytes=58 << 20
        ),
        cost_estimate=pl.CostEstimate(flops=flops, bytes_accessed=moved, transcendentals=0),
        name=kernel.__name__,
    )(*args)


def pair_features(orders, docs, query_features, key_features, work_q, work_k):
    rounds, length = orders.shape
    groups = length // GROUP
    high_count = length // LANES
    high_rows = -(-high_count // 8) * 8
    count = docs.shape[0]
    lane = lax.broadcasted_iota(jnp.int32, (LANES, length), 1)
    low_at = lax.broadcasted_iota(jnp.int32, (LANES, length), 0)
    high_at = lax.broadcasted_iota(jnp.int32, (high_rows, length), 0)
    group_at = lax.broadcasted_iota(jnp.int32, (groups, LANES), 0).astype(FLOAT)
    sorted_group = lax.shift_right_logical(lane, int(math.log2(GROUP))).astype(FLOAT)
    work_q[...] = jnp.zeros_like(work_q)
    work_k[...] = jnp.zeros_like(work_k)
    for index in range(rounds):
        row = orders[index : index + 1, :]
        high = jnp.where(high_at == lax.shift_right_logical(row, int(math.log2(LANES))), 1.0, 0.0)
        low = jnp.where(low_at == (row & (LANES - 1)), sorted_group, 0.0)
        group = times_transpose(high.astype(HALF), low.astype(HALF))
        for block in range(high_count):
            own = group[block : block + 1, :]
            after = jnp.where(own == groups - 1.0, 0.0, own + 1.0)
            at = slice(block * LANES, (block + 1) * LANES)
            rows = slice(index * groups, (index + 1) * groups)
            mine = group_at == own
            work_q[rows, at] = jnp.where(mine, 1.0, 0.0)
            work_k[rows, at] = jnp.where(mine | (group_at == after), 1.0, 0.0)
    place = lax.broadcasted_iota(jnp.int32, (count, length), 1)
    which = lax.broadcasted_iota(jnp.int32, (count, length), 0)
    same = jnp.zeros((count, length), FLOAT)
    begin = jnp.int32(0)
    for doc in range(count):
        end = begin + docs[doc]
        same = jnp.where((which == doc) & (place >= begin) & (place < end), 1.0, same)
        begin = end
    work_q[rounds * groups : rounds * groups + count, :] = same * (2.0 * rounds)
    work_k[rounds * groups : rounds * groups + count, :] = same
    query_features[...] = work_q[...].astype(HALF)
    key_features[...] = work_k[...].astype(HALF)


def project_in(
    rows_ref, gain, shift, wq_any, wv_any, orders, docs, buckets,
    whole, queries, keys, values, query_features, key_features, bucket_sums,
    wq, wv, work_q, work_k, loads, sent, arrived,
):
    place = Place()
    rows = rows_ref.shape[0]
    weights = fetch([(wq_any, wq), (wv_any, wv)], loads)
    meet(place)
    gather = Gather(place, whole, rows, (sent, arrived))

    @pl.loop(0, gather.chunks)
    def _(chunk):
        scaled, _ = normalize(rows_ref[span(chunk * CHUNK, CHUNK), :].astype(FLOAT))
        normed = (scaled * gain[...] + shift[...]).astype(HALF)
        whole[span(place.me * rows + chunk * CHUNK, CHUNK), :] = normed
        gather.send(chunk)

    pair_features(orders, docs, query_features, key_features, work_q, work_k)
    level = lax.broadcasted_iota(jnp.int32, (rows, LANES), 1)
    sums = [
        jnp.sum(jnp.where(level == buckets[:, index : index + 1], 1.0, 0.0), axis=0, keepdims=True)
        for index in range(buckets.shape[1])
    ]
    sums += [jnp.zeros((1, LANES), FLOAT)] * (8 - len(sums))
    bucket_sums[...] = jnp.concatenate(sums, axis=0)
    for weight in weights:
        weight.wait()

    def project(owner):
        at = span(owner * rows, rows)
        query = times(whole[at, :], wq[...]).astype(HALF)
        queries[at, :] = query
        for head in range(query.shape[1] // HD):
            part = query[:, head * HD : (head + 1) * HD].astype(FLOAT)
            scale = lax.rsqrt(jnp.sum(part * part, axis=-1, keepdims=True) + 1e-06)
            keys[at, head * HD : (head + 1) * HD] = (part * scale).astype(HALF)
        values[at, :] = times(whole[at, :], wv[...]).astype(HALF)

    @pl.loop(0, NARROW)
    def _(step):
        @pl.loop(0, gather.chunks)
        def _(chunk):
            @pl.when(step == 1)
            def _():
                gather.take_near(chunk)

            @pl.when(step == 2)
            def _():
                gather.take_far(chunk)

            @pl.when(step == 3)
            def _():
                gather.take_cross(chunk)

        project(in_turn(place, step))

    gather.finish()


def in_turn(place, step):
    flip_core, flip_chip = lax.rem(step, 2), lax.div(step, 2)
    core, chip = lax.rem(place.me, 2), lax.div(place.me, 2)
    core = core + flip_core * (1 - 2 * core)
    chip = chip + flip_chip * (1 - 2 * chip)
    return 2 * chip + core


def run_project_in(rows, gain, shift, wq, wv, orders, docs, buckets):
    count, width = rows.shape
    length = NARROW * count
    heads = wq.shape[1]
    depth = -(-(orders.shape[0] * (length // GROUP) + docs.shape[0]) // LANES) * LANES
    return call(
        project_in,
        [
            ((length, width), HALF),
            ((length, heads), HALF),
            ((length, heads), HALF),
            ((length, heads), HALF),
            ((depth, length), HALF),
            ((depth, length), HALF),
            ((8, LANES), FLOAT),
        ],
        [IN_VMEM, IN_VMEM, IN_VMEM, ANYWHERE, ANYWHERE, IN_VMEM, IN_SMEM, IN_VMEM],
        (rows, gain, shift, wq, wv, orders, docs, buckets),
        [
            pltpu.VMEM(wq.shape, HALF),
            pltpu.VMEM(wv.shape, HALF),
            pltpu.VMEM((depth, length), FLOAT),
            pltpu.VMEM((depth, length), FLOAT),
            DMA((2,)),
            *gather_sems(count),
        ],
        0,
        4 * length * width * heads,
        10 << 20,
    )


def doc_start(docs, position):
    start = jnp.int32(0)
    begin = jnp.int32(0)
    for doc in range(docs.shape[0]):
        start = jnp.where(position >= begin, begin, start)
        begin = begin + docs[doc]
    return start


def pair_counts(query, key, rounds, diagonal):
    total = contract_rows(query, key)
    counts = jnp.maximum(total - 2.0 * rounds, 0.0)
    if diagonal:
        rows = lax.broadcasted_iota(jnp.int32, counts.shape, 0)
        columns = lax.broadcasted_iota(jnp.int32, counts.shape, 1)
        counts = jnp.where(columns < rows, counts, 0.0)
    return counts


def attention_forward(rounds, heads, steps, docs, q_ref, k_ref, v_ref, fq_ref, fk_ref, merged_ref, logs_ref, counts, scores, peak, total, mixed):
    block = pl.program_id(0)
    size = q_ref.shape[0]
    first = lax.div(doc_start(docs, block * size), size)

    def active(step):
        return (block - step) >= first

    def rows(step):
        return span((block - step) * size, size)

    for step in range(steps):

        @pl.when(active(step))
        def _():
            counts[step] = pair_counts(fq_ref[...], fk_ref[:, rows(step)], rounds, step == 0)

    lane = lax.broadcasted_iota(jnp.int32, logs_ref.shape, 1)
    logs = jnp.zeros(logs_ref.shape, FLOAT)
    for head in range(heads):
        part_of = slice(head * HD, (head + 1) * HD)
        for step in range(steps):

            @pl.when(active(step))
            def _():
                raw = times_transpose(q_ref[:, part_of], k_ref[rows(step), part_of])
                raw = jnp.where(counts[step] > 0.0, raw, NEG)
                scores[step] = raw
                if step == 0:
                    peak[...] = raw
                else:
                    peak[...] = jnp.maximum(peak[...], raw)

        largest = jnp.max(peak[...], axis=-1, keepdims=True)
        for step in range(steps):

            @pl.when(active(step))
            def _():
                powers = counts[step] * jnp.exp2((scores[step] - largest) * EXP_SCALE)
                part = times(powers.astype(HALF), v_ref[rows(step), part_of])
                if step == 0:
                    total[...] = powers
                    mixed[...] = part
                else:
                    total[...] += powers
                    mixed[...] += part

        sums = jnp.sum(total[...], axis=-1, keepdims=True)
        alone = sums == 0.0
        own = v_ref[rows(0), part_of].astype(FLOAT)
        result = jnp.where(alone, own, mixed[...] / jnp.where(alone, 1.0, sums))
        merged_ref[:, part_of] = result.astype(HALF)
        log_sum = jnp.where(alone, -NEG, largest * EXP_SCALE + jnp.log2(jnp.where(alone, 1.0, sums)))
        logs = jnp.where(lane == head, log_sum, logs)
    logs_ref[...] = logs


def band_steps(length):
    return min(-(-(MOST - 1) // BLOCK), length // BLOCK - 1) + 1


def run_attention(queries, keys, values, query_features, key_features, docs, rounds):
    length, width = queries.shape
    depth = query_features.shape[0]
    steps = band_steps(length)
    whole = lambda i, docs: (0, 0)
    by_block = lambda i, docs: (i, 0)
    return pl.pallas_call(
        partial(attention_forward, rounds, width // HD, steps),
        grid_spec=pltpu.PrefetchScalarGridSpec(
            num_scalar_prefetch=1,
            grid=(length // BLOCK,),
            in_specs=[
                pl.BlockSpec((BLOCK, width), by_block),
                pl.BlockSpec((length, width), whole),
                pl.BlockSpec((length, width), whole),
                pl.BlockSpec((depth, BLOCK), lambda i, docs: (0, i)),
                pl.BlockSpec((depth, length), whole),
            ],
            out_specs=[
                pl.BlockSpec((BLOCK, width), by_block),
                pl.BlockSpec((BLOCK, LANES), by_block),
            ],
            scratch_shapes=[
                pltpu.VMEM((steps, BLOCK, BLOCK), FLOAT),
                pltpu.VMEM((steps, BLOCK, BLOCK), FLOAT),
                pltpu.VMEM((BLOCK, BLOCK), FLOAT),
                pltpu.VMEM((BLOCK, BLOCK), FLOAT),
                pltpu.VMEM((BLOCK, HD), FLOAT),
            ],
        ),
        out_shape=[
            jax.ShapeDtypeStruct((length, width), HALF),
            jax.ShapeDtypeStruct((length, LANES), FLOAT),
        ],
        compiler_params=pltpu.CompilerParams(vmem_limit_bytes=32 << 20),
        cost_estimate=pl.CostEstimate(flops=6 * 10**9, bytes_accessed=6 * 2**20, transcendentals=2 * 10**6),
        name="attention_forward",
    )(docs, queries, keys, values, query_features, key_features)


def attention_backward(
    rounds, heads, steps, docs, q_ref, g_ref, merged_ref, logs_ref, fq_ref, fk_ref, k_ref, v_ref, all_q_ref, all_g_ref, all_logs_ref,
    grad_q_ref, grad_v_ref, counts, dq, dk, dv,
):
    block = pl.program_id(0)
    size = q_ref.shape[0]
    length = k_ref.shape[0]
    first = lax.div(doc_start(docs, block * size), size)

    @pl.when(block == 0)
    def _():
        dk[...] = jnp.zeros_like(dk)
        dv[...] = jnp.zeros_like(dv)

    def active(step):
        return (block - step) >= first

    def rows(step):
        return span((block - step) * size, size)

    for step in range(steps):

        @pl.when(active(step))
        def _():
            counts[step] = pair_counts(fq_ref[...], fk_ref[:, rows(step)], rounds, step == 0)

    for head in range(heads):
        part_of = slice(head * HD, (head + 1) * HD)
        log_sum = logs_ref[:, head : head + 1]
        along = jnp.sum(
            g_ref[:, part_of].astype(FLOAT) * merged_ref[:, part_of].astype(FLOAT), axis=-1, keepdims=True
        )
        for step in range(steps):

            @pl.when(active(step))
            def _():
                at = rows(step)
                raw = times_transpose(q_ref[:, part_of], k_ref[at, part_of])
                count = counts[step]
                weights = count * jnp.exp2(jnp.where(count > 0.0, raw * EXP_SCALE - log_sum, NEG))
                grad_probs = times_transpose(g_ref[:, part_of], v_ref[at, part_of])
                grad_scores = (weights * (grad_probs - along)).astype(HALF)
                dv[at, part_of] += contract_rows(weights.astype(HALF), g_ref[:, part_of])
                dk[at, part_of] += contract_rows(grad_scores, q_ref[:, part_of])
                part = times(grad_scores, k_ref[at, part_of])
                here = rows(0)
                if step == 0:
                    dq[here, part_of] = part
                else:
                    dq[here, part_of] += part

    @pl.when(block == pl.num_programs(0) - 1)
    def _():
        @pl.loop(0, length // size)
        def _(index):
            at = span(index * size, size)
            for head in range(heads):
                part_of = slice(head * HD, (head + 1) * HD)
                alone = all_logs_ref[at, head : head + 1] == -NEG
                grad_v_ref[at, part_of] = (
                    dv[at, part_of] + jnp.where(alone, all_g_ref[at, part_of].astype(FLOAT), 0.0)
                ).astype(HALF)
                query = all_q_ref[at, part_of].astype(FLOAT)
                key_scale = lax.rsqrt(jnp.sum(query * query, axis=-1, keepdims=True) + 1e-06)
                unit = query * key_scale
                grad_key = dk[at, part_of] * FACTOR
                key_along = jnp.sum(grad_key * unit, axis=-1, keepdims=True)
                grad_q_ref[at, part_of] = (
                    dq[at, part_of] * FACTOR + key_scale * (grad_key - unit * key_along)
                ).astype(HALF)


def run_attention_back(queries, keys, values, grads, merged, logs, query_features, key_features, docs, rounds):
    length, width = queries.shape
    depth = query_features.shape[0]
    steps = band_steps(length)
    whole = lambda i, docs: (0, 0)
    by_block = lambda i, docs: (i, 0)
    return pl.pallas_call(
        partial(attention_backward, rounds, width // HD, steps),
        grid_spec=pltpu.PrefetchScalarGridSpec(
            num_scalar_prefetch=1,
            grid=(length // BLOCK,),
            in_specs=[
                pl.BlockSpec((BLOCK, width), by_block),
                pl.BlockSpec((BLOCK, width), by_block),
                pl.BlockSpec((BLOCK, width), by_block),
                pl.BlockSpec((BLOCK, LANES), by_block),
                pl.BlockSpec((depth, BLOCK), lambda i, docs: (0, i)),
                pl.BlockSpec((depth, length), whole),
                pl.BlockSpec((length, width), whole),
                pl.BlockSpec((length, width), whole),
                pl.BlockSpec((length, width), whole),
                pl.BlockSpec((length, width), whole),
                pl.BlockSpec((length, LANES), whole),
            ],
            out_specs=[pl.BlockSpec((length, width), whole), pl.BlockSpec((length, width), whole)],
            scratch_shapes=[
                pltpu.VMEM((steps, BLOCK, BLOCK), FLOAT),
                pltpu.VMEM((length, width), FLOAT),
                pltpu.VMEM((length, width), FLOAT),
                pltpu.VMEM((length, width), FLOAT),
            ],
        ),
        out_shape=[jax.ShapeDtypeStruct((length, width), HALF), jax.ShapeDtypeStruct((length, width), HALF)],
        compiler_params=pltpu.CompilerParams(vmem_limit_bytes=40 << 20),
        cost_estimate=pl.CostEstimate(flops=10**10, bytes_accessed=8 * 2**20, transcendentals=2 * 10**6),
        name="attention_backward",
    )(docs, queries, grads, merged, logs, query_features, key_features, keys, values, queries, grads, logs)


def feed_in(
    merged, wo, first_rows, gain, shift, up_any, up_bias, down_any, cotan_own, cotan_far,
    out_one, middle, whole, cotans, active, grad_hidden,
    up, down, near_out, near_in, far_out, far_in, loads, cotan_sent, cotan_arrived, sent, arrived, gather_sent, gather_arrived,
):
    place = Place()
    rows, width = first_rows.shape
    weights = fetch([(down_any, down), (up_any, up)], loads)
    own_at, far_at = span(place.me * rows, rows), span(place.far * rows, rows)
    local = [
        pltpu.make_async_copy(cotan_own, cotans.at[own_at, :], loads.at[2]),
        pltpu.make_async_copy(cotan_far, cotans.at[far_at, :], loads.at[3]),
    ]
    for copy in local:
        copy.start()
    meet(place)
    spread = [
        remote(cotan_own, cotans.at[own_at, :], cotan_sent.at[0], cotan_arrived.at[0], place.near),
        remote(cotan_far, cotans.at[far_at, :], cotan_sent.at[1], cotan_arrived.at[1], place.near),
    ]
    for copy in spread:
        copy.start()
    scatter = Scatter(
        place, lambda at: times(merged[at, :], wo[...]), rows, (near_out, near_in, far_out, far_in), (sent, arrived)
    )
    gather = Gather(place, whole, rows, (gather_sent, gather_arrived))
    scatter.start()

    @pl.loop(0, scatter.chunks)
    def _(chunk):
        at = span(chunk * CHUNK, CHUNK)
        middle[at, :] = first_rows[at, :].astype(FLOAT) + scatter.chip_sum(chunk)

    weights[0].wait()
    for copy in local + spread:
        copy.wait()

    def back(owner):
        @pl.loop(0, 2)
        def _(half):
            at = span(half * (width // 2), width // 2)
            grad_hidden[span(owner * rows, rows), at] = times_transpose(
                cotans[span(owner * rows, rows), :], down[at, :]
            ).astype(HALF)

    @pl.loop(0, NARROW)
    def _(owner):
        back(owner)

    @pl.loop(0, scatter.chunks)
    def _(chunk):
        at = span(chunk * CHUNK, CHUNK)
        value = middle[at, :] + scatter.take_far(chunk)
        middle[at, :] = value
        out_one[at, :] = value.astype(HALF)
        scaled, _ = normalize(value)
        whole[span(place.me * rows + chunk * CHUNK, CHUNK), :] = (scaled * gain[...] + shift[...]).astype(HALF)
        gather.send(chunk)

    weights[1].wait()

    @pl.loop(0, NARROW)
    def _(step):
        @pl.loop(0, gather.chunks)
        def _(chunk):
            @pl.when(step == 1)
            def _():
                gather.take_near(chunk)

            @pl.when(step == 2)
            def _():
                gather.take_far(chunk)

            @pl.when(step == 3)
            def _():
                gather.take_cross(chunk)

        owner = in_turn(place, step)
        row_at = span(owner * rows, rows)

        @pl.loop(0, 2)
        def _(half):
            at = span(half * (width // 2), width // 2)
            hidden = times(whole[row_at, :], up[:, at]) + up_bias[:, at]
            square = hidden * hidden
            inner = math.sqrt(2.0 / math.pi) * hidden * (1.0 + 0.044715 * square)
            bend = jnp.tanh(inner)
            half_more = 0.5 + 0.5 * bend
            active[row_at, at] = (hidden * half_more).astype(HALF)
            slope = half_more + 0.5 * hidden * (1.0 - bend * bend) * (
                math.sqrt(2.0 / math.pi) * (1.0 + 3.0 * 0.044715 * square)
            )
            grad_hidden[row_at, at] = (grad_hidden[row_at, at].astype(FLOAT) * slope).astype(HALF)

    scatter.finish()
    gather.finish()


def run_feed_in(merged, wo, first_rows, gain, shift, up, up_bias, down, cotan_own, cotan_far):
    rows, width = first_rows.shape
    length, hidden = NARROW * rows, up.shape[1]
    return call(
        feed_in,
        [
            ((rows, width), HALF),
            ((rows, width), FLOAT),
            ((length, width), HALF),
            ((length, width), HALF),
            ((length, hidden), HALF),
            ((length, hidden), HALF),
        ],
        [IN_VMEM] * 5 + [ANYWHERE, IN_VMEM, ANYWHERE, IN_VMEM, IN_VMEM],
        (merged, wo, first_rows, gain, shift, up, up_bias, down, cotan_own, cotan_far),
        [
            pltpu.VMEM(up.shape, HALF),
            pltpu.VMEM(down.shape, HALF),
            *scatter_buffers(rows, width),
            DMA((4,)),
            DMA((2,)),
            DMA((2,)),
            *scatter_sems(rows),
            *gather_sems(rows),
        ],
        1,
        4 * length * width * hidden,
        24 << 20,
    )


def feed_back(
    grad_hidden, up, middle, gain, cotan_one, active_any, down_any, cotans_any, whole_any, merged_any, wo_any,
    grad_one, grad_merged, grad_up, grad_down, grad_out, fed_own, fed_far, sums,
    active, down, cotans, whole, merged, wo, grad_rows, near_out, near_in, far_out, far_in, fed_out, fed_in,
    loads, sent, arrived, gather_sent, gather_arrived, fed_sent, fed_arrived,
):
    place = Place()
    rows, width = middle.shape
    handles = fetch(
        [(active_any, active), (cotans_any, cotans), (down_any, down), (whole_any, whole), (wo_any, wo), (merged_any, merged)],
        loads,
    )
    meet(place)
    scatter = Scatter(
        place,
        lambda at: times_transpose(grad_hidden[at, :], up[...]),
        rows,
        (near_out, near_in, far_out, far_in),
        (sent, arrived),
    )
    gather = Gather(place, grad_rows, rows, (gather_sent, gather_arrived))
    scatter.start()

    handles[0].wait()
    handles[1].wait()
    tiles(grad_down, active, cotans)
    handles[2].wait()

    def fed_copy(part, chunk):
        index = part * scatter.chunks + chunk
        at = span(chunk * CHUNK, CHUNK)
        return remote(fed_out.at[part, at, :], fed_in.at[part, at, :], fed_sent.at[index], fed_arrived.at[index], place.near)

    @pl.loop(0, scatter.chunks)
    def _(chunk):
        at = span(chunk * CHUNK, CHUNK)
        for part, owner in enumerate((place.cross, place.near)):
            fed_out[part, at, :] = times(active[span(owner * rows + chunk * CHUNK, CHUNK), :], down[...]).astype(HALF)
            fed_copy(part, chunk).start()

    totals = [jnp.zeros((1, width), FLOAT), jnp.zeros((1, width), FLOAT)]

    def back(chunk, totals):
        at = span(chunk * CHUNK, CHUNK)
        grad_normed = scatter.chip_sum(chunk) + scatter.take_far(chunk)
        scaled, inverse = normalize(middle[at, :])
        grad = cotan_one[at, :].astype(FLOAT) + norm_back(grad_normed, scaled, inverse, gain[...])
        low = grad.astype(HALF)
        grad_one[at, :] = low
        grad_rows[span(place.me * rows + chunk * CHUNK, CHUNK), :] = low
        gather.send(chunk)
        return [
            totals[0] + jnp.sum(grad_normed * scaled, axis=0, keepdims=True),
            totals[1] + jnp.sum(grad_normed, axis=0, keepdims=True),
        ]

    totals = lax.fori_loop(0, scatter.chunks, back, totals)

    @pl.loop(0, scatter.chunks)
    def _(chunk):
        at = span(chunk * CHUNK, CHUNK)
        for part, (owner, target) in enumerate(((place.far, fed_far), (place.me, fed_own))):
            own = times(active[span(owner * rows + chunk * CHUNK, CHUNK), :], down[...])
            fed_copy(part, chunk).wait_recv()
            target[at, :] = (own + fed_in[part, at, :].astype(FLOAT)).astype(HALF)

    handles[3].wait()
    tiles(grad_up, whole, grad_hidden)
    sums[...] = jnp.concatenate(
        [*totals, column_sums(grad_hidden[...]), column_sums(cotans[...]), jnp.zeros((4, width), FLOAT)], axis=0
    )
    handles[4].wait()

    @pl.loop(0, NARROW)
    def _(step):
        @pl.loop(0, gather.chunks)
        def _(chunk):
            @pl.when(step == 1)
            def _():
                gather.take_near(chunk)

            @pl.when(step == 2)
            def _():
                gather.take_far(chunk)

            @pl.when(step == 3)
            def _():
                gather.take_cross(chunk)

        at = span(in_turn(place, step) * rows, rows)
        grad_merged[at, :] = times_transpose(grad_rows[at, :], wo[...]).astype(HALF)

    handles[5].wait()
    grad_out[...] = contract_rows(merged[...], grad_rows[...]).astype(HALF)
    scatter.finish()
    gather.finish()

    @pl.loop(0, scatter.chunks)
    def _(chunk):
        fed_copy(0, chunk).wait_send()
        fed_copy(1, chunk).wait_send()


def tiles(result, left, right):
    width = 256

    @pl.loop(0, left.shape[1] // width)
    def _(index):
        at = span(index * width, width)
        result[at, :] = contract_rows(left[:, at], right[...]).astype(result.dtype)


def run_feed_back(grad_hidden, up, middle, gain, cotan_one, active, down, cotans, whole, merged, wo):
    rows, width = middle.shape
    length, hidden = grad_hidden.shape
    heads = merged.shape[1]
    return call(
        feed_back,
        [
            ((rows, width), HALF),
            ((length, heads), HALF),
            ((width, hidden), HALF),
            ((hidden, width), HALF),
            ((heads, width), HALF),
            ((rows, width), HALF),
            ((rows, width), HALF),
            ((8, width), FLOAT),
        ],
        [IN_VMEM] * 5 + [ANYWHERE] * 6,
        (grad_hidden, up, middle, gain, cotan_one, active, down, cotans, whole, merged, wo),
        [
            pltpu.VMEM(active.shape, HALF),
            pltpu.VMEM(down.shape, HALF),
            pltpu.VMEM(cotans.shape, HALF),
            pltpu.VMEM(whole.shape, HALF),
            pltpu.VMEM(merged.shape, HALF),
            pltpu.VMEM(wo.shape, HALF),
            pltpu.VMEM((length, width), HALF),
            *scatter_buffers(rows, width),
            pltpu.VMEM((2, rows, width), HALF),
            pltpu.VMEM((2, rows, width), HALF),
            DMA((6,)),
            *scatter_sems(rows),
            *gather_sems(rows),
            DMA((2 * (rows // CHUNK),)),
            DMA((2 * (rows // CHUNK),)),
        ],
        2,
        8 * length * width * hidden,
        30 << 20,
    )


def project_back(
    grad_query, grad_value, wq, wv, whole_any, second_rows, gain, cotan_two, fed_own, fed_far, down_bias,
    out_two, grad_two, grad_weights, sums,
    whole, near_out, near_in, far_out, far_in, loads, sent, arrived,
):
    place = Place()
    rows, width = second_rows.shape
    heads = grad_query.shape[1]
    [load] = fetch([(whole_any, whole)], loads)
    meet(place)
    scatter = Scatter(
        place,
        lambda at: times_transpose(grad_query[at, :], wq[...]) + times_transpose(grad_value[at, :], wv[...]),
        rows,
        (near_out, near_in, far_out, far_in),
        (sent, arrived),
    )
    scatter.start()
    out_two[...] = (
        second_rows[...].astype(FLOAT) + (fed_own[...].astype(FLOAT) + fed_far[...].astype(FLOAT) + down_bias[...])
    ).astype(HALF)
    load.wait()

    @pl.loop(0, width // 256)
    def _(index):
        at = span(index * 256, 256)
        grad_weights[at, 0:heads] = contract_rows(whole[:, at], grad_query[...]).astype(HALF)
        grad_weights[at, heads : 2 * heads] = contract_rows(whole[:, at], grad_value[...]).astype(HALF)

    def back(chunk, totals):
        at = span(chunk * CHUNK, CHUNK)
        grad_normed = scatter.chip_sum(chunk) + scatter.take_far(chunk)
        scaled, inverse = normalize(second_rows[at, :].astype(FLOAT))
        grad_two[at, :] = (
            cotan_two[at, :].astype(FLOAT) + norm_back(grad_normed, scaled, inverse, gain[...])
        ).astype(HALF)
        return [
            totals[0] + jnp.sum(grad_normed * scaled, axis=0, keepdims=True),
            totals[1] + jnp.sum(grad_normed, axis=0, keepdims=True),
        ]

    totals = lax.fori_loop(
        0, scatter.chunks, back, [jnp.zeros((1, width), FLOAT), jnp.zeros((1, width), FLOAT)]
    )
    sums[...] = jnp.concatenate([*totals, jnp.zeros((6, width), FLOAT)], axis=0)
    scatter.finish()


def run_project_back(grad_query, grad_value, wq, wv, whole, second_rows, gain, cotan_two, fed_own, fed_far, down_bias):
    rows, width = second_rows.shape
    length, heads = grad_query.shape
    return call(
        project_back,
        [
            ((rows, width), HALF),
            ((rows, width), HALF),
            ((width, 2 * heads), HALF),
            ((8, width), FLOAT),
        ],
        [IN_VMEM] * 4 + [ANYWHERE] + [IN_VMEM] * 6,
        (grad_query, grad_value, wq, wv, whole, second_rows, gain, cotan_two, fed_own, fed_far, down_bias),
        [
            pltpu.VMEM((length, width), HALF),
            *scatter_buffers(rows, width),
            DMA((1,)),
            *scatter_sems(rows),
        ],
        3,
        8 * length * width * heads,
        14 << 20,
    )


def ring_place(members, index):
    column, row = lax.rem(index, 2), lax.div(index, 2)
    return row + column * (members - 1 - 2 * row)


def ring_member(members, place):
    back = lax.div(place, members // 2)
    return 2 * place + back * (2 * (members - 1 - place) + 1 - 2 * place)


def sum_wide(members, arrays, *refs):
    data, small_ins = refs[:arrays], refs[arrays : arrays + 3]
    results, small_out = refs[arrays + 3 : 2 * arrays + 3], refs[2 * arrays + 3]
    landed = refs[2 * arrays + 4 : 3 * arrays + 4]
    narrow_all, wide_all, sent, arrived, narrow_sent, narrow_arrived, wide_sent, wide_arrived = refs[3 * arrays + 4 :]
    wide, narrow = lax.axis_index("wide"), lax.axis_index("narrow")
    here = ring_place(members, wide)
    neighbours = (
        ring_member(members, lax.rem(here + 1, members)),
        ring_member(members, lax.rem(here + members - 1, members)),
    )
    barrier = pltpu.get_barrier_semaphore()

    @pl.loop(1, NARROW)
    def _(step):
        pl.semaphore_signal(
            barrier, inc=1, device_id={"narrow": lax.rem(narrow + step, NARROW)}, device_id_type=MESH
        )

    @pl.loop(1, members)
    def _(step):
        pl.semaphore_signal(barrier, inc=1, device_id={"wide": lax.rem(wide + step, members)}, device_id_type=MESH)

    pl.semaphore_wait(barrier, NARROW - 1 + members - 1)

    def piece(direction, step):
        if direction == 0:
            at = lax.rem(here - step + 2 * members, members)
        else:
            at = lax.rem(here + step, members)
        return 2 * at + direction

    def copy(kind, array, direction, step):
        source = (data, results)[kind][array]
        target = (landed, results)[kind][array]
        at = piece(direction, step)
        index = ((kind * 2 + direction) * arrays + array) * (members - 1) + (step - kind * (members - 1))
        return pltpu.make_async_remote_copy(
            src_ref=source.at[at],
            dst_ref=target.at[at],
            send_sem=sent.at[index],
            recv_sem=arrived.at[index],
            device_id={"wide": neighbours[direction]},
            device_id_type=MESH,
        )

    def landing(kind, array, direction, step):
        source = (data, results)[kind][array]
        target = (landed, results)[kind][array]
        at = piece(direction, step + 1)
        index = ((kind * 2 + direction) * arrays + array) * (members - 1) + (step - kind * (members - 1))
        return pltpu.make_async_remote_copy(
            src_ref=source.at[at],
            dst_ref=target.at[at],
            send_sem=sent.at[index],
            recv_sem=arrived.at[index],
            device_id={"wide": neighbours[direction]},
            device_id_type=MESH,
        )

    lanes = [(array, direction) for array in range(arrays) for direction in range(2)]
    for array, direction in lanes:
        copy(0, array, direction, 0).start()

    vectors = small_ins[0].shape[0]
    mine = narrow_all.at[narrow]
    narrow_all[narrow] = small_ins[0][...] + small_ins[1][...]

    def to_narrow(step):
        return pltpu.make_async_remote_copy(
            src_ref=mine,
            dst_ref=mine,
            send_sem=narrow_sent.at[step],
            recv_sem=narrow_arrived.at[step],
            device_id={"narrow": lax.rem(narrow + step, NARROW)},
            device_id_type=MESH,
        )

    for step in range(1, NARROW):
        to_narrow(step).start()
    for step in range(1, NARROW):
        to_narrow(step).wait()
    total = narrow_all[0]
    for index in range(1, NARROW):
        total = total + narrow_all[index]
    wide_all[wide] = total + small_ins[2][...]
    own = wide_all.at[wide]

    def to_wide(step):
        return pltpu.make_async_remote_copy(
            src_ref=own,
            dst_ref=own,
            send_sem=wide_sent.at[step],
            recv_sem=wide_arrived.at[step],
            device_id={"wide": lax.rem(wide + step, members)},
            device_id_type=MESH,
        )

    @pl.loop(1, members)
    def _(step):
        to_wide(step).start()

    @pl.loop(0, members - 2)
    def _(step):
        for array, direction in lanes:
            at = piece(direction, step + 1)
            landing(0, array, direction, step).wait_recv()
            data[array][at] = (data[array][at].astype(FLOAT) + landed[array][at].astype(FLOAT)).astype(HALF)
            copy(0, array, direction, step + 1).start()

    last = members - 1
    for array, direction in lanes:
        at = piece(direction, last)
        landing(0, array, direction, last - 1).wait_recv()
        results[array][at] = (data[array][at].astype(FLOAT) + landed[array][at].astype(FLOAT)).astype(HALF)
        copy(1, array, direction, last).start()

    @pl.loop(last, 2 * last - 1)
    def _(step):
        for array, direction in lanes:
            landing(1, array, direction, step).wait_recv()
            copy(1, array, direction, step + 1).start()

    for array, direction in lanes:
        landing(1, array, direction, 2 * last - 1).wait_recv()

    @pl.loop(1, members)
    def _(step):
        to_wide(step).wait()

    small_out[...] = jnp.zeros_like(small_out)

    @pl.loop(0, members)
    def _(index):
        small_out[...] += wide_all[index]

    @pl.loop(0, last)
    def _(step):
        for array, direction in lanes:
            copy(0, array, direction, step).wait_send()
            copy(1, array, direction, last + step).wait_send()


def run_sum_wide(members, arrays, narrow_small, narrow_more, wide_small):
    width = narrow_small.shape[1]
    shaped = []
    for array in arrays:
        size = array.size // (2 * members)
        columns = max(LANES, array.shape[1] * 8 // members)
        shaped.append(array.reshape(2 * members, size // columns, columns))
    copies = 4 * len(arrays) * (members - 1)
    results = call(
        partial_named(sum_wide, members, len(arrays)),
        [(a.shape, HALF) for a in shaped] + [((8, width), FLOAT)],
        [IN_VMEM] * (len(arrays) + 3),
        (*shaped, narrow_small, narrow_more, wide_small),
        [pltpu.VMEM(a.shape, HALF) for a in shaped]
        + [
            pltpu.VMEM((NARROW, 8, width), FLOAT),
            pltpu.VMEM((members, 8, width), FLOAT),
            DMA((copies,)),
            DMA((copies,)),
            DMA((NARROW,)),
            DMA((NARROW,)),
            DMA((members,)),
            DMA((members,)),
        ],
        4,
        10**6,
        24 << 20,
    )
    return [r.reshape(a.shape) for r, a in zip(results, arrays)], results[-1]


def partial_named(function, *args):
    bound = partial(function, *args)
    bound.__name__ = function.__name__
    return bound


def per_device(
    stream_one,
    stream_two,
    attention_gain,
    attention_shift,
    query_proj,
    value_proj,
    output_proj,
    forward_gain,
    forward_shift,
    up_proj,
    up_bias,
    down_proj,
    down_bias,
    bucket_ids,
    sort_orders,
    doc_lengths,
    cotan_one,
    cotan_two,
):
    members = lax.axis_size("wide")
    row = lambda vector: vector.reshape(1, -1)
    across = [(i, (i + NARROW // 2) % NARROW) for i in range(NARROW)]
    orders, docs = sort_orders[0], doc_lengths[0]
    rounds = orders.shape[0]
    gain_one, gain_two = row(attention_gain), row(forward_gain)

    gathered, queries, keys, values, query_features, key_features, bucket_sums = run_project_in(
        stream_two, gain_one, row(attention_shift), query_proj, value_proj, orders, docs, bucket_ids
    )
    cotan_two_later, queries = lax.optimization_barrier((cotan_two, queries))
    cotan_far = lax.ppermute(cotan_two_later, "narrow", across)
    merged, logs = run_attention(queries, keys, values, query_features, key_features, docs, rounds)
    out_one, middle, whole, cotans, active, grad_hidden = run_feed_in(
        merged, output_proj, stream_one, gain_two, row(forward_shift), up_proj, row(up_bias), down_proj, cotan_two, cotan_far
    )
    grad_one, grad_merged, grad_up, grad_down, grad_out, fed_own, fed_far, sums_two = run_feed_back(
        grad_hidden, up_proj, middle, gain_two, cotan_one, active, down_proj, cotans, whole, merged, output_proj
    )
    fed_other = lax.ppermute(fed_far, "narrow", across)
    grad_query, grad_value = run_attention_back(
        queries, keys, values, grad_merged, merged, logs, query_features, key_features, docs, rounds
    )
    out_two, grad_two, grad_weights, sums_one = run_project_back(
        grad_query, grad_value, query_proj, value_proj, gathered, stream_two, gain_one, cotan_two, fed_own, fed_other, row(down_bias)
    )
    width = stream_one.shape[1]
    bucket_row = bucket_sums[:rounds, :NB].reshape(1, -1)
    bucket_row = jnp.pad(bucket_row, ((0, 0), (0, width - bucket_row.shape[1])))
    blank = jnp.zeros((1, width), FLOAT)
    narrow_small = jnp.concatenate([sums_one[0:2], sums_two[0:2], bucket_row, blank, blank, blank], axis=0)
    wide_small = jnp.concatenate([blank] * 5 + [sums_two[2:4], blank], axis=0)
    (grad_up, grad_down, grad_out, grad_weights), small = run_sum_wide(
        members, [grad_up, grad_down, grad_out, grad_weights], narrow_small, jnp.zeros_like(narrow_small), wide_small
    )
    heads = query_proj.shape[1]
    return (
        out_one,
        out_two,
        grad_one,
        grad_two,
        small[0],
        small[1],
        grad_weights[:, :heads].astype(FLOAT),
        grad_weights[:, heads:].astype(FLOAT),
        grad_out.astype(FLOAT),
        small[2],
        small[3],
        grad_up.astype(FLOAT),
        small[5],
        grad_down.astype(FLOAT),
        small[6],
        small[4, : rounds * NB].reshape(rounds, NB).astype(jnp.int32),
    )


def solution(mesh):
    rows = P(("wide", "narrow"), None)
    columns = P(None, "narrow")
    return jax.shard_map(
        per_device,
        mesh=mesh,
        in_specs=(
            rows,
            rows,
            P(),
            P(),
            columns,
            columns,
            P("narrow", None),
            P(),
            P(),
            columns,
            P("narrow"),
            P("narrow", None),
            P(),
            rows,
            P("wide", None, None),
            P("wide", None),
            rows,
            rows,
        ),
        out_specs=(
            rows,
            rows,
            rows,
            rows,
            P(),
            P(),
            columns,
            columns,
            P("narrow", None),
            P(),
            P(),
            columns,
            P("narrow"),
            P("narrow", None),
            P(),
            P(),
        ),
        check_vma=False,
    )
```

```python
import math
from types import SimpleNamespace

import jax
import jax.numpy as jnp
from jax import lax
from jax.experimental import pallas as pl
from jax.experimental.pallas import tpu as pltpu
from jax.sharding import PartitionSpec as P

HD = 128
GROUP = 64
NB = 24
MOST = 768
BLOCK = 256
LANES = 128
CHUNK = 128
NARROW = 4
VMEM_LIMIT = 60 << 20

FLOAT = jnp.float32
HALF = jnp.bfloat16
NEG = -1e30
EXP_SCALE = math.log2(math.e) / math.sqrt(HD)
FACTOR = 1.0 / math.sqrt(HD)
MESH = pl.DeviceIdType.MESH
IN_VMEM = pl.BlockSpec(memory_space=pltpu.VMEM)
IN_SMEM = pl.BlockSpec(memory_space=pltpu.SMEM)
ANYWHERE = pl.BlockSpec(memory_space=pl.ANY)
DMA = pltpu.SemaphoreType.DMA
WIDE = "wide"
DOCS = "docs"
FROM_HBM = "_any"


def normalize(inputs):
    center = inputs - jnp.mean(inputs, axis=-1, keepdims=True)
    inverse = lax.rsqrt(jnp.mean(center * center, axis=-1, keepdims=True) + 1e-05)
    return (center * inverse, inverse)


def norm_back(grad_out, scaled, inverse, gain):
    spread = grad_out * gain
    return inverse * (
        spread
        - jnp.mean(spread, axis=-1, keepdims=True)
        - scaled * jnp.mean(spread * scaled, axis=-1, keepdims=True)
    )


def contract_rows(left, right):
    return lax.dot_general(left, right, (((0,), (0,)), ((), ())), preferred_element_type=FLOAT)


def times_transpose(left, right):
    return lax.dot_general(left, right, (((1,), (1,)), ((), ())), preferred_element_type=FLOAT)


def times(left, right):
    return jnp.dot(left, right, preferred_element_type=FLOAT)


def column_sums(rows):
    return times(jnp.ones((8, rows.shape[0]), rows.dtype), rows)[0:1]


class Place:
    def __init__(self):
        index = lax.axis_index("narrow")
        core, chip = lax.rem(index, 2), lax.div(index, 2)
        self.me = index
        self.near = 2 * chip + 1 - core
        self.far = 2 * (1 - chip) + core
        self.cross = 2 * (1 - chip) + 1 - core


def span(start, size):
    return pl.ds(pl.multiple_of(start, size), size)


def remote(source, target, sent, arrived, other):
    return pltpu.make_async_remote_copy(
        src_ref=source,
        dst_ref=target,
        send_sem=sent,
        recv_sem=arrived,
        device_id={"narrow": other},
        device_id_type=MESH,
    )


class Gather:
    def __init__(self, place, whole, rows, sems):
        self.place, self.whole, self.rows = place, whole, rows
        self.sent, self.arrived = sems
        self.chunks = rows // CHUNK

    def at(self, owner, chunk):
        return self.whole.at[span(owner * self.rows + chunk * CHUNK, CHUNK), :]

    def copy(self, lane, owner, chunk, other):
        index = lane * self.chunks + chunk
        piece = self.at(owner, chunk)
        return remote(piece, piece, self.sent.at[index], self.arrived.at[index], other)

    def to_far(self, chunk):
        return self.copy(0, self.place.me, chunk, self.place.far)

    def to_near(self, chunk):
        return self.copy(1, self.place.me, chunk, self.place.near)

    def onward(self, chunk):
        return self.copy(2, self.place.far, chunk, self.place.near)

    def send(self, chunk):
        self.to_far(chunk).start()
        self.to_near(chunk).start()

    def take_near(self, chunk):
        self.to_near(chunk).wait_recv()

    def take_far(self, chunk):
        self.to_far(chunk).wait_recv()
        self.onward(chunk).start()

    def take_cross(self, chunk):
        self.onward(chunk).wait_recv()

    def finish(self):
        @pl.loop(0, self.chunks)
        def _(chunk):
            self.to_far(chunk).wait_send()
            self.to_near(chunk).wait_send()
            self.onward(chunk).wait_send()


class Scatter:
    def __init__(self, place, term, rows, buffers, sems):
        self.place, self.term, self.rows = place, term, rows
        self.near_out, self.near_in, self.far_out, self.far_in = buffers
        self.sent, self.arrived = sems
        self.chunks = rows // CHUNK

    def to_near(self, part, chunk):
        index = part * self.chunks + chunk
        at = span(chunk * CHUNK, CHUNK)
        return remote(
            self.near_out.at[part, at, :],
            self.near_in.at[part, at, :],
            self.sent.at[index],
            self.arrived.at[index],
            self.place.near,
        )

    def to_far(self, chunk):
        index = 2 * self.chunks + chunk
        at = span(chunk * CHUNK, CHUNK)
        return remote(
            self.far_out.at[at, :], self.far_in.at[at, :], self.sent.at[index], self.arrived.at[index], self.place.far
        )

    def part(self, owner, chunk):
        return self.term(span(owner * self.rows + chunk * CHUNK, CHUNK))

    def start(self, between=lambda: None):
        @pl.loop(0, self.chunks)
        def _(chunk):
            self.near_out[0, span(chunk * CHUNK, CHUNK), :] = self.part(self.place.cross, chunk).astype(HALF)
            self.to_near(0, chunk).start()

        between()

        @pl.loop(0, self.chunks)
        def _(chunk):
            at = span(chunk * CHUNK, CHUNK)
            own = self.part(self.place.far, chunk)
            self.to_near(0, chunk).wait_recv()
            self.far_out[at, :] = (own + self.near_in[0, at, :].astype(FLOAT)).astype(HALF)
            self.to_far(chunk).start()

        between()

        @pl.loop(0, self.chunks)
        def _(chunk):
            self.near_out[1, span(chunk * CHUNK, CHUNK), :] = self.part(self.place.near, chunk).astype(HALF)
            self.to_near(1, chunk).start()

    def chip_sum(self, chunk):
        own = self.part(self.place.me, chunk)
        self.to_near(1, chunk).wait_recv()
        return own + self.near_in[1, span(chunk * CHUNK, CHUNK), :].astype(FLOAT)

    def take_far(self, chunk):
        self.to_far(chunk).wait_recv()
        return self.far_in[span(chunk * CHUNK, CHUNK), :].astype(FLOAT)

    def finish(self):
        @pl.loop(0, self.chunks)
        def _(chunk):
            self.to_near(0, chunk).wait_send()
            self.to_near(1, chunk).wait_send()
            self.to_far(chunk).wait_send()


def pair_features(orders, docs, query_features, key_features, found):
    rounds, length = orders.shape
    groups = length // GROUP
    high_count = length // LANES
    high_rows = -(-high_count // 8) * 8
    count = docs.shape[0]
    depth = query_features.shape[0]
    lane = lax.broadcasted_iota(jnp.int32, (LANES, length), 1)
    low_at = lax.broadcasted_iota(jnp.int32, (LANES, length), 0)
    high_at = lax.broadcasted_iota(jnp.int32, (high_rows, length), 0)
    group_at = lax.broadcasted_iota(jnp.int32, (groups, LANES), 0).astype(FLOAT)
    sorted_group = lax.shift_right_logical(lane, int(math.log2(GROUP))).astype(FLOAT)

    @pl.loop(0, rounds)
    def _(index):
        row = orders[pl.ds(index, 1), :]
        high = jnp.where(high_at == lax.shift_right_logical(row, int(math.log2(LANES))), 1.0, 0.0)
        low = jnp.where(low_at == (row & (LANES - 1)), sorted_group, 0.0)
        found[index, :high_rows, :LANES] = times_transpose(high.astype(HALF), low.astype(HALF))
    place = lax.broadcasted_iota(jnp.int32, (count, LANES), 1)
    which = lax.broadcasted_iota(jnp.int32, (count, LANES), 0)
    begins = jnp.zeros((count, LANES), jnp.int32)
    ends = jnp.zeros((count, LANES), jnp.int32)
    begin = jnp.int32(0)
    for doc in range(count):
        end = begin + docs[doc]
        begins = jnp.where(which == doc, begin, begins)
        ends = jnp.where(which == doc, end, ends)
        begin = end
    rest = jnp.zeros((depth - rounds * groups - count, LANES), FLOAT)
    for block in range(high_count):
        mine, window = [], []
        for index in range(rounds):
            own = found[index, block : block + 1, :LANES]
            after = jnp.where(own == groups - 1.0, 0.0, own + 1.0)
            here = group_at == own
            mine.append(jnp.where(here, 1.0, 0.0))
            window.append(jnp.where(here | (group_at == after), 1.0, 0.0))
        at = place + block * LANES
        same = jnp.where((at >= begins) & (at < ends), 1.0, 0.0)
        lanes = slice(block * LANES, (block + 1) * LANES)
        query_features[:, lanes] = jnp.concatenate([*mine, same * (2.0 * rounds), rest], axis=0).astype(HALF)
        key_features[:, lanes] = jnp.concatenate([*window, same, rest], axis=0).astype(HALF)


def in_turn(place, step):
    flip_core, flip_chip = lax.rem(step, 2), lax.div(step, 2)
    core, chip = lax.rem(place.me, 2), lax.div(place.me, 2)
    core = core + flip_core * (1 - 2 * core)
    chip = chip + flip_chip * (1 - 2 * chip)
    return 2 * chip + core


def take_in_turn(gather, step):
    takes = (gather.take_near, gather.take_far, gather.take_cross)

    @pl.loop(0, gather.chunks)
    def _(chunk):
        for index, take in enumerate(takes):
            if isinstance(step, int):
                if step == index + 1:
                    take(chunk)
            else:
                pl.when(step == index + 1)(lambda take=take: take(chunk))


def pair_bias(query_features, key_features, rounds, diagonal):
    counts = jnp.maximum(contract_rows(key_features, query_features) - 2.0 * rounds, 0.0)
    bias = jnp.where(counts > 0.0, jnp.log2(counts), NEG)
    if diagonal:
        key_at = lax.broadcasted_iota(jnp.int32, bias.shape, 0)
        query_at = lax.broadcasted_iota(jnp.int32, bias.shape, 1)
        bias = jnp.where(key_at < query_at, bias, NEG)
    return bias


def band_steps(length):
    return min(-(-(MOST - 1) // BLOCK), length // BLOCK - 1) + 1


def block_biases(block, steps, features, rounds, bias):
    query_features, key_features = features
    at = span(block * BLOCK, BLOCK)
    for step in range(steps):
        bias[step] = pair_bias(
            query_features[:, at], key_features[:, span((block - step) * BLOCK, BLOCK)], rounds, step == 0
        )


def attend(block, steps, rounds, queries, keys, values, features, merged, logs, bias, scores):
    at = span(block * BLOCK, BLOCK)
    heads = queries.shape[1] // HD
    block_biases(block, steps, features, rounds, bias)
    for head in range(heads):
        part = slice(head * HD, (head + 1) * HD)
        query = queries[at, part]
        peak = jnp.full((1, BLOCK), 2 * NEG, FLOAT)
        for step in range(steps):
            key_at = span((block - step) * BLOCK, BLOCK)
            score = times_transpose(keys[key_at, part], query) * EXP_SCALE + bias[step]
            scores[span((head * steps + step) * BLOCK, BLOCK), :] = score
            peak = jnp.maximum(peak, jnp.max(score, axis=0, keepdims=True))
        alone = peak < 0.5 * NEG
        peak = jnp.where(alone, 0.0, peak)
        total = jnp.zeros((1, BLOCK), FLOAT)
        mixed = jnp.zeros((HD, BLOCK), FLOAT)
        for step in range(steps):
            key_at = span((block - step) * BLOCK, BLOCK)
            powers = jnp.exp2(scores[span((head * steps + step) * BLOCK, BLOCK), :] - peak)
            total = total + jnp.sum(powers, axis=0, keepdims=True)
            mixed = mixed + contract_rows(values[key_at, part], powers.astype(HALF))
        total = jnp.where(alone, 1.0, total)
        mixed = jnp.where(alone, values[at, part].astype(FLOAT).T, mixed / total)
        merged[at, part] = mixed.T.astype(HALF)
        logs[head : head + 1, at] = jnp.where(alone, -NEG, peak + jnp.log2(total))


def attend_back(block, steps, rounds, queries, keys, values, features, grads, merged, logs, dq, dk, dv, bias, after):
    at = span(block * BLOCK, BLOCK)
    heads = queries.shape[1] // HD
    block_biases(block, steps, features, rounds, bias)
    ones = jnp.ones((8, HD), HALF)
    for head in range(heads):
        part = slice(head * HD, (head + 1) * HD)
        query, grad = queries[at, part], grads[at, part]
        log_sum = logs[head : head + 1, at]
        product = grad.astype(FLOAT) * merged[at, part].astype(FLOAT)
        coarse = product.astype(HALF)
        fine = (product - coarse.astype(FLOAT)).astype(HALF)
        along = (times_transpose(ones, coarse) + times_transpose(ones, fine))[0:1]
        grad_query = jnp.zeros((HD, BLOCK), FLOAT)
        for step in range(steps):
            key_at = span((block - step) * BLOCK, BLOCK)
            key = keys[key_at, part]
            weights = jnp.exp2(times_transpose(key, query) * EXP_SCALE + bias[step] - log_sum)
            grad_probs = times_transpose(values[key_at, part], grad)
            grad_scores = (weights * (grad_probs - along)).astype(HALF)
            grad_value = times(weights.astype(HALF), grad)
            grad_key = times(grad_scores, query)
            if step == 0:
                dv[key_at, part] = grad_value
                dk[key_at, part] = grad_key
            else:
                dv[key_at, part] += grad_value
                dk[key_at, part] += grad_key
            grad_query = grad_query + contract_rows(key, grad_scores)
        dq[at, part] = grad_query.T
        after(head)


def finish_attention(queries, grads, logs, dq, dk, dv, grad_query, grad_value):
    length, width = queries.shape

    @pl.loop(0, length // BLOCK)
    def _(block):
        at = span(block * BLOCK, BLOCK)
        alone = jnp.where(logs[:, at] == -NEG, 1.0, 0.0).T
        for head in range(width // HD):
            part = slice(head * HD, (head + 1) * HD)
            grad_value[at, part] = (dv[at, part] + alone[:, head : head + 1] * grads[at, part].astype(FLOAT)).astype(HALF)
            query = queries[at, part].astype(FLOAT)
            key_scale = lax.rsqrt(jnp.sum(query * query, axis=-1, keepdims=True) + 1e-06)
            unit = query * key_scale
            grad_key = dk[at, part] * FACTOR
            key_along = jnp.sum(grad_key * unit, axis=-1, keepdims=True)
            grad_query[at, part] = (dq[at, part] * FACTOR + key_scale * (grad_key - unit * key_along)).astype(HALF)


def gelu_and_slope(hidden):
    square = hidden * hidden
    bend = jnp.tanh(math.sqrt(2.0 / math.pi) * hidden * (1.0 + 0.044715 * square))
    half_more = 0.5 + 0.5 * bend
    slope = half_more + 0.5 * hidden * (1.0 - bend * bend) * (
        math.sqrt(2.0 / math.pi) * (1.0 + 3.0 * 0.044715 * square)
    )
    return hidden * half_more, slope


def weight_grad(result, left, right, rows=None, add=False):
    width = 256
    height = result.shape[1] * result.shape[2] // right.shape[1]
    pieces = width // height
    rows = slice(None) if rows is None else rows

    @pl.loop(0, left.shape[1] // width)
    def _(index):
        block = contract_rows(left[rows, span(index * width, width)], right[rows, :])
        at = pl.ds(index * pieces, pieces)
        block = block.reshape(pieces, *result.shape[1:])
        if add:
            block = block + result[at].astype(FLOAT)
        result[at] = block.astype(result.dtype)


def ring_place(members, index):
    column, row = lax.rem(index, 2), lax.div(index, 2)
    return row + column * (members - 1 - 2 * row)


def ring_member(members, place):
    back = lax.div(place, members // 2)
    return 2 * place + back * (2 * (members - 1 - place) + 1 - 2 * place)


class Ring:
    def __init__(self, members, data, landed, result, sent, arrived, kept):
        self.members, self.data, self.landed, self.result = members, data, landed, result
        self.sent, self.arrived, self.kept, self.stage = sent, arrived, kept, 0
        self.here = ring_place(members, lax.axis_index("wide"))
        self.neighbours = (
            ring_member(members, lax.rem(self.here + 1, members)),
            ring_member(members, lax.rem(self.here + members - 1, members)),
        )

    def piece(self, direction, step):
        if direction == 0:
            return 2 * lax.rem(self.here - step + 2 * self.members, self.members)
        return 2 * lax.rem(self.here + step, self.members) + 1

    def copy(self, direction, step, at, gathering, fresh):
        index = direction * 2 * (self.members - 1) + step
        source = self.landed if gathering and not fresh else self.data
        return pltpu.make_async_remote_copy(
            src_ref=source.at[at],
            dst_ref=self.landed.at[at],
            send_sem=self.sent.at[index],
            recv_sem=self.arrived.at[index],
            device_id={"wide": self.neighbours[direction]},
            device_id_type=MESH,
        )

    def outgoing(self, direction, step, gathering=False, fresh=False):
        return self.copy(direction, step, self.piece(direction, step), gathering, fresh)

    def incoming(self, direction, step, gathering=False):
        return self.copy(direction, step, self.piece(direction, step + 1), gathering, False)

    def begin(self):
        for direction in range(2):
            self.outgoing(direction, 0).start()

    def add(self, direction, step):
        self.incoming(direction, step).wait_recv()
        at = self.piece(direction, step + 1)
        self.data[at] = (self.data[at].astype(FLOAT) + self.landed[at].astype(FLOAT)).astype(HALF)
        return at

    def keep(self, direction, step):
        at = self.piece(direction, step)
        source = self.data if isinstance(step, int) and step == self.members - 1 else self.landed
        return pltpu.make_async_copy(
            source.at[at], self.result.at[at], self.kept.at[direction * self.members + step - (self.members - 1)]
        )

    def advance(self):
        stage, last = self.stage, self.members - 1
        if stage == 14:
            return
        self.stage = stage + 1
        low, high = stage * 2 * last // 14, (stage + 1) * 2 * last // 14

        def repeat(begin, end, act):
            if end == begin + 1:
                act(begin)
            elif end > begin:
                pl.loop(begin, end)(act)

        def reduce(step):
            for direction in range(2):
                self.add(direction, step)
                self.outgoing(direction, step + 1).start()

        def forward(step):
            for direction in range(2):
                self.incoming(direction, step, True).wait_recv()
                self.outgoing(direction, step + 1, True).start()
                self.keep(direction, step + 1).start()

        repeat(low, min(high, last - 1), reduce)
        if low <= last - 1 < high:
            for direction in range(2):
                self.add(direction, last - 1)
                self.outgoing(direction, last, True, True).start()
                self.keep(direction, last).start()
        repeat(max(low, last), min(high, 2 * last - 1), forward)
        if low <= 2 * last - 1 < high:
            for direction in range(2):
                self.incoming(direction, 2 * last - 1, True).wait_recv()
                self.keep(direction, 2 * last).start()

    def finish(self):
        last = self.members - 1
        for direction in range(2):
            self.keep(direction, last).wait()
            self.outgoing(direction, last, True, True).wait_send()

        @pl.loop(0, last)
        def _(step):
            for direction in range(2):
                self.outgoing(direction, step).wait_send()

        @pl.loop(last + 1, 2 * last)
        def _(step):
            for direction in range(2):
                self.outgoing(direction, step, True).wait_send()
                self.keep(direction, step).wait()

        for direction in range(2):
            self.keep(direction, 2 * last).wait()


class Exchange:
    def __init__(self, members, data, landed, result, first, unit, bits, sems, stored):
        self.members, self.data, self.landed, self.result = members, data, landed, result
        self.first, self.unit, self.bits = first, unit, bits
        self.sent, self.arrived, self.stored, self.stage = *sems, stored, 0
        self.wide = lax.axis_index("wide")

    def bit(self, step):
        return lax.rem(lax.div(self.wide, 1 << self.bits[step]), 2)

    def size(self, step):
        return self.unit * (self.members >> (step + 1))

    def part(self, step, kept):
        start = self.first
        for before in range(step):
            start = start + self.bit(before) * self.size(before)
        bit = self.bit(step)
        return pl.ds(start + (bit if kept else 1 - bit) * self.size(step), self.size(step))

    def landing(self, step):
        return pl.ds(self.first + self.unit * self.members - 2 * self.size(step), self.size(step))

    def copy(self, step, gathering):
        index = step + gathering * len(self.bits)
        at = self.part(step, gathering)
        source = self.result if gathering and step < len(self.bits) - 1 else self.data
        return pltpu.make_async_remote_copy(
            src_ref=source.at[at],
            dst_ref=self.result.at[at] if gathering else self.landed.at[self.landing(step)],
            send_sem=self.sent.at[index],
            recv_sem=self.arrived.at[index],
            device_id={"wide": self.wide + (1 - 2 * self.bit(step)) * (1 << self.bits[step])},
            device_id_type=MESH,
        )

    def begin(self):
        self.copy(0, False).start()

    def advance(self):
        count, stage = len(self.bits), self.stage
        if stage == 2 * count:
            return
        self.stage = stage + 1
        if stage < count:
            self.copy(stage, False).wait_recv()
            kept, landed = self.part(stage, True), self.landing(stage)

            @pl.loop(0, self.size(stage))
            def _(index):
                at = kept.start + index
                self.data[at] = (
                    self.data[at].astype(FLOAT) + self.landed[landed.start + index].astype(FLOAT)
                ).astype(HALF)

        else:
            self.copy(2 * count - 1 - stage, True).wait_recv()
        if stage < count - 1:
            self.copy(stage + 1, False).start()
            return
        if stage == count - 1:
            self.store().start()
        if stage == count:
            self.store().wait()
        if stage < 2 * count - 1:
            self.copy(2 * count - 2 - stage, True).start()

    def store(self):
        at = self.part(len(self.bits) - 1, True)
        return pltpu.make_async_copy(self.data.at[at], self.result.at[at], self.stored)

    def finish(self):
        for step in range(len(self.bits)):
            self.copy(step, False).wait_send()
            self.copy(step, True).wait_send()


class Everyone:
    def __init__(self, axis, slots, sent, arrived):
        self.axis, self.slots, self.sent, self.arrived = axis, slots, sent, arrived
        self.me, self.members = lax.axis_index(axis), slots.shape[0]

    def copy(self, step):
        mine = self.slots.at[self.me]
        return pltpu.make_async_remote_copy(
            src_ref=mine,
            dst_ref=mine,
            send_sem=self.sent.at[step],
            recv_sem=self.arrived.at[step],
            device_id={self.axis: lax.rem(self.me + step, self.members)},
            device_id_type=MESH,
        )

    def send(self, value):
        self.slots[self.me] = value

        @pl.loop(1, self.members)
        def _(step):
            self.copy(step).start()

    def total(self):
        @pl.loop(1, self.members)
        def _(step):
            self.copy(step).wait()

        return lax.fori_loop(1, self.members, lambda index, total: total + self.slots[index], self.slots[0])


def advance(*exchanges):
    for exchange in exchanges:
        exchange.advance()


def meet_all(members):
    barrier = pltpu.get_barrier_semaphore()
    narrow, wide = lax.axis_index("narrow"), lax.axis_index("wide")

    @pl.loop(1, NARROW)
    def _(step):
        pl.semaphore_signal(
            barrier, inc=1, device_id={"narrow": lax.rem(narrow + step, NARROW)}, device_id_type=MESH
        )

    @pl.loop(1, members)
    def _(step):
        pl.semaphore_signal(barrier, inc=1, device_id={"wide": lax.rem(wide + step, members)}, device_id_type=MESH)

    pl.semaphore_wait(barrier, NARROW - 1 + members - 1)


def layer(members, ref):
    place = Place()
    second_rows = ref.stream_two
    rows, width = second_rows.shape
    orders, docs = ref.orders, ref.docs
    rounds, length = orders.shape
    heads = ref.wq.shape[1]
    chunks = rows // CHUNK
    whole_one, whole_two, cotans, grad_rows = (ref.whole_one, ref.whole_two, ref.cotans, ref.grad_rows)
    queries, keys, values, merged, logs = (ref.queries, ref.keys, ref.values, ref.merged, ref.logs)
    features = (ref.query_features, ref.key_features)
    wq, wv, wo, up, down = (ref.wq, ref.wv, ref.wo, ref.up, ref.down)
    active, grad_hidden, middle, first_rows = (ref.active, ref.grad_hidden, ref.middle, ref.first_rows)
    grad_merged, bias, sums = ref.grad_merged, ref.bias, ref.sums
    dq, dk, dv = (ref.totals.at[pl.ds(i * length, length), :] for i in range(3))
    own_at, far_at = span(place.me * rows, rows), span(place.far * rows, rows)
    loads, stores = ref.loads, ref.stores

    def load(index, source, target):
        copy = pltpu.make_async_copy(source, target, loads.at[index])
        copy.start()
        return copy

    load_wq, load_wv = load(0, ref.wq_any, wq), load(1, ref.wv_any, wv)
    load_cotan = load(2, ref.cotan_two_any, cotans.at[own_at, :])
    load_wo, load_first = load(3, ref.wo_any, wo), load(4, ref.stream_one_any, first_rows)
    load_down, load_up = load(5, ref.down_any, down), load(6, ref.up_any, up)
    meet_all(members)

    up_ring, down_ring = rings = [
        Ring(
            members, ref.sum_data[i], ref.sum_landed[i], ref.sum_results[i], ref.ring_sent.at[i], ref.ring_arrived.at[i],
            ref.ring_kept.at[i],
        )
        for i in range(2)
    ]
    bits = list(range(members.bit_length() - 1))
    swapped = bits[1::-1] + bits[2:]
    lanes = ((2, 0, bits), (2, members, swapped), (3, 0, bits), (3, members, swapped))
    out_sum, out_swap, in_sum, in_swap = exchanges = [
        Exchange(
            members, ref.sum_data[array], ref.sum_landed[array], ref.sum_results[array], first, 1, order,
            (ref.sum_sent.at[lane], ref.sum_arrived.at[lane]), ref.sum_stored.at[lane],
        )
        for lane, (array, first, order) in enumerate(lanes)
    ]
    queue = [up_ring, down_ring]

    def serve(*more):
        ring = queue.pop(0)
        queue.append(ring)
        advance(ring, *more)

    gather = Gather(place, whole_one, rows, (ref.gather_sent.at[0], ref.gather_arrived.at[0]))

    @pl.loop(0, chunks)
    def _(chunk):
        scaled, _ = normalize(second_rows[span(chunk * CHUNK, CHUNK), :].astype(FLOAT))
        normed = (scaled * ref.gain_one[...] + ref.shift_one[...]).astype(HALF)
        whole_one[span(place.me * rows + chunk * CHUNK, CHUNK), :] = normed
        gather.send(chunk)

    pair_features(orders, docs, *features, bias)
    level = lax.broadcasted_iota(jnp.int32, (LANES, rows), 0)
    counted = jnp.ones((8, rows), HALF)
    sums[...] = jnp.zeros_like(sums)
    for index in range(rounds):
        found = jnp.where(level == ref.buckets[index : index + 1, :], 1.0, 0.0).astype(HALF)
        sums[4:5, index * LANES : (index + 1) * LANES] = times_transpose(counted, found)[0:1]
    load_wq.wait()
    load_wv.wait()

    def project(owner):
        at = span(owner * rows, rows)
        query = times(whole_one[at, :], wq[...]).astype(HALF)
        queries[at, :] = query
        for head in range(heads // HD):
            part = query[:, head * HD : (head + 1) * HD].astype(FLOAT)
            scale = lax.rsqrt(jnp.sum(part * part, axis=-1, keepdims=True) + 1e-06)
            keys[at, head * HD : (head + 1) * HD] = (part * scale).astype(HALF)
        values[at, :] = times(whole_one[at, :], wv[...]).astype(HALF)

    @pl.loop(0, NARROW)
    def _(step):
        take_in_turn(gather, step)
        project(in_turn(place, step))

    gather.finish()

    load_cotan.wait()
    spread = Gather(place, cotans, rows, (ref.gather_sent.at[1], ref.gather_arrived.at[1]))

    @pl.loop(0, chunks)
    def _(chunk):
        spread.send(chunk)

    steps = band_steps(length)
    blocks = length // BLOCK

    def forward(block, count):
        attend(block, count, rounds, queries, keys, values, features, merged, logs, bias, ref.totals)

    for block in range(steps - 1):
        forward(block, block + 1)

    @pl.loop(steps - 1, blocks)
    def _(block):
        forward(block, steps)

    buffers = (ref.near_out, ref.near_in, ref.far_out, ref.far_in)
    load_wo.wait()
    scatter = Scatter(
        place, lambda at: times(merged[at, :], wo[...]), rows, buffers, (ref.scatter_sent.at[0], ref.scatter_arrived.at[0])
    )
    scatter.start()
    load_first.wait()

    @pl.loop(0, chunks)
    def _(chunk):
        at = span(chunk * CHUNK, CHUNK)
        middle[at, :] = first_rows[at, :].astype(FLOAT) + scatter.chip_sum(chunk)

    @pl.loop(0, chunks)
    def _(chunk):
        spread.take_near(chunk)
        spread.take_far(chunk)

    load_down.wait()
    half_width = width // 2

    def grad_active(owner):
        @pl.loop(0, 2)
        def _(half):
            at = span(half * half_width, half_width)
            grad_hidden[span(owner * rows, rows), at] = times_transpose(
                cotans[span(owner * rows, rows), :], down[at, :]
            ).astype(HALF)

    @pl.loop(0, NARROW)
    def _(step):
        @pl.when(step == NARROW - 1)
        def _():
            @pl.loop(0, chunks)
            def _(chunk):
                spread.take_cross(chunk)

        grad_active(in_turn(place, step))

    gather = Gather(place, whole_two, rows, (ref.gather_sent.at[2], ref.gather_arrived.at[2]))
    load_up.wait()

    @pl.loop(0, chunks)
    def _(chunk):
        at = span(chunk * CHUNK, CHUNK)
        value = middle[at, :] + scatter.take_far(chunk)
        middle[at, :] = value
        first_rows[at, :] = value.astype(HALF)
        scaled, _ = normalize(value)
        whole_two[span(place.me * rows + chunk * CHUNK, CHUNK), :] = (
            scaled * ref.gain_two[...] + ref.shift_two[...]
        ).astype(HALF)
        gather.send(chunk)

    store_one = pltpu.make_async_copy(first_rows, ref.out_one, stores.at[0])
    store_one.start()

    def feed(step):
        take_in_turn(gather, step)
        row_at = span(in_turn(place, step) * rows, rows)

        @pl.loop(0, 2)
        def _(half):
            at = span(half * half_width, half_width)
            value, slope = gelu_and_slope(times(whole_two[row_at, :], up[:, at]) + ref.up_bias[:, at])
            active[row_at, at] = value.astype(HALF)
            grad_hidden[row_at, at] = (grad_hidden[row_at, at].astype(FLOAT) * slope).astype(HALF)

    chip = lax.div(place.me, 2)
    here, there = span(chip * 2 * rows, 2 * rows), span((1 - chip) * 2 * rows, 2 * rows)
    pl.loop(0, NARROW // 2)(feed)
    weight_grad(ref.sum_data[1], active, cotans, here)
    weight_grad(ref.sum_data[0], whole_two, grad_hidden, here)
    pl.loop(NARROW // 2, NARROW)(feed)
    scatter.finish()

    scatter = Scatter(
        place,
        lambda at: times_transpose(grad_hidden[at, :], up[...]),
        rows,
        buffers,
        (ref.scatter_sent.at[1], ref.scatter_arrived.at[1]),
    )
    scatter.start()
    store_one.wait()
    load_cotan_one = load(7, ref.cotan_one_any, first_rows)
    weight_grad(ref.sum_data[1], active, cotans, there, True)
    down_ring.begin()
    weight_grad(ref.sum_data[0], whole_two, grad_hidden, there, True)
    up_ring.begin()
    queue.reverse()
    back = Gather(place, grad_rows, rows, (ref.gather_sent.at[3], ref.gather_arrived.at[3]))
    load_cotan_one.wait()

    for chunk in range(chunks):
        at = span(chunk * CHUNK, CHUNK)
        grad_normed = scatter.chip_sum(chunk) + scatter.take_far(chunk)
        scaled, inverse = normalize(middle[at, :])
        grad = first_rows[at, :].astype(FLOAT) + norm_back(grad_normed, scaled, inverse, ref.gain_two[...])
        grad_rows[span(place.me * rows + chunk * CHUNK, CHUNK), :] = grad.astype(HALF)
        back.send(chunk)
        sums[2:3, :] += jnp.sum(grad_normed * scaled, axis=0, keepdims=True)
        sums[3:4, :] += jnp.sum(grad_normed, axis=0, keepdims=True)
        serve()
        serve()

    def merge_back(step):
        at = span(in_turn(place, step) * rows, rows)
        grad_merged[at, :] = times_transpose(grad_rows[at, :], wo[...]).astype(HALF)

    store_grad = pltpu.make_async_copy(grad_rows.at[own_at, :], ref.grad_one, stores.at[1])
    store_grad.start()
    own_sums = ref.wide_all.at[lax.axis_index(WIDE)]
    own_sums[5:6, :] = column_sums(grad_hidden[...])
    own_sums[6:7, :] = column_sums(cotans[...])
    scatter.finish()
    gather.finish()
    spread.finish()

    serve()
    merge_back(0)
    take_in_turn(back, 1)
    merge_back(1)
    serve()
    for chunk in range(chunks):
        back.take_far(chunk)
        serve()
    merge_back(2)
    take_in_turn(back, 3)
    merge_back(3)
    serve()
    weight_grad(ref.sum_data[2], merged, grad_rows)
    out_sum.begin()
    out_swap.begin()
    serve()

    fed = Scatter(
        place, lambda at: times(active[at, :], down[...]), rows, buffers, (ref.scatter_sent.at[2], ref.scatter_arrived.at[2])
    )
    fed.start(serve)
    serve()

    for block in range(blocks):

        def after(head, block=block):
            if block > 1 or head == heads // HD - 1:
                serve(*([out_sum, out_swap][head % 2 : head % 2 + 1] if block > 1 else []))

        attend_back(
            block, min(block + 1, steps), rounds, queries, keys, values, features, grad_merged, merged, logs, dq, dk, dv, bias, after
        )

    grad_query, grad_value = ref.grad_query, ref.grad_value
    finish_attention(queries, grad_merged, logs, dq, dk, dv, grad_query, grad_value)
    serve()
    weight_grad(ref.sum_data[3], whole_one, ref.grad_both)
    in_sum.begin()
    in_swap.begin()
    serve(out_sum, out_swap)

    @pl.loop(0, chunks)
    def _(chunk):
        at = span(chunk * CHUNK, CHUNK)
        middle[at, :] = fed.chip_sum(chunk) + fed.take_far(chunk) + ref.down_bias[...]
        first_two = second_rows[at, :].astype(FLOAT) + middle[at, :]
        cotans[span(place.near * rows + chunk * CHUNK, CHUNK), :] = first_two.astype(HALF)

    store_two = pltpu.make_async_copy(cotans.at[span(place.near * rows, rows), :], ref.out_two, stores.at[2])
    store_two.start()
    fed.finish()
    ready = ref.ready
    for other in (place.near, place.far):
        pl.semaphore_signal(ready, inc=1, device_id={"narrow": other}, device_id_type=MESH)
    pl.semaphore_wait(ready, 2)

    scatter = Scatter(
        place,
        lambda at: times_transpose(grad_query[at, :], wq[...]) + times_transpose(grad_value[at, :], wv[...]),
        rows,
        buffers,
        (ref.scatter_sent.at[3], ref.scatter_arrived.at[3]),
    )
    scatter.start(lambda: serve(in_swap, in_sum))
    serve(in_swap, in_sum)

    for chunk in range(chunks):
        at = span(chunk * CHUNK, CHUNK)
        grad_normed = scatter.chip_sum(chunk) + scatter.take_far(chunk)
        scaled, inverse = normalize(second_rows[at, :].astype(FLOAT))
        mine = span(place.me * rows + chunk * CHUNK, CHUNK)
        cotans[mine, :] = (
            cotans[mine, :].astype(FLOAT) + norm_back(grad_normed, scaled, inverse, ref.gain_one[...])
        ).astype(HALF)
        sums[0:1, :] += jnp.sum(grad_normed * scaled, axis=0, keepdims=True)
        sums[1:2, :] += jnp.sum(grad_normed, axis=0, keepdims=True)
        serve(*exchanges)
        serve()

    store_last = pltpu.make_async_copy(cotans.at[own_at, :], ref.grad_two, stores.at[3])
    store_last.start()
    over_narrow = Everyone("narrow", ref.narrow_all, ref.narrow_sent, ref.narrow_arrived)
    over_wide = Everyone("wide", ref.wide_all, ref.wide_sent, ref.wide_arrived)
    over_narrow.send(sums[...])
    serve(*exchanges)
    sums[...] = over_narrow.total()
    sums[5:7, :] = own_sums[5:7, :]
    over_wide.send(sums[...])
    while min(exchange.stage for exchange in exchanges) < 2 * len(bits) or min(ring.stage for ring in rings) < 14:
        serve(*exchanges)
    ref.small[...] = over_wide.total()
    scatter.finish()
    back.finish()
    for copy in (store_grad, store_two, store_last):
        copy.wait()
    for exchange in [*exchanges, *rings]:
        exchange.finish()


def pieces(members, shape):
    columns = shape[1] if members <= 8 else LANES
    return (2 * members, shape[0] * shape[1] // (2 * members * columns), columns)


def run_layer(members, args):
    rows, width = args.stream_two.shape
    length, heads, hidden = NARROW * rows, args.wq_any.shape[1], args.up_any.shape[1]
    rounds = args.orders.shape[0]
    chunks = rows // CHUNK
    depth = -(-(rounds * (length // GROUP) + args.docs.shape[0]) // LANES) * LANES
    weights = [(width, hidden), (hidden, width), (heads, width), (width, 2 * heads)]
    cut = [pieces(members, shape) for shape in weights]
    args = vars(args)
    in_specs = [IN_SMEM if k == DOCS else ANYWHERE if k.endswith(FROM_HBM) else IN_VMEM for k in args]
    outs = dict(
        out_one=((rows, width), HALF),
        out_two=((rows, width), HALF),
        grad_one=((rows, width), HALF),
        grad_two=((rows, width), HALF),
        small=((8, width), FLOAT),
    )
    out_shape = [jax.ShapeDtypeStruct(*o) for o in outs.values()] + [jax.ShapeDtypeStruct(shape, HALF) for shape in cut]
    out_specs = [ANYWHERE] * 4 + [IN_VMEM] + [ANYWHERE] * len(cut)
    tall = pltpu.VMEM((length, width), HALF)
    slim = pltpu.VMEM((length, heads), HALF)
    gather_sems, scatter_sems = DMA((4, 3 * chunks)), DMA((4, 3 * chunks))
    sum_sems = DMA((4, 2 * (members.bit_length() - 1)))
    ring_sems = DMA((2, 4 * (members - 1)))
    scratch = dict(
        whole_one=tall,
        whole_two=tall,
        cotans=tall,
        grad_rows=tall,
        active=pltpu.VMEM((length, hidden), HALF),
        grad_hidden=pltpu.VMEM((length, hidden), HALF),
        queries=slim,
        keys=slim,
        values=slim,
        merged=slim,
        grad_merged=slim,
        grad_both=pltpu.VMEM((length, 2 * heads), HALF),
        logs=pltpu.VMEM((8, length), FLOAT),
        query_features=pltpu.VMEM((depth, length), HALF),
        key_features=pltpu.VMEM((depth, length), HALF),
        wq=pltpu.VMEM((width, heads), HALF),
        wv=pltpu.VMEM((width, heads), HALF),
        wo=pltpu.VMEM((heads, width), HALF),
        up=pltpu.VMEM((width, hidden), HALF),
        down=pltpu.VMEM((hidden, width), HALF),
        middle=pltpu.VMEM((rows, width), FLOAT),
        first_rows=pltpu.VMEM((rows, width), HALF),
        bias=pltpu.VMEM((max(rounds, band_steps(length)), BLOCK, BLOCK), FLOAT),
        totals=pltpu.VMEM((3 * length, heads), FLOAT),
        sums=pltpu.VMEM((8, width), FLOAT),
        near_out=pltpu.VMEM((2, rows, width), HALF),
        near_in=pltpu.VMEM((2, rows, width), HALF),
        far_out=pltpu.VMEM((rows, width), HALF),
        far_in=pltpu.VMEM((rows, width), HALF),
        narrow_all=pltpu.VMEM((NARROW, 8, width), FLOAT),
        wide_all=pltpu.VMEM((members, 8, width), FLOAT),
        narrow_sent=DMA((NARROW,)),
        narrow_arrived=DMA((NARROW,)),
        wide_sent=DMA((members,)),
        wide_arrived=DMA((members,)),
        loads=DMA((8,)),
        stores=DMA((4,)),
        ready=pltpu.SemaphoreType.REGULAR,
        gather_sent=gather_sems,
        gather_arrived=gather_sems,
        scatter_sent=scatter_sems,
        scatter_arrived=scatter_sems,
        ring_sent=ring_sems,
        ring_arrived=ring_sems,
        ring_kept=DMA((2, 2 * members)),
        sum_sent=sum_sems,
        sum_arrived=sum_sems,
        sum_stored=DMA((4,)),
    )
    sum_buffers = [pltpu.VMEM(shape, HALF) for shape in cut]

    def kernel(*refs):
        count = len(args) + len(outs)
        named = dict(zip([*args, *outs], refs[:count]))
        results, rest = refs[count : count + len(cut)], refs[count + len(cut) :]
        named |= dict(zip(scratch, rest))
        rest = rest[len(scratch) :]
        ref = SimpleNamespace(**named, sum_results=results, sum_data=rest[: len(cut)], sum_landed=rest[len(cut) :])
        ref.grad_query = ref.grad_both.at[:, pl.ds(0, heads)]
        ref.grad_value = ref.grad_both.at[:, pl.ds(heads, heads)]
        layer(members, ref)

    found = pl.pallas_call(
        kernel,
        out_shape=out_shape,
        in_specs=in_specs,
        out_specs=out_specs,
        scratch_shapes=[*scratch.values(), *sum_buffers, *sum_buffers],
        compiler_params=pltpu.CompilerParams(collective_id=0, has_side_effects=True, vmem_limit_bytes=VMEM_LIMIT),
        name=layer.__name__,
    )(*args.values())
    sums = [result.reshape(shape) for result, shape in zip(found[len(outs) :], weights)]
    return SimpleNamespace(**dict(zip(outs, found))), sums


def finish(*refs):
    up, down, out, both, small, *rows = refs[:9]
    grad_up, grad_down, grad_out, grad_query, grad_value, *rest = refs[9:]
    heads = grad_query.shape[1]
    grad_up[...] = up[...].astype(FLOAT)
    grad_down[...] = down[...].astype(FLOAT)
    grad_out[...] = out[...].astype(FLOAT)
    grad_query[...] = both[:, :heads].astype(FLOAT)
    grad_value[...] = both[:, heads:].astype(FLOAT)
    for source, target in zip(rows, rest):
        target[...] = source[...]
    for source, target in zip((0, 1, 2, 3, 5, 6), rest[len(rows) :]):
        target[...] = small[source : source + 1, :]
    counts = rest[-1]
    for index in range(counts.shape[0]):
        counts[index : index + 1, :] = small[4:5, index * LANES : index * LANES + counts.shape[1]].astype(jnp.int32)


def run_finish(grads, small, rows, rounds):
    up, down, out, both = grads
    parts = 8
    vector = jax.ShapeDtypeStruct((1, small.shape[1]), FLOAT)
    taken = [up, down, out, both, small, *rows]
    given = [
        jax.ShapeDtypeStruct(up.shape, FLOAT),
        jax.ShapeDtypeStruct(down.shape, FLOAT),
        jax.ShapeDtypeStruct(out.shape, FLOAT),
        jax.ShapeDtypeStruct((both.shape[0], both.shape[1] // 2), FLOAT),
        jax.ShapeDtypeStruct((both.shape[0], both.shape[1] // 2), FLOAT),
        *[jax.ShapeDtypeStruct(r.shape, r.dtype) for r in rows],
        *[vector] * 6,
        jax.ShapeDtypeStruct((rounds, NB), jnp.int32),
    ]

    def spec(array):
        if array.shape[0] < LANES:
            return pl.BlockSpec(array.shape, lambda i: (0, 0))
        return pl.BlockSpec((array.shape[0] // parts, array.shape[1]), lambda i: (i, 0))

    return pl.pallas_call(
        finish,
        grid=(parts,),
        out_shape=given,
        in_specs=[spec(a) for a in taken],
        out_specs=[spec(a) for a in given],
        compiler_params=pltpu.CompilerParams(vmem_limit_bytes=VMEM_LIMIT),
        name=finish.__name__,
    )(*taken)


def per_device(
    stream_one,
    stream_two,
    attention_gain,
    attention_shift,
    query_proj,
    value_proj,
    output_proj,
    forward_gain,
    forward_shift,
    up_proj,
    up_bias,
    down_proj,
    down_bias,
    bucket_ids,
    sort_orders,
    doc_lengths,
    cotan_one,
    cotan_two,
):
    members = lax.axis_size("wide")
    row = lambda vector: vector.reshape(1, -1)
    found, grads = run_layer(
        members,
        SimpleNamespace(
            stream_one_any=stream_one,
            stream_two=stream_two,
            gain_one=row(attention_gain),
            shift_one=row(attention_shift),
            wq_any=query_proj,
            wv_any=value_proj,
            wo_any=output_proj,
            gain_two=row(forward_gain),
            shift_two=row(forward_shift),
            up_any=up_proj,
            up_bias=row(up_bias),
            down_any=down_proj,
            down_bias=row(down_bias),
            buckets=bucket_ids.T,
            orders=sort_orders[0],
            docs=doc_lengths[0],
            cotan_one_any=cotan_one,
            cotan_two_any=cotan_two,
        ),
    )
    rows = [found.out_one, found.out_two, found.grad_one, found.grad_two]
    grad_up, grad_down, grad_out, grad_query, grad_value, *rest = run_finish(
        grads, found.small, rows, sort_orders.shape[1]
    )
    gain_one, shift_one, gain_two, shift_two, bias_up, bias_down = [vector.reshape(-1) for vector in rest[4:10]]
    return (
        *rest[:4],
        gain_one,
        shift_one,
        grad_query,
        grad_value,
        grad_out,
        gain_two,
        shift_two,
        grad_up,
        bias_up,
        grad_down,
        bias_down,
        rest[10],
    )


def solution(mesh):
    rows = P(("wide", "narrow"), None)
    columns = P(None, "narrow")
    return jax.shard_map(
        per_device,
        mesh=mesh,
        in_specs=(
            rows,
            rows,
            P(),
            P(),
            columns,
            columns,
            P("narrow", None),
            P(),
            P(),
            columns,
            P("narrow"),
            P("narrow", None),
            P(),
            rows,
            P("wide", None, None),
            P("wide", None),
            rows,
            rows,
        ),
        out_specs=(
            rows,
            rows,
            rows,
            rows,
            P(),
            P(),
            columns,
            columns,
            P("narrow", None),
            P(),
            P(),
            columns,
            P("narrow"),
            P("narrow", None),
            P(),
            P(),
        ),
        check_vma=False,
    )
```

```python
import math
from types import SimpleNamespace

import jax
import jax.numpy as jnp
from jax import lax
from jax.experimental import pallas as pl
from jax.experimental.pallas import tpu as pltpu
from jax.sharding import PartitionSpec as P

HD = 128
GROUP = 64
NB = 24
MOST = 768
BLOCK = 256
LANES = 128
CHUNK = 128
NARROW = 4
VMEM_LIMIT = 60 << 20

FLOAT = jnp.float32
HALF = jnp.bfloat16
NEG = -1e30
EXP_SCALE = math.log2(math.e) / math.sqrt(HD)
FACTOR = 1.0 / math.sqrt(HD)
MESH = pl.DeviceIdType.MESH
IN_VMEM = pl.BlockSpec(memory_space=pltpu.VMEM)
IN_SMEM = pl.BlockSpec(memory_space=pltpu.SMEM)
ANYWHERE = pl.BlockSpec(memory_space=pl.ANY)
DMA = pltpu.SemaphoreType.DMA
WIDE = "wide"
DOCS = "docs"
FROM_HBM = "_any"


def normalize(inputs):
    center = inputs - jnp.mean(inputs, axis=-1, keepdims=True)
    inverse = lax.rsqrt(jnp.mean(center * center, axis=-1, keepdims=True) + 1e-05)
    return (center * inverse, inverse)


def norm_back(grad_out, scaled, inverse, gain):
    spread = grad_out * gain
    return inverse * (
        spread
        - jnp.mean(spread, axis=-1, keepdims=True)
        - scaled * jnp.mean(spread * scaled, axis=-1, keepdims=True)
    )


def contract_rows(left, right):
    return lax.dot_general(left, right, (((0,), (0,)), ((), ())), preferred_element_type=FLOAT)


def times_transpose(left, right):
    return lax.dot_general(left, right, (((1,), (1,)), ((), ())), preferred_element_type=FLOAT)


def times(left, right):
    return jnp.dot(left, right, preferred_element_type=FLOAT)


def column_sums(rows):
    return times(jnp.ones((8, rows.shape[0]), rows.dtype), rows)[0:1]


class Place:
    def __init__(self):
        index = lax.axis_index("narrow")
        core, chip = lax.rem(index, 2), lax.div(index, 2)
        self.me = index
        self.near = 2 * chip + 1 - core
        self.far = 2 * (1 - chip) + core
        self.cross = 2 * (1 - chip) + 1 - core


def span(start, size):
    return pl.ds(pl.multiple_of(start, size), size)


def remote(source, target, sent, arrived, other):
    return pltpu.make_async_remote_copy(
        src_ref=source,
        dst_ref=target,
        send_sem=sent,
        recv_sem=arrived,
        device_id={"narrow": other},
        device_id_type=MESH,
    )


class Gather:
    def __init__(self, place, whole, rows, sems):
        self.place, self.whole, self.rows = place, whole, rows
        self.sent, self.arrived = sems
        self.chunks = rows // CHUNK

    def at(self, owner, chunk):
        return self.whole.at[span(owner * self.rows + chunk * CHUNK, CHUNK), :]

    def copy(self, lane, owner, chunk, other):
        index = lane * self.chunks + chunk
        piece = self.at(owner, chunk)
        return remote(piece, piece, self.sent.at[index], self.arrived.at[index], other)

    def to_far(self, chunk):
        return self.copy(0, self.place.me, chunk, self.place.far)

    def to_near(self, chunk):
        return self.copy(1, self.place.me, chunk, self.place.near)

    def onward(self, chunk):
        return self.copy(2, self.place.far, chunk, self.place.near)

    def send(self, chunk):
        self.to_far(chunk).start()
        self.to_near(chunk).start()

    def take_near(self, chunk):
        self.to_near(chunk).wait_recv()

    def take_far(self, chunk):
        self.to_far(chunk).wait_recv()
        self.onward(chunk).start()

    def take_cross(self, chunk):
        self.onward(chunk).wait_recv()

    def finish(self):
        @pl.loop(0, self.chunks)
        def _(chunk):
            self.to_far(chunk).wait_send()
            self.to_near(chunk).wait_send()
            self.onward(chunk).wait_send()


class Scatter:
    def __init__(self, place, term, rows, buffers, sems):
        self.place, self.term, self.rows = place, term, rows
        self.near_out, self.near_in, self.far_out, self.far_in = buffers
        self.sent, self.arrived = sems
        self.chunks = rows // CHUNK

    def to_near(self, part, chunk):
        index = part * self.chunks + chunk
        at = span(chunk * CHUNK, CHUNK)
        return remote(
            self.near_out.at[part, at, :],
            self.near_in.at[part, at, :],
            self.sent.at[index],
            self.arrived.at[index],
            self.place.near,
        )

    def to_far(self, chunk):
        index = 2 * self.chunks + chunk
        at = span(chunk * CHUNK, CHUNK)
        return remote(
            self.far_out.at[at, :], self.far_in.at[at, :], self.sent.at[index], self.arrived.at[index], self.place.far
        )

    def part(self, owner, chunk):
        return self.term(span(owner * self.rows + chunk * CHUNK, CHUNK))

    def start(self, between=lambda: None):
        @pl.loop(0, self.chunks)
        def _(chunk):
            self.near_out[0, span(chunk * CHUNK, CHUNK), :] = self.part(self.place.cross, chunk).astype(HALF)
            self.to_near(0, chunk).start()

        between()

        @pl.loop(0, self.chunks)
        def _(chunk):
            at = span(chunk * CHUNK, CHUNK)
            own = self.part(self.place.far, chunk)
            self.to_near(0, chunk).wait_recv()
            self.far_out[at, :] = (own + self.near_in[0, at, :].astype(FLOAT)).astype(HALF)
            self.to_far(chunk).start()

        between()

        @pl.loop(0, self.chunks)
        def _(chunk):
            self.near_out[1, span(chunk * CHUNK, CHUNK), :] = self.part(self.place.near, chunk).astype(HALF)
            self.to_near(1, chunk).start()

    def chip_sum(self, chunk):
        own = self.part(self.place.me, chunk)
        self.to_near(1, chunk).wait_recv()
        return own + self.near_in[1, span(chunk * CHUNK, CHUNK), :].astype(FLOAT)

    def take_far(self, chunk):
        self.to_far(chunk).wait_recv()
        return self.far_in[span(chunk * CHUNK, CHUNK), :].astype(FLOAT)

    def finish(self):
        @pl.loop(0, self.chunks)
        def _(chunk):
            self.to_near(0, chunk).wait_send()
            self.to_near(1, chunk).wait_send()
            self.to_far(chunk).wait_send()


def pair_features(orders, docs, query_features, key_features, found):
    rounds, length = orders.shape
    groups = length // GROUP
    high_count = length // LANES
    high_rows = -(-high_count // 8) * 8
    count = docs.shape[0]
    depth = query_features.shape[0]
    lane = lax.broadcasted_iota(jnp.int32, (LANES, length), 1)
    low_at = lax.broadcasted_iota(jnp.int32, (LANES, length), 0)
    high_at = lax.broadcasted_iota(jnp.int32, (high_rows, length), 0)
    group_at = lax.broadcasted_iota(jnp.int32, (groups, LANES), 0).astype(FLOAT)
    sorted_group = lax.shift_right_logical(lane, int(math.log2(GROUP))).astype(FLOAT)

    @pl.loop(0, rounds)
    def _(index):
        row = orders[pl.ds(index, 1), :]
        high = jnp.where(high_at == lax.shift_right_logical(row, int(math.log2(LANES))), 1.0, 0.0)
        low = jnp.where(low_at == (row & (LANES - 1)), sorted_group, 0.0)
        found[index, :high_rows, :LANES] = times_transpose(high.astype(HALF), low.astype(HALF))
    place = lax.broadcasted_iota(jnp.int32, (count, LANES), 1)
    which = lax.broadcasted_iota(jnp.int32, (count, LANES), 0)
    begins = jnp.zeros((count, LANES), jnp.int32)
    ends = jnp.zeros((count, LANES), jnp.int32)
    begin = jnp.int32(0)
    for doc in range(count):
        end = begin + docs[doc]
        begins = jnp.where(which == doc, begin, begins)
        ends = jnp.where(which == doc, end, ends)
        begin = end
    rest = jnp.zeros((depth - rounds * groups - count, LANES), FLOAT)
    for block in range(high_count):
        mine, window = [], []
        for index in range(rounds):
            own = found[index, block : block + 1, :LANES]
            after = jnp.where(own == groups - 1.0, 0.0, own + 1.0)
            here = group_at == own
            mine.append(jnp.where(here, 1.0, 0.0))
            window.append(jnp.where(here | (group_at == after), 1.0, 0.0))
        at = place + block * LANES
        same = jnp.where((at >= begins) & (at < ends), 1.0, 0.0)
        lanes = slice(block * LANES, (block + 1) * LANES)
        query_features[:, lanes] = jnp.concatenate([*mine, same * (2.0 * rounds), rest], axis=0).astype(HALF)
        key_features[:, lanes] = jnp.concatenate([*window, same, rest], axis=0).astype(HALF)


def in_turn(place, step):
    flip_core, flip_chip = lax.rem(step, 2), lax.div(step, 2)
    core, chip = lax.rem(place.me, 2), lax.div(place.me, 2)
    core = core + flip_core * (1 - 2 * core)
    chip = chip + flip_chip * (1 - 2 * chip)
    return 2 * chip + core


def by_arrival(gather, act, after=None):
    place, rows = gather.place, gather.rows
    act(span(place.me * rows, rows))

    @pl.loop(0, gather.chunks)
    def _(chunk):
        gather.take_near(chunk)

    act(span(place.near * rows, rows))
    by_chunk(gather, act, after)


def by_chunk(gather, act, after=None):
    place, rows = gather.place, gather.rows

    @pl.loop(0, gather.chunks)
    def _(chunk):
        gather.take_far(chunk)
        if after is not None:
            pl.when(chunk == gather.chunks - 1)(after)
        act(span(place.far * rows + chunk * CHUNK, CHUNK))
        gather.take_cross(chunk)
        act(span(place.cross * rows + chunk * CHUNK, CHUNK))


def pair_bias(query_features, key_features, rounds, diagonal):
    counts = jnp.maximum(contract_rows(key_features, query_features) - 2.0 * rounds, 0.0)
    bias = jnp.where(counts > 0.0, jnp.log2(counts), NEG)
    if diagonal:
        key_at = lax.broadcasted_iota(jnp.int32, bias.shape, 0)
        query_at = lax.broadcasted_iota(jnp.int32, bias.shape, 1)
        bias = jnp.where(key_at < query_at, bias, NEG)
    return bias


def band_steps(length):
    return min(-(-(MOST - 1) // BLOCK), length // BLOCK - 1) + 1


def block_biases(block, steps, features, rounds, bias):
    query_features, key_features = features
    at = span(block * BLOCK, BLOCK)
    for step in range(steps):
        bias[step] = pair_bias(
            query_features[:, at], key_features[:, span((block - step) * BLOCK, BLOCK)], rounds, step == 0
        )


def attend(block, steps, rounds, queries, keys, values, features, merged, logs, bias, scores):
    at = span(block * BLOCK, BLOCK)
    heads = queries.shape[1] // HD
    block_biases(block, steps, features, rounds, bias)
    for head in range(heads):
        part = slice(head * HD, (head + 1) * HD)
        query = queries[at, part]
        peak = jnp.full((1, BLOCK), 2 * NEG, FLOAT)
        for step in range(steps):
            key_at = span((block - step) * BLOCK, BLOCK)
            score = times_transpose(keys[key_at, part], query) * EXP_SCALE + bias[step]
            scores[span((head * steps + step) * BLOCK, BLOCK), :] = score
            peak = jnp.maximum(peak, jnp.max(score, axis=0, keepdims=True))
        alone = peak < 0.5 * NEG
        peak = jnp.where(alone, 0.0, peak)
        total = jnp.zeros((1, BLOCK), FLOAT)
        mixed = jnp.zeros((HD, BLOCK), FLOAT)
        for step in range(steps):
            key_at = span((block - step) * BLOCK, BLOCK)
            powers = jnp.exp2(scores[span((head * steps + step) * BLOCK, BLOCK), :] - peak)
            total = total + jnp.sum(powers, axis=0, keepdims=True)
            mixed = mixed + contract_rows(values[key_at, part], powers.astype(HALF))
        total = jnp.where(alone, 1.0, total)
        mixed = jnp.where(alone, values[at, part].astype(FLOAT).T, mixed / total)
        merged[at, part] = mixed.T.astype(HALF)
        logs[head : head + 1, at] = jnp.where(alone, -NEG, peak + jnp.log2(total))


def attend_back(block, steps, rounds, queries, keys, values, features, grads, merged, logs, dq, dk, dv, bias, after):
    at = span(block * BLOCK, BLOCK)
    heads = queries.shape[1] // HD
    block_biases(block, steps, features, rounds, bias)
    ones = jnp.ones((8, HD), HALF)
    for head in range(heads):
        part = slice(head * HD, (head + 1) * HD)
        query, grad = queries[at, part], grads[at, part]
        log_sum = logs[head : head + 1, at]
        product = grad.astype(FLOAT) * merged[at, part].astype(FLOAT)
        coarse = product.astype(HALF)
        fine = (product - coarse.astype(FLOAT)).astype(HALF)
        along = (times_transpose(ones, coarse) + times_transpose(ones, fine))[0:1]
        grad_query = jnp.zeros((HD, BLOCK), FLOAT)
        for step in range(steps):
            key_at = span((block - step) * BLOCK, BLOCK)
            key = keys[key_at, part]
            weights = jnp.exp2(times_transpose(key, query) * EXP_SCALE + bias[step] - log_sum)
            grad_probs = times_transpose(values[key_at, part], grad)
            grad_scores = (weights * (grad_probs - along)).astype(HALF)
            grad_value = times(weights.astype(HALF), grad)
            grad_key = times(grad_scores, query)
            if step == 0:
                dv[key_at, part] = grad_value
                dk[key_at, part] = grad_key
            else:
                dv[key_at, part] += grad_value
                dk[key_at, part] += grad_key
            grad_query = grad_query + contract_rows(key, grad_scores)
        dq[at, part] = grad_query.T
        after(head)


def finish_attention(queries, grads, logs, dq, dk, dv, grad_query, grad_value):
    length, width = queries.shape

    @pl.loop(0, length // BLOCK)
    def _(block):
        at = span(block * BLOCK, BLOCK)
        alone = jnp.where(logs[:, at] == -NEG, 1.0, 0.0).T
        for head in range(width // HD):
            part = slice(head * HD, (head + 1) * HD)
            grad_value[at, part] = (dv[at, part] + alone[:, head : head + 1] * grads[at, part].astype(FLOAT)).astype(HALF)
            query = queries[at, part].astype(FLOAT)
            key_scale = lax.rsqrt(jnp.sum(query * query, axis=-1, keepdims=True) + 1e-06)
            unit = query * key_scale
            grad_key = dk[at, part] * FACTOR
            key_along = jnp.sum(grad_key * unit, axis=-1, keepdims=True)
            grad_query[at, part] = (dq[at, part] * FACTOR + key_scale * (grad_key - unit * key_along)).astype(HALF)


def gelu_and_slope(hidden):
    square = hidden * hidden
    bend = jnp.tanh(math.sqrt(2.0 / math.pi) * hidden * (1.0 + 0.044715 * square))
    half_more = 0.5 + 0.5 * bend
    slope = half_more + 0.5 * hidden * (1.0 - bend * bend) * (
        math.sqrt(2.0 / math.pi) * (1.0 + 3.0 * 0.044715 * square)
    )
    return hidden * half_more, slope


def weight_grad(result, left, right, rows=None, add=False):
    width = 256
    height = result.shape[1] * result.shape[2] // right.shape[1]
    pieces = width // height
    rows = slice(None) if rows is None else rows

    @pl.loop(0, left.shape[1] // width)
    def _(index):
        block = contract_rows(left[rows, span(index * width, width)], right[rows, :])
        at = pl.ds(index * pieces, pieces)
        block = block.reshape(pieces, *result.shape[1:])
        if add:
            block = block + result[at].astype(FLOAT)
        result[at] = block.astype(result.dtype)


def ring_place(members, index):
    column, row = lax.rem(index, 2), lax.div(index, 2)
    return row + column * (members - 1 - 2 * row)


def ring_member(members, place):
    back = lax.div(place, members // 2)
    return 2 * place + back * (2 * (members - 1 - place) + 1 - 2 * place)


class Ring:
    def __init__(self, members, data, landed, result, sent, arrived, kept):
        self.members, self.data, self.landed, self.result = members, data, landed, result
        self.sent, self.arrived, self.kept, self.stage = sent, arrived, kept, 0
        self.here = ring_place(members, lax.axis_index("wide"))
        self.neighbours = (
            ring_member(members, lax.rem(self.here + 1, members)),
            ring_member(members, lax.rem(self.here + members - 1, members)),
        )

    def piece(self, direction, step):
        if direction == 0:
            return 2 * lax.rem(self.here - step + 2 * self.members, self.members)
        return 2 * lax.rem(self.here + step, self.members) + 1

    def copy(self, direction, step, at, gathering, fresh):
        index = direction * 2 * (self.members - 1) + step
        source = self.landed if gathering and not fresh else self.data
        return pltpu.make_async_remote_copy(
            src_ref=source.at[at],
            dst_ref=self.landed.at[at],
            send_sem=self.sent.at[index],
            recv_sem=self.arrived.at[index],
            device_id={"wide": self.neighbours[direction]},
            device_id_type=MESH,
        )

    def outgoing(self, direction, step, gathering=False, fresh=False):
        return self.copy(direction, step, self.piece(direction, step), gathering, fresh)

    def incoming(self, direction, step, gathering=False):
        return self.copy(direction, step, self.piece(direction, step + 1), gathering, False)

    def begin(self):
        for direction in range(2):
            self.outgoing(direction, 0).start()

    def add(self, direction, step):
        self.incoming(direction, step).wait_recv()
        at = self.piece(direction, step + 1)
        self.data[at] = (self.data[at].astype(FLOAT) + self.landed[at].astype(FLOAT)).astype(HALF)
        return at

    def keep(self, direction, step):
        at = self.piece(direction, step)
        source = self.data if isinstance(step, int) and step == self.members - 1 else self.landed
        return pltpu.make_async_copy(
            source.at[at], self.result.at[at], self.kept.at[direction * self.members + step - (self.members - 1)]
        )

    def advance(self):
        stage, last = self.stage, self.members - 1
        if stage == 14:
            return
        self.stage = stage + 1
        low, high = stage * 2 * last // 14, (stage + 1) * 2 * last // 14

        def repeat(begin, end, act):
            if end == begin + 1:
                act(begin)
            elif end > begin:
                pl.loop(begin, end)(act)

        def reduce(step):
            for direction in range(2):
                self.add(direction, step)
                self.outgoing(direction, step + 1).start()

        def forward(step):
            for direction in range(2):
                self.incoming(direction, step, True).wait_recv()
                self.outgoing(direction, step + 1, True).start()
                self.keep(direction, step + 1).start()

        repeat(low, min(high, last - 1), reduce)
        if low <= last - 1 < high:
            for direction in range(2):
                self.add(direction, last - 1)
                self.outgoing(direction, last, True, True).start()
                self.keep(direction, last).start()
        repeat(max(low, last), min(high, 2 * last - 1), forward)
        if low <= 2 * last - 1 < high:
            for direction in range(2):
                self.incoming(direction, 2 * last - 1, True).wait_recv()
                self.keep(direction, 2 * last).start()

    def finish(self):
        last = self.members - 1
        for direction in range(2):
            self.keep(direction, last).wait()
            self.outgoing(direction, last, True, True).wait_send()

        @pl.loop(0, last)
        def _(step):
            for direction in range(2):
                self.outgoing(direction, step).wait_send()

        @pl.loop(last + 1, 2 * last)
        def _(step):
            for direction in range(2):
                self.outgoing(direction, step, True).wait_send()
                self.keep(direction, step).wait()

        for direction in range(2):
            self.keep(direction, 2 * last).wait()


class Exchange:
    def __init__(self, members, data, landed, result, first, unit, bits, sems, stored):
        self.members, self.data, self.landed, self.result = members, data, landed, result
        self.first, self.unit, self.bits = first, unit, bits
        self.sent, self.arrived, self.stored, self.stage = *sems, stored, 0
        self.wide = lax.axis_index("wide")

    def bit(self, step):
        return lax.rem(lax.div(self.wide, 1 << self.bits[step]), 2)

    def size(self, step):
        return self.unit * (self.members >> (step + 1))

    def part(self, step, kept):
        start = self.first
        for before in range(step):
            start = start + self.bit(before) * self.size(before)
        bit = self.bit(step)
        return pl.ds(start + (bit if kept else 1 - bit) * self.size(step), self.size(step))

    def landing(self, step):
        return pl.ds(self.first + self.unit * self.members - 2 * self.size(step), self.size(step))

    def copy(self, step, gathering):
        index = step + gathering * len(self.bits)
        at = self.part(step, gathering)
        source = self.result if gathering and step < len(self.bits) - 1 else self.data
        return pltpu.make_async_remote_copy(
            src_ref=source.at[at],
            dst_ref=self.result.at[at] if gathering else self.landed.at[self.landing(step)],
            send_sem=self.sent.at[index],
            recv_sem=self.arrived.at[index],
            device_id={"wide": self.wide + (1 - 2 * self.bit(step)) * (1 << self.bits[step])},
            device_id_type=MESH,
        )

    def begin(self):
        self.copy(0, False).start()

    def advance(self):
        count, stage = len(self.bits), self.stage
        if stage == 2 * count:
            return
        self.stage = stage + 1
        if stage < count:
            self.copy(stage, False).wait_recv()
            kept, landed = self.part(stage, True), self.landing(stage)

            @pl.loop(0, self.size(stage))
            def _(index):
                at = kept.start + index
                self.data[at] = (
                    self.data[at].astype(FLOAT) + self.landed[landed.start + index].astype(FLOAT)
                ).astype(HALF)

        else:
            self.copy(2 * count - 1 - stage, True).wait_recv()
        if stage < count - 1:
            self.copy(stage + 1, False).start()
            return
        if stage == count - 1:
            self.store().start()
        if stage == count:
            self.store().wait()
        if stage < 2 * count - 1:
            self.copy(2 * count - 2 - stage, True).start()

    def store(self):
        at = self.part(len(self.bits) - 1, True)
        return pltpu.make_async_copy(self.data.at[at], self.result.at[at], self.stored)

    def finish(self):
        for step in range(len(self.bits)):
            self.copy(step, False).wait_send()
            self.copy(step, True).wait_send()


class Everyone:
    def __init__(self, axis, slots, sent, arrived):
        self.axis, self.slots, self.sent, self.arrived = axis, slots, sent, arrived
        self.me, self.members = lax.axis_index(axis), slots.shape[0]

    def copy(self, step):
        mine = self.slots.at[self.me]
        return pltpu.make_async_remote_copy(
            src_ref=mine,
            dst_ref=mine,
            send_sem=self.sent.at[step],
            recv_sem=self.arrived.at[step],
            device_id={self.axis: lax.rem(self.me + step, self.members)},
            device_id_type=MESH,
        )

    def send(self, value):
        self.slots[self.me] = value

        @pl.loop(1, self.members)
        def _(step):
            self.copy(step).start()

    def total(self):
        @pl.loop(1, self.members)
        def _(step):
            self.copy(step).wait()

        return lax.fori_loop(1, self.members, lambda index, total: total + self.slots[index], self.slots[0])


def advance(*exchanges):
    for exchange in exchanges:
        exchange.advance()


def meet_all(members):
    barrier = pltpu.get_barrier_semaphore()
    narrow, wide = lax.axis_index("narrow"), lax.axis_index("wide")

    @pl.loop(1, NARROW)
    def _(step):
        pl.semaphore_signal(
            barrier, inc=1, device_id={"narrow": lax.rem(narrow + step, NARROW)}, device_id_type=MESH
        )

    @pl.loop(1, members)
    def _(step):
        pl.semaphore_signal(barrier, inc=1, device_id={"wide": lax.rem(wide + step, members)}, device_id_type=MESH)

    pl.semaphore_wait(barrier, NARROW - 1 + members - 1)


def layer(members, ref):
    place = Place()
    second_rows = ref.stream_two
    rows, width = second_rows.shape
    orders, docs = ref.orders, ref.docs
    rounds, length = orders.shape
    heads = ref.wq.shape[1]
    chunks = rows // CHUNK
    whole_one, whole_two, cotans, grad_rows = (ref.whole_one, ref.whole_two, ref.cotans, ref.grad_rows)
    queries, keys, values, merged, logs = (ref.queries, ref.keys, ref.values, ref.merged, ref.logs)
    features = (ref.query_features, ref.key_features)
    wq, wv, wo, up, down = (ref.wq, ref.wv, ref.wo, ref.up, ref.down)
    active, grad_hidden, middle, first_rows = (ref.active, ref.grad_hidden, ref.middle, ref.first_rows)
    grad_merged, bias, sums = ref.grad_merged, ref.bias, ref.sums
    dq, dk, dv = (ref.totals.at[pl.ds(i * length, length), :] for i in range(3))
    own_at, far_at = span(place.me * rows, rows), span(place.far * rows, rows)
    loads, stores = ref.loads, ref.stores

    def load(index, source, target):
        copy = pltpu.make_async_copy(source, target, loads.at[index])
        copy.start()
        return copy

    load_wq, load_wv = load(0, ref.wq_any, wq), load(1, ref.wv_any, wv)
    load_cotan = load(2, ref.cotan_two_any, cotans.at[own_at, :])
    load_wo, load_first = load(3, ref.wo_any, wo), load(4, ref.stream_one_any, first_rows)
    load_down, load_up = load(5, ref.down_any, down), load(6, ref.up_any, up)
    meet_all(members)

    up_ring, down_ring = rings = [
        Ring(
            members, ref.sum_data[i], ref.sum_landed[i], ref.sum_results[i], ref.ring_sent.at[i], ref.ring_arrived.at[i],
            ref.ring_kept.at[i],
        )
        for i in range(2)
    ]
    bits = list(range(members.bit_length() - 1))
    swapped = bits[1::-1] + bits[2:]
    lanes = ((2, 0, bits), (2, members, swapped), (3, 0, bits), (3, members, swapped))
    out_sum, out_swap, in_sum, in_swap = exchanges = [
        Exchange(
            members, ref.sum_data[array], ref.sum_landed[array], ref.sum_results[array], first, 1, order,
            (ref.sum_sent.at[lane], ref.sum_arrived.at[lane]), ref.sum_stored.at[lane],
        )
        for lane, (array, first, order) in enumerate(lanes)
    ]
    queue = [up_ring, down_ring]

    def serve(*more):
        ring = queue.pop(0)
        queue.append(ring)
        advance(ring, *more)

    gather = Gather(place, whole_one, rows, (ref.gather_sent.at[0], ref.gather_arrived.at[0]))

    @pl.loop(0, chunks)
    def _(chunk):
        scaled, _ = normalize(second_rows[span(chunk * CHUNK, CHUNK), :].astype(FLOAT))
        normed = (scaled * ref.gain_one[...] + ref.shift_one[...]).astype(HALF)
        whole_one[span(place.me * rows + chunk * CHUNK, CHUNK), :] = normed
        gather.send(chunk)

    pair_features(orders, docs, *features, bias)
    level = lax.broadcasted_iota(jnp.int32, (LANES, rows), 0)
    counted = jnp.ones((8, rows), HALF)
    sums[...] = jnp.zeros_like(sums)
    for index in range(rounds):
        found = jnp.where(level == ref.buckets[index : index + 1, :], 1.0, 0.0).astype(HALF)
        sums[4:5, index * LANES : (index + 1) * LANES] = times_transpose(counted, found)[0:1]
    load_wq.wait()
    load_wv.wait()

    def project(at):
        query = times(whole_one[at, :], wq[...]).astype(HALF)
        queries[at, :] = query
        for head in range(heads // HD):
            part = query[:, head * HD : (head + 1) * HD].astype(FLOAT)
            scale = lax.rsqrt(jnp.sum(part * part, axis=-1, keepdims=True) + 1e-06)
            keys[at, head * HD : (head + 1) * HD] = (part * scale).astype(HALF)
        values[at, :] = times(whole_one[at, :], wv[...]).astype(HALF)

    load_cotan.wait()
    spread = Gather(place, cotans, rows, (ref.gather_sent.at[1], ref.gather_arrived.at[1]))

    def send_cotangents():
        @pl.loop(0, chunks)
        def _(chunk):
            spread.send(chunk)

    by_arrival(gather, project, send_cotangents)
    gather.finish()

    steps = band_steps(length)
    blocks = length // BLOCK

    def forward(block, count):
        attend(block, count, rounds, queries, keys, values, features, merged, logs, bias, ref.totals)

    for block in range(steps - 1):
        forward(block, block + 1)

    @pl.loop(steps - 1, blocks)
    def _(block):
        forward(block, steps)

    buffers = (ref.near_out, ref.near_in, ref.far_out, ref.far_in)
    load_wo.wait()
    scatter = Scatter(
        place, lambda at: times(merged[at, :], wo[...]), rows, buffers, (ref.scatter_sent.at[0], ref.scatter_arrived.at[0])
    )
    scatter.start()
    load_first.wait()

    @pl.loop(0, chunks)
    def _(chunk):
        at = span(chunk * CHUNK, CHUNK)
        middle[at, :] = first_rows[at, :].astype(FLOAT) + scatter.chip_sum(chunk)

    @pl.loop(0, chunks)
    def _(chunk):
        spread.take_near(chunk)
        spread.take_far(chunk)

    load_down.wait()
    half_width = width // 2

    def grad_active(owner):
        @pl.loop(0, 2)
        def _(half):
            at = span(half * half_width, half_width)
            grad_hidden[span(owner * rows, rows), at] = times_transpose(
                cotans[span(owner * rows, rows), :], down[at, :]
            ).astype(HALF)

    @pl.loop(0, NARROW)
    def _(step):
        @pl.when(step == NARROW - 1)
        def _():
            @pl.loop(0, chunks)
            def _(chunk):
                spread.take_cross(chunk)

        grad_active(in_turn(place, step))

    gather = Gather(place, whole_two, rows, (ref.gather_sent.at[2], ref.gather_arrived.at[2]))
    load_up.wait()

    @pl.loop(0, chunks)
    def _(chunk):
        at = span(chunk * CHUNK, CHUNK)
        value = middle[at, :] + scatter.take_far(chunk)
        middle[at, :] = value
        first_rows[at, :] = value.astype(HALF)
        scaled, _ = normalize(value)
        whole_two[span(place.me * rows + chunk * CHUNK, CHUNK), :] = (
            scaled * ref.gain_two[...] + ref.shift_two[...]
        ).astype(HALF)
        gather.send(chunk)

    store_one = pltpu.make_async_copy(first_rows, ref.out_one, stores.at[0])
    store_one.start()

    def feed(row_at):
        @pl.loop(0, 2)
        def _(half):
            at = span(half * half_width, half_width)
            value, slope = gelu_and_slope(times(whole_two[row_at, :], up[:, at]) + ref.up_bias[:, at])
            active[row_at, at] = value.astype(HALF)
            grad_hidden[row_at, at] = (grad_hidden[row_at, at].astype(FLOAT) * slope).astype(HALF)

    chip = lax.div(place.me, 2)
    here, there = span(chip * 2 * rows, 2 * rows), span((1 - chip) * 2 * rows, 2 * rows)
    feed(span(place.me * rows, rows))

    @pl.loop(0, chunks)
    def _(chunk):
        gather.take_near(chunk)

    feed(span(place.near * rows, rows))
    weight_grad(ref.sum_data[1], active, cotans, here)
    weight_grad(ref.sum_data[0], whole_two, grad_hidden, here)
    by_chunk(gather, feed)
    scatter.finish()

    store_one.wait()
    load_cotan_one = load(7, ref.cotan_one_any, first_rows)
    scatter = Scatter(
        place,
        lambda at: times_transpose(grad_hidden[at, :], up[...]),
        rows,
        buffers,
        (ref.scatter_sent.at[1], ref.scatter_arrived.at[1]),
    )

    weight_grad(ref.sum_data[1], active, cotans, there, True)
    down_ring.begin()
    scatter.start()
    weight_grad(ref.sum_data[0], whole_two, grad_hidden, there, True)
    up_ring.begin()
    queue.reverse()
    back = Gather(place, grad_rows, rows, (ref.gather_sent.at[3], ref.gather_arrived.at[3]))
    load_cotan_one.wait()

    for chunk in range(chunks):
        at = span(chunk * CHUNK, CHUNK)
        grad_normed = scatter.chip_sum(chunk) + scatter.take_far(chunk)
        scaled, inverse = normalize(middle[at, :])
        grad = first_rows[at, :].astype(FLOAT) + norm_back(grad_normed, scaled, inverse, ref.gain_two[...])
        grad_rows[span(place.me * rows + chunk * CHUNK, CHUNK), :] = grad.astype(HALF)
        back.send(chunk)
        sums[2:3, :] += jnp.sum(grad_normed * scaled, axis=0, keepdims=True)
        sums[3:4, :] += jnp.sum(grad_normed, axis=0, keepdims=True)
        serve()
        serve()

    def merge_back(at):
        grad_merged[at, :] = times_transpose(grad_rows[at, :], wo[...]).astype(HALF)

    store_grad = pltpu.make_async_copy(grad_rows.at[own_at, :], ref.grad_one, stores.at[1])
    store_grad.start()
    own_sums = ref.wide_all.at[lax.axis_index(WIDE)]
    own_sums[5:6, :] = column_sums(grad_hidden[...])
    own_sums[6:7, :] = column_sums(cotans[...])
    scatter.finish()
    gather.finish()
    spread.finish()

    merge_back(span(place.me * rows, rows))
    serve()

    @pl.loop(0, chunks)
    def _(chunk):
        back.take_near(chunk)

    merge_back(span(place.near * rows, rows))
    serve()
    for chunk in range(chunks):
        back.take_far(chunk)
        merge_back(span(place.far * rows + chunk * CHUNK, CHUNK))
        back.take_cross(chunk)
        merge_back(span(place.cross * rows + chunk * CHUNK, CHUNK))
        serve()
    serve()
    weight_grad(ref.sum_data[2], merged, grad_rows)
    out_sum.begin()
    out_swap.begin()
    serve()

    fed = Scatter(
        place, lambda at: times(active[at, :], down[...]), rows, buffers, (ref.scatter_sent.at[2], ref.scatter_arrived.at[2])
    )
    fed.start()
    serve()

    def take_fed():
        @pl.loop(0, chunks)
        def _(chunk):
            at = span(chunk * CHUNK, CHUNK)
            total = fed.chip_sum(chunk) + fed.take_far(chunk) + ref.down_bias[...]
            cotans[span(place.near * rows + chunk * CHUNK, CHUNK), :] = (
                second_rows[at, :].astype(FLOAT) + total
            ).astype(HALF)

        store_two.start()
        fed.finish()
        for other in (place.near, place.far):
            pl.semaphore_signal(ref.ready, inc=1, device_id={"narrow": other}, device_id_type=MESH)

    store_two = pltpu.make_async_copy(cotans.at[span(place.near * rows, rows), :], ref.out_two, stores.at[2])

    for block in range(blocks):

        def after(head, block=block):
            if head == heads // HD - 1 or block > 2:
                serve(*([out_sum, out_swap] if block > 2 and head else []))

        attend_back(
            block, min(block + 1, steps), rounds, queries, keys, values, features, grad_merged, merged, logs, dq, dk, dv, bias, after
        )
        if block == blocks - 2:
            take_fed()

    grad_query, grad_value = ref.grad_query, ref.grad_value
    finish_attention(queries, grad_merged, logs, dq, dk, dv, grad_query, grad_value)
    serve()
    weight_grad(ref.sum_data[3], whole_one, ref.grad_both)
    in_sum.begin()
    in_swap.begin()
    pl.semaphore_wait(ref.ready, 2)

    scatter = Scatter(
        place,
        lambda at: times_transpose(grad_query[at, :], wq[...]) + times_transpose(grad_value[at, :], wv[...]),
        rows,
        buffers,
        (ref.scatter_sent.at[3], ref.scatter_arrived.at[3]),
    )
    scatter.start()
    serve(out_sum, out_swap)
    serve(in_swap, in_sum)

    for chunk in range(chunks):
        at = span(chunk * CHUNK, CHUNK)
        grad_normed = scatter.chip_sum(chunk) + scatter.take_far(chunk)
        scaled, inverse = normalize(second_rows[at, :].astype(FLOAT))
        mine = span(place.me * rows + chunk * CHUNK, CHUNK)
        cotans[mine, :] = (
            cotans[mine, :].astype(FLOAT) + norm_back(grad_normed, scaled, inverse, ref.gain_one[...])
        ).astype(HALF)
        sums[0:1, :] += jnp.sum(grad_normed * scaled, axis=0, keepdims=True)
        sums[1:2, :] += jnp.sum(grad_normed, axis=0, keepdims=True)
        serve(*exchanges)
        serve()

    store_last = pltpu.make_async_copy(cotans.at[own_at, :], ref.grad_two, stores.at[3])
    store_last.start()
    over_narrow = Everyone("narrow", ref.narrow_all, ref.narrow_sent, ref.narrow_arrived)
    over_wide = Everyone("wide", ref.wide_all, ref.wide_sent, ref.wide_arrived)
    over_narrow.send(sums[...])
    serve(*exchanges)
    sums[...] = over_narrow.total()
    sums[5:7, :] = own_sums[5:7, :]
    over_wide.send(sums[...])
    while min(exchange.stage for exchange in exchanges) < 2 * len(bits) or min(ring.stage for ring in rings) < 14:
        serve(*exchanges)
    ref.small[...] = over_wide.total()
    scatter.finish()
    back.finish()
    for copy in (store_grad, store_two, store_last):
        copy.wait()
    for exchange in [*exchanges, *rings]:
        exchange.finish()


def pieces(members, shape):
    columns = shape[1] if members <= 8 else LANES
    return (2 * members, shape[0] * shape[1] // (2 * members * columns), columns)


def run_layer(members, args):
    rows, width = args.stream_two.shape
    length, heads, hidden = NARROW * rows, args.wq_any.shape[1], args.up_any.shape[1]
    rounds = args.orders.shape[0]
    chunks = rows // CHUNK
    depth = -(-(rounds * (length // GROUP) + args.docs.shape[0]) // LANES) * LANES
    weights = [(width, hidden), (hidden, width), (heads, width), (width, 2 * heads)]
    cut = [pieces(members, shape) for shape in weights]
    args = vars(args)
    in_specs = [IN_SMEM if k == DOCS else ANYWHERE if k.endswith(FROM_HBM) else IN_VMEM for k in args]
    outs = dict(
        out_one=((rows, width), HALF),
        out_two=((rows, width), HALF),
        grad_one=((rows, width), HALF),
        grad_two=((rows, width), HALF),
        small=((8, width), FLOAT),
    )
    out_shape = [jax.ShapeDtypeStruct(*o) for o in outs.values()] + [jax.ShapeDtypeStruct(shape, HALF) for shape in cut]
    out_specs = [ANYWHERE] * 4 + [IN_VMEM] + [ANYWHERE] * len(cut)
    tall = pltpu.VMEM((length, width), HALF)
    slim = pltpu.VMEM((length, heads), HALF)
    gather_sems, scatter_sems = DMA((4, 3 * chunks)), DMA((4, 3 * chunks))
    sum_sems = DMA((4, 2 * (members.bit_length() - 1)))
    ring_sems = DMA((2, 4 * (members - 1)))
    scratch = dict(
        whole_one=tall,
        whole_two=tall,
        cotans=tall,
        grad_rows=tall,
        active=pltpu.VMEM((length, hidden), HALF),
        grad_hidden=pltpu.VMEM((length, hidden), HALF),
        queries=slim,
        keys=slim,
        values=slim,
        merged=slim,
        grad_merged=slim,
        grad_both=pltpu.VMEM((length, 2 * heads), HALF),
        logs=pltpu.VMEM((8, length), FLOAT),
        query_features=pltpu.VMEM((depth, length), HALF),
        key_features=pltpu.VMEM((depth, length), HALF),
        wq=pltpu.VMEM((width, heads), HALF),
        wv=pltpu.VMEM((width, heads), HALF),
        wo=pltpu.VMEM((heads, width), HALF),
        up=pltpu.VMEM((width, hidden), HALF),
        down=pltpu.VMEM((hidden, width), HALF),
        middle=pltpu.VMEM((rows, width), FLOAT),
        first_rows=pltpu.VMEM((rows, width), HALF),
        bias=pltpu.VMEM((max(rounds, band_steps(length)), BLOCK, BLOCK), FLOAT),
        totals=pltpu.VMEM((3 * length, heads), FLOAT),
        sums=pltpu.VMEM((8, width), FLOAT),
        near_out=pltpu.VMEM((2, rows, width), HALF),
        near_in=pltpu.VMEM((2, rows, width), HALF),
        far_out=pltpu.VMEM((rows, width), HALF),
        far_in=pltpu.VMEM((rows, width), HALF),
        narrow_all=pltpu.VMEM((NARROW, 8, width), FLOAT),
        wide_all=pltpu.VMEM((members, 8, width), FLOAT),
        narrow_sent=DMA((NARROW,)),
        narrow_arrived=DMA((NARROW,)),
        wide_sent=DMA((members,)),
        wide_arrived=DMA((members,)),
        loads=DMA((8,)),
        stores=DMA((4,)),
        ready=pltpu.SemaphoreType.REGULAR,
        gather_sent=gather_sems,
        gather_arrived=gather_sems,
        scatter_sent=scatter_sems,
        scatter_arrived=scatter_sems,
        ring_sent=ring_sems,
        ring_arrived=ring_sems,
        ring_kept=DMA((2, 2 * members)),
        sum_sent=sum_sems,
        sum_arrived=sum_sems,
        sum_stored=DMA((4,)),
    )
    sum_buffers = [pltpu.VMEM(shape, HALF) for shape in cut]

    def kernel(*refs):
        count = len(args) + len(outs)
        named = dict(zip([*args, *outs], refs[:count]))
        results, rest = refs[count : count + len(cut)], refs[count + len(cut) :]
        named |= dict(zip(scratch, rest))
        rest = rest[len(scratch) :]
        ref = SimpleNamespace(**named, sum_results=results, sum_data=rest[: len(cut)], sum_landed=rest[len(cut) :])
        ref.grad_query = ref.grad_both.at[:, pl.ds(0, heads)]
        ref.grad_value = ref.grad_both.at[:, pl.ds(heads, heads)]
        layer(members, ref)

    found = pl.pallas_call(
        kernel,
        out_shape=out_shape,
        in_specs=in_specs,
        out_specs=out_specs,
        scratch_shapes=[*scratch.values(), *sum_buffers, *sum_buffers],
        compiler_params=pltpu.CompilerParams(collective_id=0, has_side_effects=True, vmem_limit_bytes=VMEM_LIMIT),
        name=layer.__name__,
    )(*args.values())
    sums = [result.reshape(shape) for result, shape in zip(found[len(outs) :], weights)]
    return SimpleNamespace(**dict(zip(outs, found))), sums


def finish(*refs):
    up, down, out, both, small, *rows = refs[:9]
    grad_up, grad_down, grad_out, grad_query, grad_value, *rest = refs[9:]
    heads = grad_query.shape[1]
    grad_up[...] = up[...].astype(FLOAT)
    grad_down[...] = down[...].astype(FLOAT)
    grad_out[...] = out[...].astype(FLOAT)
    grad_query[...] = both[:, :heads].astype(FLOAT)
    grad_value[...] = both[:, heads:].astype(FLOAT)
    for source, target in zip(rows, rest):
        target[...] = source[...]
    for source, target in zip((0, 1, 2, 3, 5, 6), rest[len(rows) :]):
        target[...] = small[source : source + 1, :]
    counts = rest[-1]
    for index in range(counts.shape[0]):
        counts[index : index + 1, :] = small[4:5, index * LANES : index * LANES + counts.shape[1]].astype(jnp.int32)


def run_finish(grads, small, rows, rounds):
    up, down, out, both = grads
    parts = 4
    vector = jax.ShapeDtypeStruct((1, small.shape[1]), FLOAT)
    taken = [up, down, out, both, small, *rows]
    given = [
        jax.ShapeDtypeStruct(up.shape, FLOAT),
        jax.ShapeDtypeStruct(down.shape, FLOAT),
        jax.ShapeDtypeStruct(out.shape, FLOAT),
        jax.ShapeDtypeStruct((both.shape[0], both.shape[1] // 2), FLOAT),
        jax.ShapeDtypeStruct((both.shape[0], both.shape[1] // 2), FLOAT),
        *[jax.ShapeDtypeStruct(r.shape, r.dtype) for r in rows],
        *[vector] * 6,
        jax.ShapeDtypeStruct((rounds, NB), jnp.int32),
    ]

    def spec(array):
        if array.shape[0] < LANES:
            return pl.BlockSpec(array.shape, lambda i: (0, 0))
        return pl.BlockSpec((array.shape[0] // parts, array.shape[1]), lambda i: (i, 0))

    return pl.pallas_call(
        finish,
        grid=(parts,),
        out_shape=given,
        in_specs=[spec(a) for a in taken],
        out_specs=[spec(a) for a in given],
        compiler_params=pltpu.CompilerParams(vmem_limit_bytes=VMEM_LIMIT),
        name=finish.__name__,
    )(*taken)


def per_device(
    stream_one,
    stream_two,
    attention_gain,
    attention_shift,
    query_proj,
    value_proj,
    output_proj,
    forward_gain,
    forward_shift,
    up_proj,
    up_bias,
    down_proj,
    down_bias,
    bucket_ids,
    sort_orders,
    doc_lengths,
    cotan_one,
    cotan_two,
):
    members = lax.axis_size("wide")
    row = lambda vector: vector.reshape(1, -1)
    found, grads = run_layer(
        members,
        SimpleNamespace(
            stream_one_any=stream_one,
            stream_two=stream_two,
            gain_one=row(attention_gain),
            shift_one=row(attention_shift),
            wq_any=query_proj,
            wv_any=value_proj,
            wo_any=output_proj,
            gain_two=row(forward_gain),
            shift_two=row(forward_shift),
            up_any=up_proj,
            up_bias=row(up_bias),
            down_any=down_proj,
            down_bias=row(down_bias),
            buckets=bucket_ids.T,
            orders=sort_orders[0],
            docs=doc_lengths[0],
            cotan_one_any=cotan_one,
            cotan_two_any=cotan_two,
        ),
    )
    rows = [found.out_one, found.out_two, found.grad_one, found.grad_two]
    grad_up, grad_down, grad_out, grad_query, grad_value, *rest = run_finish(
        grads, found.small, rows, sort_orders.shape[1]
    )
    gain_one, shift_one, gain_two, shift_two, bias_up, bias_down = [vector.reshape(-1) for vector in rest[4:10]]
    return (
        *rest[:4],
        gain_one,
        shift_one,
        grad_query,
        grad_value,
        grad_out,
        gain_two,
        shift_two,
        grad_up,
        bias_up,
        grad_down,
        bias_down,
        rest[10],
    )


def solution(mesh):
    rows = P(("wide", "narrow"), None)
    columns = P(None, "narrow")
    return jax.shard_map(
        per_device,
        mesh=mesh,
        in_specs=(
            rows,
            rows,
            P(),
            P(),
            columns,
            columns,
            P("narrow", None),
            P(),
            P(),
            columns,
            P("narrow"),
            P("narrow", None),
            P(),
            rows,
            P("wide", None, None),
            P("wide", None),
            rows,
            rows,
        ),
        out_specs=(
            rows,
            rows,
            rows,
            rows,
            P(),
            P(),
            columns,
            columns,
            P("narrow", None),
            P(),
            P(),
            columns,
            P("narrow"),
            P("narrow", None),
            P(),
            P(),
        ),
        check_vma=False,
    )
```

```python
import math
from types import SimpleNamespace

import jax
import jax.numpy as jnp
from jax import lax
from jax.experimental import pallas as pl
from jax.experimental.pallas import tpu as pltpu
from jax.sharding import PartitionSpec as P

HD = 128
GROUP = 64
NB = 24
MOST = 768
BLOCK = 256
LANES = 128
CHUNK = 128
NARROW = 4
VMEM_LIMIT = 60 << 20

FLOAT = jnp.float32
HALF = jnp.bfloat16
NEG = -1e30
EXP_SCALE = math.log2(math.e) / math.sqrt(HD)
FACTOR = 1.0 / math.sqrt(HD)
MESH = pl.DeviceIdType.MESH
IN_VMEM = pl.BlockSpec(memory_space=pltpu.VMEM)
IN_SMEM = pl.BlockSpec(memory_space=pltpu.SMEM)
ANYWHERE = pl.BlockSpec(memory_space=pl.ANY)
DMA = pltpu.SemaphoreType.DMA
WIDE = "wide"
DOCS = "docs"
FROM_HBM = "_any"


def normalize(inputs):
    center = inputs - jnp.mean(inputs, axis=-1, keepdims=True)
    inverse = lax.rsqrt(jnp.mean(center * center, axis=-1, keepdims=True) + 1e-05)
    return (center * inverse, inverse)


def norm_back(grad_out, scaled, inverse, gain):
    spread = grad_out * gain
    return inverse * (
        spread
        - jnp.mean(spread, axis=-1, keepdims=True)
        - scaled * jnp.mean(spread * scaled, axis=-1, keepdims=True)
    )


def contract_rows(left, right):
    return lax.dot_general(left, right, (((0,), (0,)), ((), ())), preferred_element_type=FLOAT)


def times_transpose(left, right):
    return lax.dot_general(left, right, (((1,), (1,)), ((), ())), preferred_element_type=FLOAT)


def times(left, right):
    return jnp.dot(left, right, preferred_element_type=FLOAT)


def column_sums(rows):
    return times(jnp.ones((8, rows.shape[0]), rows.dtype), rows)[0:1]


class Place:
    def __init__(self):
        index = lax.axis_index("narrow")
        core, chip = lax.rem(index, 2), lax.div(index, 2)
        self.me = index
        self.near = 2 * chip + 1 - core
        self.far = 2 * (1 - chip) + core
        self.cross = 2 * (1 - chip) + 1 - core


def span(start, size):
    return pl.ds(pl.multiple_of(start, size), size)


def remote(source, target, sent, arrived, other):
    return pltpu.make_async_remote_copy(
        src_ref=source,
        dst_ref=target,
        send_sem=sent,
        recv_sem=arrived,
        device_id={"narrow": other},
        device_id_type=MESH,
    )


class Gather:
    def __init__(self, place, whole, rows, sems):
        self.place, self.whole, self.rows = place, whole, rows
        self.sent, self.arrived = sems
        self.chunks = rows // CHUNK

    def at(self, owner, chunk):
        return self.whole.at[span(owner * self.rows + chunk * CHUNK, CHUNK), :]

    def copy(self, lane, owner, chunk, other):
        index = lane * self.chunks + chunk
        piece = self.at(owner, chunk)
        return remote(piece, piece, self.sent.at[index], self.arrived.at[index], other)

    def to_far(self, chunk):
        return self.copy(0, self.place.me, chunk, self.place.far)

    def to_near(self, chunk):
        return self.copy(1, self.place.me, chunk, self.place.near)

    def onward(self, chunk):
        return self.copy(2, self.place.far, chunk, self.place.near)

    def send(self, chunk):
        self.to_far(chunk).start()
        self.to_near(chunk).start()

    def take_near(self, chunk):
        self.to_near(chunk).wait_recv()

    def take_far(self, chunk):
        self.to_far(chunk).wait_recv()
        self.onward(chunk).start()

    def take_cross(self, chunk):
        self.onward(chunk).wait_recv()

    def finish(self):
        @pl.loop(0, self.chunks)
        def _(chunk):
            self.to_far(chunk).wait_send()
            self.to_near(chunk).wait_send()
            self.onward(chunk).wait_send()


class Scatter:
    def __init__(self, place, term, rows, buffers, sems):
        self.place, self.term, self.rows = place, term, rows
        self.near_out, self.near_in, self.far_out, self.far_in = buffers
        self.sent, self.arrived = sems
        self.chunks = rows // CHUNK

    def to_near(self, part, chunk):
        index = part * self.chunks + chunk
        at = span(chunk * CHUNK, CHUNK)
        return remote(
            self.near_out.at[part, at, :],
            self.near_in.at[part, at, :],
            self.sent.at[index],
            self.arrived.at[index],
            self.place.near,
        )

    def to_far(self, chunk):
        index = 2 * self.chunks + chunk
        at = span(chunk * CHUNK, CHUNK)
        return remote(
            self.far_out.at[at, :], self.far_in.at[at, :], self.sent.at[index], self.arrived.at[index], self.place.far
        )

    def part(self, owner, chunk):
        return self.term(span(owner * self.rows + chunk * CHUNK, CHUNK))

    def start(self, between=lambda: None):
        @pl.loop(0, self.chunks)
        def _(chunk):
            self.near_out[0, span(chunk * CHUNK, CHUNK), :] = self.part(self.place.cross, chunk).astype(HALF)
            self.to_near(0, chunk).start()

        between()

        @pl.loop(0, self.chunks)
        def _(chunk):
            at = span(chunk * CHUNK, CHUNK)
            own = self.part(self.place.far, chunk)
            self.to_near(0, chunk).wait_recv()
            self.far_out[at, :] = (own + self.near_in[0, at, :].astype(FLOAT)).astype(HALF)
            self.to_far(chunk).start()

        between()

        @pl.loop(0, self.chunks)
        def _(chunk):
            self.near_out[1, span(chunk * CHUNK, CHUNK), :] = self.part(self.place.near, chunk).astype(HALF)
            self.to_near(1, chunk).start()

    def chip_sum(self, chunk):
        own = self.part(self.place.me, chunk)
        self.to_near(1, chunk).wait_recv()
        return own + self.near_in[1, span(chunk * CHUNK, CHUNK), :].astype(FLOAT)

    def take_far(self, chunk):
        self.to_far(chunk).wait_recv()
        return self.far_in[span(chunk * CHUNK, CHUNK), :].astype(FLOAT)

    def finish(self):
        @pl.loop(0, self.chunks)
        def _(chunk):
            self.to_near(0, chunk).wait_send()
            self.to_near(1, chunk).wait_send()
            self.to_far(chunk).wait_send()


def pair_features(orders, docs, query_features, key_features, found):
    rounds, length = orders.shape
    groups = length // GROUP
    high_count = length // LANES
    high_rows = -(-high_count // 8) * 8
    count = docs.shape[0]
    depth = query_features.shape[0]
    lane = lax.broadcasted_iota(jnp.int32, (LANES, length), 1)
    low_at = lax.broadcasted_iota(jnp.int32, (LANES, length), 0)
    high_at = lax.broadcasted_iota(jnp.int32, (high_rows, length), 0)
    group_at = lax.broadcasted_iota(jnp.int32, (groups, LANES), 0).astype(FLOAT)
    sorted_group = lax.shift_right_logical(lane, int(math.log2(GROUP))).astype(FLOAT)

    @pl.loop(0, rounds)
    def _(index):
        row = orders[pl.ds(index, 1), :]
        high = jnp.where(high_at == lax.shift_right_logical(row, int(math.log2(LANES))), 1.0, 0.0)
        low = jnp.where(low_at == (row & (LANES - 1)), sorted_group, 0.0)
        found[index, :high_rows, :LANES] = times_transpose(high.astype(HALF), low.astype(HALF))
    place = lax.broadcasted_iota(jnp.int32, (count, LANES), 1)
    which = lax.broadcasted_iota(jnp.int32, (count, LANES), 0)
    begins = jnp.zeros((count, LANES), jnp.int32)
    ends = jnp.zeros((count, LANES), jnp.int32)
    begin = jnp.int32(0)
    for doc in range(count):
        end = begin + docs[doc]
        begins = jnp.where(which == doc, begin, begins)
        ends = jnp.where(which == doc, end, ends)
        begin = end
    rest = jnp.zeros((depth - rounds * groups - count, LANES), FLOAT)
    for block in range(high_count):
        mine, window = [], []
        for index in range(rounds):
            own = found[index, block : block + 1, :LANES]
            after = jnp.where(own == groups - 1.0, 0.0, own + 1.0)
            here = group_at == own
            mine.append(jnp.where(here, 1.0, 0.0))
            window.append(jnp.where(here | (group_at == after), 1.0, 0.0))
        at = place + block * LANES
        same = jnp.where((at >= begins) & (at < ends), 1.0, 0.0)
        lanes = slice(block * LANES, (block + 1) * LANES)
        query_features[:, lanes] = jnp.concatenate([*mine, same * (2.0 * rounds), rest], axis=0).astype(HALF)
        key_features[:, lanes] = jnp.concatenate([*window, same, rest], axis=0).astype(HALF)


def in_turn(place, step):
    flip_core, flip_chip = lax.rem(step, 2), lax.div(step, 2)
    core, chip = lax.rem(place.me, 2), lax.div(place.me, 2)
    core = core + flip_core * (1 - 2 * core)
    chip = chip + flip_chip * (1 - 2 * chip)
    return 2 * chip + core


def by_arrival(gather, act, after=None):
    place, rows = gather.place, gather.rows
    act(span(place.me * rows, rows))

    @pl.loop(0, gather.chunks)
    def _(chunk):
        gather.take_near(chunk)

    act(span(place.near * rows, rows))
    by_chunk(gather, act, after)


def by_chunk(gather, act, after=None):
    place, rows = gather.place, gather.rows

    @pl.loop(0, gather.chunks)
    def _(chunk):
        gather.take_far(chunk)
        if after is not None:
            pl.when(chunk == gather.chunks - 1)(after)
        act(span(place.far * rows + chunk * CHUNK, CHUNK))
        gather.take_cross(chunk)
        act(span(place.cross * rows + chunk * CHUNK, CHUNK))


def pair_bias(query_features, key_features, rounds, diagonal):
    counts = jnp.maximum(contract_rows(key_features, query_features) - 2.0 * rounds, 0.0)
    bias = jnp.where(counts > 0.0, jnp.log2(counts), NEG)
    if diagonal:
        key_at = lax.broadcasted_iota(jnp.int32, bias.shape, 0)
        query_at = lax.broadcasted_iota(jnp.int32, bias.shape, 1)
        bias = jnp.where(key_at < query_at, bias, NEG)
    return bias


def band_steps(length):
    return min(-(-(MOST - 1) // BLOCK), length // BLOCK - 1) + 1


def block_biases(block, steps, features, rounds, bias):
    query_features, key_features = features
    at = span(block * BLOCK, BLOCK)
    for step in range(steps):
        bias[step] = pair_bias(
            query_features[:, at], key_features[:, span((block - step) * BLOCK, BLOCK)], rounds, step == 0
        )


def attend(block, steps, rounds, queries, keys, values, features, merged, logs, bias, scores):
    at = span(block * BLOCK, BLOCK)
    heads = queries.shape[1] // HD
    block_biases(block, steps, features, rounds, bias)
    for head in range(heads):
        part = slice(head * HD, (head + 1) * HD)
        query = queries[at, part]
        peak = jnp.full((1, BLOCK), 2 * NEG, FLOAT)
        for step in range(steps):
            key_at = span((block - step) * BLOCK, BLOCK)
            score = times_transpose(keys[key_at, part], query) * EXP_SCALE + bias[step]
            scores[span((head * steps + step) * BLOCK, BLOCK), :] = score
            peak = jnp.maximum(peak, jnp.max(score, axis=0, keepdims=True))
        alone = peak < 0.5 * NEG
        peak = jnp.where(alone, 0.0, peak)
        total = jnp.zeros((1, BLOCK), FLOAT)
        mixed = jnp.zeros((HD, BLOCK), FLOAT)
        for step in range(steps):
            key_at = span((block - step) * BLOCK, BLOCK)
            powers = jnp.exp2(scores[span((head * steps + step) * BLOCK, BLOCK), :] - peak)
            total = total + jnp.sum(powers, axis=0, keepdims=True)
            mixed = mixed + contract_rows(values[key_at, part], powers.astype(HALF))
        total = jnp.where(alone, 1.0, total)
        mixed = jnp.where(alone, values[at, part].astype(FLOAT).T, mixed / total)
        merged[at, part] = mixed.T.astype(HALF)
        logs[head : head + 1, at] = jnp.where(alone, -NEG, peak + jnp.log2(total))


def attend_back(block, steps, rounds, queries, keys, values, features, grads, merged, logs, dq, dk, dv, bias):
    at = span(block * BLOCK, BLOCK)
    heads = queries.shape[1] // HD
    block_biases(block, steps, features, rounds, bias)
    ones = jnp.ones((8, HD), HALF)

    @pl.loop(0, heads)
    def _(head):
        part = span(head * HD, HD)
        query, grad = queries[at, part], grads[at, part]
        log_sum = logs[pl.ds(head, 1), at]
        product = grad.astype(FLOAT) * merged[at, part].astype(FLOAT)
        coarse = product.astype(HALF)
        fine = (product - coarse.astype(FLOAT)).astype(HALF)
        along = (times_transpose(ones, coarse) + times_transpose(ones, fine))[0:1]
        grad_query = jnp.zeros((HD, BLOCK), FLOAT)
        for step in range(steps):
            key_at = span((block - step) * BLOCK, BLOCK)
            key = keys[key_at, part]
            weights = jnp.exp2(times_transpose(key, query) * EXP_SCALE + bias[step] - log_sum)
            grad_probs = times_transpose(values[key_at, part], grad)
            grad_scores = (weights * (grad_probs - along)).astype(HALF)
            grad_value = times(weights.astype(HALF), grad)
            grad_key = times(grad_scores, query)
            if step == 0:
                dv[key_at, part] = grad_value
                dk[key_at, part] = grad_key
            else:
                dv[key_at, part] += grad_value
                dk[key_at, part] += grad_key
            grad_query = grad_query + contract_rows(key, grad_scores)
        dq[at, part] = grad_query.T


def finish_attention(queries, grads, logs, dq, dk, dv, grad_query, grad_value):
    length, width = queries.shape

    @pl.loop(0, length // BLOCK)
    def _(block):
        at = span(block * BLOCK, BLOCK)
        alone = jnp.where(logs[:, at] == -NEG, 1.0, 0.0).T
        for head in range(width // HD):
            part = slice(head * HD, (head + 1) * HD)
            grad_value[at, part] = (dv[at, part] + alone[:, head : head + 1] * grads[at, part].astype(FLOAT)).astype(HALF)
            query = queries[at, part].astype(FLOAT)
            key_scale = lax.rsqrt(jnp.sum(query * query, axis=-1, keepdims=True) + 1e-06)
            unit = query * key_scale
            grad_key = dk[at, part] * FACTOR
            key_along = jnp.sum(grad_key * unit, axis=-1, keepdims=True)
            grad_query[at, part] = (dq[at, part] * FACTOR + key_scale * (grad_key - unit * key_along)).astype(HALF)


def gelu_and_slope(hidden):
    square = hidden * hidden
    bend = jnp.tanh(math.sqrt(2.0 / math.pi) * hidden * (1.0 + 0.044715 * square))
    half_more = 0.5 + 0.5 * bend
    slope = half_more + 0.5 * hidden * (1.0 - bend * bend) * (
        math.sqrt(2.0 / math.pi) * (1.0 + 3.0 * 0.044715 * square)
    )
    return hidden * half_more, slope


def weight_grad(result, left, right, rows=None, add=False):
    width = 256
    height = result.shape[1] * result.shape[2] // right.shape[1]
    pieces = width // height
    rows = slice(None) if rows is None else rows

    @pl.loop(0, left.shape[1] // width)
    def _(index):
        block = contract_rows(left[rows, span(index * width, width)], right[rows, :])
        at = pl.ds(index * pieces, pieces)
        block = block.reshape(pieces, *result.shape[1:])
        if add:
            block = block + result[at].astype(FLOAT)
        result[at] = block.astype(result.dtype)


def ring_place(members, index):
    column, row = lax.rem(index, 2), lax.div(index, 2)
    return row + column * (members - 1 - 2 * row)


def ring_member(members, place):
    back = lax.div(place, members // 2)
    return 2 * place + back * (2 * (members - 1 - place) + 1 - 2 * place)


class Ring:
    def __init__(self, members, data, landed, result, sent, arrived, kept):
        self.members, self.data, self.landed, self.result = members, data, landed, result
        self.sent, self.arrived, self.kept, self.stage = sent, arrived, kept, 0
        self.here = ring_place(members, lax.axis_index("wide"))
        self.neighbours = (
            ring_member(members, lax.rem(self.here + 1, members)),
            ring_member(members, lax.rem(self.here + members - 1, members)),
        )

    def piece(self, direction, step):
        if direction == 0:
            return 2 * lax.rem(self.here - step + 2 * self.members, self.members)
        return 2 * lax.rem(self.here + step, self.members) + 1

    def copy(self, direction, step, at, gathering, fresh):
        index = direction * 2 * (self.members - 1) + step
        source = self.landed if gathering and not fresh else self.data
        return pltpu.make_async_remote_copy(
            src_ref=source.at[at],
            dst_ref=self.landed.at[at],
            send_sem=self.sent.at[index],
            recv_sem=self.arrived.at[index],
            device_id={"wide": self.neighbours[direction]},
            device_id_type=MESH,
        )

    def outgoing(self, direction, step, gathering=False, fresh=False):
        return self.copy(direction, step, self.piece(direction, step), gathering, fresh)

    def incoming(self, direction, step, gathering=False):
        return self.copy(direction, step, self.piece(direction, step + 1), gathering, False)

    def begin(self):
        for direction in range(2):
            self.outgoing(direction, 0).start()

    def add(self, direction, step):
        self.incoming(direction, step).wait_recv()
        at = self.piece(direction, step + 1)
        height = min(16, self.data.shape[1])

        @pl.loop(0, self.data.shape[1] // height)
        def _(index):
            rows = span(index * height, height)
            self.data[at, rows] = (
                self.data[at, rows].astype(FLOAT) + self.landed[at, rows].astype(FLOAT)
            ).astype(HALF)

        return at

    def keep(self, direction, step):
        at = self.piece(direction, step)
        source = self.data if isinstance(step, int) and step == self.members - 1 else self.landed
        return pltpu.make_async_copy(
            source.at[at], self.result.at[at], self.kept.at[direction * self.members + step - (self.members - 1)]
        )

    def advance(self):
        stage, last = self.stage, self.members - 1
        if stage == 14:
            return
        self.stage = stage + 1
        low, high = stage * 2 * last // 14, (stage + 1) * 2 * last // 14

        def repeat(begin, end, act):
            if end == begin + 1:
                act(begin)
            elif end > begin:
                pl.loop(begin, end)(act)

        def reduce(step):
            for direction in range(2):
                self.add(direction, step)
                self.outgoing(direction, step + 1).start()

        def forward(step):
            for direction in range(2):
                self.incoming(direction, step, True).wait_recv()
                self.outgoing(direction, step + 1, True).start()
                self.keep(direction, step + 1).start()

        repeat(low, min(high, last - 1), reduce)
        if low <= last - 1 < high:
            for direction in range(2):
                self.add(direction, last - 1)
                self.outgoing(direction, last, True, True).start()
                self.keep(direction, last).start()
        repeat(max(low, last), min(high, 2 * last - 1), forward)
        if low <= 2 * last - 1 < high:
            for direction in range(2):
                self.incoming(direction, 2 * last - 1, True).wait_recv()
                self.keep(direction, 2 * last).start()

    def finish(self):
        last = self.members - 1
        for direction in range(2):
            self.keep(direction, last).wait()
            self.outgoing(direction, last, True, True).wait_send()

        @pl.loop(0, last)
        def _(step):
            for direction in range(2):
                self.outgoing(direction, step).wait_send()

        @pl.loop(last + 1, 2 * last)
        def _(step):
            for direction in range(2):
                self.outgoing(direction, step, True).wait_send()
                self.keep(direction, step).wait()

        for direction in range(2):
            self.keep(direction, 2 * last).wait()


class Exchange:
    def __init__(self, members, data, landed, result, first, unit, bits, sems, stored):
        self.members, self.data, self.landed, self.result = members, data, landed, result
        self.first, self.unit, self.bits = first, unit, bits
        self.sent, self.arrived, self.stored, self.stage = *sems, stored, 0
        self.wide = lax.axis_index("wide")

    def bit(self, step):
        return lax.rem(lax.div(self.wide, 1 << self.bits[step]), 2)

    def size(self, step):
        return self.unit * (self.members >> (step + 1))

    def part(self, step, kept):
        start = self.first
        for before in range(step):
            start = start + self.bit(before) * self.size(before)
        bit = self.bit(step)
        return pl.ds(start + (bit if kept else 1 - bit) * self.size(step), self.size(step))

    def landing(self, step):
        return pl.ds(self.first + self.unit * self.members - 2 * self.size(step), self.size(step))

    def copy(self, step, gathering):
        index = step + gathering * len(self.bits)
        at = self.part(step, gathering)
        source = self.result if gathering and step < len(self.bits) - 1 else self.data
        return pltpu.make_async_remote_copy(
            src_ref=source.at[at],
            dst_ref=self.result.at[at] if gathering else self.landed.at[self.landing(step)],
            send_sem=self.sent.at[index],
            recv_sem=self.arrived.at[index],
            device_id={"wide": self.wide + (1 - 2 * self.bit(step)) * (1 << self.bits[step])},
            device_id_type=MESH,
        )

    def begin(self):
        self.copy(0, False).start()

    def advance(self):
        count, stage = len(self.bits), self.stage
        if stage == 2 * count:
            return
        self.stage = stage + 1
        if stage < count:
            self.copy(stage, False).wait_recv()
            kept, landed = self.part(stage, True), self.landing(stage)

            @pl.loop(0, self.size(stage))
            def _(index):
                at = kept.start + index
                self.data[at] = (
                    self.data[at].astype(FLOAT) + self.landed[landed.start + index].astype(FLOAT)
                ).astype(HALF)

        else:
            self.copy(2 * count - 1 - stage, True).wait_recv()
        if stage < count - 1:
            self.copy(stage + 1, False).start()
            return
        if stage == count - 1:
            self.store().start()
        if stage == count:
            self.store().wait()
        if stage < 2 * count - 1:
            self.copy(2 * count - 2 - stage, True).start()

    def store(self):
        at = self.part(len(self.bits) - 1, True)
        return pltpu.make_async_copy(self.data.at[at], self.result.at[at], self.stored)

    def finish(self):
        for step in range(len(self.bits)):
            self.copy(step, False).wait_send()
            self.copy(step, True).wait_send()


class Everyone:
    def __init__(self, axis, slots, sent, arrived):
        self.axis, self.slots, self.sent, self.arrived = axis, slots, sent, arrived
        self.me, self.members = lax.axis_index(axis), slots.shape[0]

    def copy(self, step):
        mine = self.slots.at[self.me]
        return pltpu.make_async_remote_copy(
            src_ref=mine,
            dst_ref=mine,
            send_sem=self.sent.at[step],
            recv_sem=self.arrived.at[step],
            device_id={self.axis: lax.rem(self.me + step, self.members)},
            device_id_type=MESH,
        )

    def send(self, value):
        self.slots[self.me] = value

        @pl.loop(1, self.members)
        def _(step):
            self.copy(step).start()

    def total(self):
        @pl.loop(1, self.members)
        def _(step):
            self.copy(step).wait()

        return lax.fori_loop(1, self.members, lambda index, total: total + self.slots[index], self.slots[0])


def advance(*exchanges):
    for exchange in exchanges:
        exchange.advance()


def greet_all(members):
    barrier = pltpu.get_barrier_semaphore()
    narrow, wide = lax.axis_index("narrow"), lax.axis_index("wide")

    @pl.loop(1, NARROW)
    def _(step):
        pl.semaphore_signal(
            barrier, inc=1, device_id={"narrow": lax.rem(narrow + step, NARROW)}, device_id_type=MESH
        )

    @pl.loop(1, members)
    def _(step):
        pl.semaphore_signal(barrier, inc=1, device_id={"wide": lax.rem(wide + step, members)}, device_id_type=MESH)

    return lambda: pl.semaphore_wait(barrier, NARROW - 1 + members - 1)


def layer(members, ref):
    place = Place()
    second_rows = ref.stream_two
    rows, width = second_rows.shape
    orders, docs = ref.orders, ref.docs
    rounds, length = orders.shape
    heads = ref.wq.shape[1]
    chunks = rows // CHUNK
    whole_one, whole_two, cotans, grad_rows = (ref.whole_one, ref.whole_two, ref.cotans, ref.grad_rows)
    queries, keys, values, merged, logs = (ref.queries, ref.keys, ref.values, ref.merged, ref.logs)
    features = (ref.query_features, ref.key_features)
    wq, wv, wo, up, down = (ref.wq, ref.wv, ref.wo, ref.up, ref.down)
    active, grad_hidden, middle, first_rows = (ref.active, ref.grad_hidden, ref.middle, ref.first_rows)
    grad_merged, bias, sums = ref.grad_merged, ref.bias, ref.sums
    dq, dk, dv = (ref.totals.at[pl.ds(i * length, length), :] for i in range(3))
    own_at, far_at = span(place.me * rows, rows), span(place.far * rows, rows)
    loads, stores = ref.loads, ref.stores

    def load(index, source, target):
        copy = pltpu.make_async_copy(source, target, loads.at[index])
        copy.start()
        return copy

    meet = greet_all(members)
    load_wq, load_wv = load(0, ref.wq_any, wq), load(1, ref.wv_any, wv)
    load_cotan = load(2, ref.cotan_two_any, cotans.at[own_at, :])
    load_wo, load_first = load(3, ref.wo_any, wo), load(4, ref.stream_one_any, first_rows)
    load_down, load_up = load(5, ref.down_any, down), load(6, ref.up_any, up)

    up_ring, down_ring = rings = [
        Ring(
            members, ref.sum_data[i], ref.sum_landed[i], ref.sum_results[i], ref.ring_sent.at[i], ref.ring_arrived.at[i],
            ref.ring_kept.at[i],
        )
        for i in range(2)
    ]
    bits = list(range(members.bit_length() - 1))
    swapped = bits[1::-1] + bits[2:]
    lanes = ((2, 0, bits), (2, members, swapped), (3, 0, bits), (3, members, swapped))
    out_sum, out_swap, in_sum, in_swap = exchanges = [
        Exchange(
            members, ref.sum_data[array], ref.sum_landed[array], ref.sum_results[array], first, 1, order,
            (ref.sum_sent.at[lane], ref.sum_arrived.at[lane]), ref.sum_stored.at[lane],
        )
        for lane, (array, first, order) in enumerate(lanes)
    ]
    queue = [up_ring, down_ring]

    def serve(*more):
        ring = queue.pop(0)
        queue.append(ring)
        advance(ring, *more)

    gather = Gather(place, whole_one, rows, (ref.gather_sent.at[0], ref.gather_arrived.at[0]))

    @pl.loop(0, chunks)
    def _(chunk):
        scaled, _ = normalize(second_rows[span(chunk * CHUNK, CHUNK), :].astype(FLOAT))
        normed = (scaled * ref.gain_one[...] + ref.shift_one[...]).astype(HALF)
        whole_one[span(place.me * rows + chunk * CHUNK, CHUNK), :] = normed

    meet()

    @pl.loop(0, chunks)
    def _(chunk):
        gather.send(chunk)

    pair_features(orders, docs, *features, bias)
    level = lax.broadcasted_iota(jnp.int32, (LANES, rows), 0)
    counted = jnp.ones((8, rows), HALF)
    sums[...] = jnp.zeros_like(sums)
    for index in range(rounds):
        found = jnp.where(level == ref.buckets[index : index + 1, :], 1.0, 0.0).astype(HALF)
        sums[4:5, index * LANES : (index + 1) * LANES] = times_transpose(counted, found)[0:1]
    load_wq.wait()
    load_wv.wait()

    def project(at):
        query = times(whole_one[at, :], wq[...]).astype(HALF)
        queries[at, :] = query
        for head in range(heads // HD):
            part = query[:, head * HD : (head + 1) * HD].astype(FLOAT)
            scale = lax.rsqrt(jnp.sum(part * part, axis=-1, keepdims=True) + 1e-06)
            keys[at, head * HD : (head + 1) * HD] = (part * scale).astype(HALF)
        values[at, :] = times(whole_one[at, :], wv[...]).astype(HALF)

    load_cotan.wait()
    spread = Gather(place, cotans, rows, (ref.gather_sent.at[1], ref.gather_arrived.at[1]))

    def send_cotangents():
        @pl.loop(0, chunks)
        def _(chunk):
            spread.send(chunk)

    by_arrival(gather, project, send_cotangents)
    gather.finish()

    steps = band_steps(length)
    blocks = length // BLOCK

    def forward(block, count):
        attend(block, count, rounds, queries, keys, values, features, merged, logs, bias, ref.totals)

    for block in range(steps - 1):
        forward(block, block + 1)

    @pl.loop(steps - 1, blocks)
    def _(block):
        forward(block, steps)

    buffers = (ref.near_out, ref.near_in, ref.far_out, ref.far_in)
    load_wo.wait()
    scatter = Scatter(
        place, lambda at: times(merged[at, :], wo[...]), rows, buffers, (ref.scatter_sent.at[0], ref.scatter_arrived.at[0])
    )
    scatter.start()
    load_first.wait()

    @pl.loop(0, chunks)
    def _(chunk):
        at = span(chunk * CHUNK, CHUNK)
        middle[at, :] = first_rows[at, :].astype(FLOAT) + scatter.chip_sum(chunk)

    @pl.loop(0, chunks)
    def _(chunk):
        spread.take_near(chunk)
        spread.take_far(chunk)

    load_down.wait()
    half_width = width // 2

    def grad_active(owner):
        @pl.loop(0, 2)
        def _(half):
            at = span(half * half_width, half_width)
            grad_hidden[span(owner * rows, rows), at] = times_transpose(
                cotans[span(owner * rows, rows), :], down[at, :]
            ).astype(HALF)

    @pl.loop(0, NARROW)
    def _(step):
        @pl.when(step == NARROW - 1)
        def _():
            @pl.loop(0, chunks)
            def _(chunk):
                spread.take_cross(chunk)

        grad_active(in_turn(place, step))

    gather = Gather(place, whole_two, rows, (ref.gather_sent.at[2], ref.gather_arrived.at[2]))
    load_up.wait()

    @pl.loop(0, chunks)
    def _(chunk):
        at = span(chunk * CHUNK, CHUNK)
        value = middle[at, :] + scatter.take_far(chunk)
        middle[at, :] = value
        first_rows[at, :] = value.astype(HALF)
        scaled, _ = normalize(value)
        whole_two[span(place.me * rows + chunk * CHUNK, CHUNK), :] = (
            scaled * ref.gain_two[...] + ref.shift_two[...]
        ).astype(HALF)
        gather.send(chunk)

    store_one = pltpu.make_async_copy(first_rows, ref.out_one, stores.at[0])
    store_one.start()

    def feed(row_at):
        @pl.loop(0, 2)
        def _(half):
            at = span(half * half_width, half_width)
            value, slope = gelu_and_slope(times(whole_two[row_at, :], up[:, at]) + ref.up_bias[:, at])
            active[row_at, at] = value.astype(HALF)
            grad_hidden[row_at, at] = (grad_hidden[row_at, at].astype(FLOAT) * slope).astype(HALF)

    chip = lax.div(place.me, 2)
    here, there = span(chip * 2 * rows, 2 * rows), span((1 - chip) * 2 * rows, 2 * rows)
    feed(span(place.me * rows, rows))

    @pl.loop(0, chunks)
    def _(chunk):
        gather.take_near(chunk)

    feed(span(place.near * rows, rows))
    weight_grad(ref.sum_data[1], active, cotans, here)
    weight_grad(ref.sum_data[0], whole_two, grad_hidden, here)
    by_chunk(gather, feed)
    scatter.finish()

    store_one.wait()
    load_cotan_one = load(7, ref.cotan_one_any, first_rows)
    scatter = Scatter(
        place,
        lambda at: times_transpose(grad_hidden[at, :], up[...]),
        rows,
        buffers,
        (ref.scatter_sent.at[1], ref.scatter_arrived.at[1]),
    )

    weight_grad(ref.sum_data[1], active, cotans, there, True)
    down_ring.begin()
    scatter.start()
    weight_grad(ref.sum_data[0], whole_two, grad_hidden, there, True)
    up_ring.begin()
    queue.reverse()
    back = Gather(place, grad_rows, rows, (ref.gather_sent.at[3], ref.gather_arrived.at[3]))
    load_cotan_one.wait()

    for chunk in range(chunks):
        at = span(chunk * CHUNK, CHUNK)
        grad_normed = scatter.chip_sum(chunk) + scatter.take_far(chunk)
        scaled, inverse = normalize(middle[at, :])
        grad = first_rows[at, :].astype(FLOAT) + norm_back(grad_normed, scaled, inverse, ref.gain_two[...])
        grad_rows[span(place.me * rows + chunk * CHUNK, CHUNK), :] = grad.astype(HALF)
        back.send(chunk)
        sums[2:3, :] += jnp.sum(grad_normed * scaled, axis=0, keepdims=True)
        sums[3:4, :] += jnp.sum(grad_normed, axis=0, keepdims=True)
        serve()
        serve()

    def merge_back(at):
        grad_merged[at, :] = times_transpose(grad_rows[at, :], wo[...]).astype(HALF)

    store_grad = pltpu.make_async_copy(grad_rows.at[own_at, :], ref.grad_one, stores.at[1])
    store_grad.start()
    own_sums = ref.wide_all.at[lax.axis_index(WIDE)]
    own_sums[5:6, :] = column_sums(grad_hidden[...])
    own_sums[6:7, :] = column_sums(cotans[...])
    scatter.finish()
    gather.finish()
    spread.finish()

    merge_back(span(place.me * rows, rows))
    serve()

    @pl.loop(0, chunks)
    def _(chunk):
        back.take_near(chunk)

    merge_back(span(place.near * rows, rows))
    serve()
    for chunk in range(chunks):
        back.take_far(chunk)
        merge_back(span(place.far * rows + chunk * CHUNK, CHUNK))
        back.take_cross(chunk)
        merge_back(span(place.cross * rows + chunk * CHUNK, CHUNK))
        serve()
    serve()
    weight_grad(ref.sum_data[2], merged, grad_rows)
    out_sum.begin()
    out_swap.begin()
    serve()

    fed = Scatter(
        place, lambda at: times(active[at, :], down[...]), rows, buffers, (ref.scatter_sent.at[2], ref.scatter_arrived.at[2])
    )
    fed.start()
    serve()

    def take_fed():
        @pl.loop(0, chunks)
        def _(chunk):
            at = span(chunk * CHUNK, CHUNK)
            total = fed.chip_sum(chunk) + fed.take_far(chunk) + ref.down_bias[...]
            cotans[span(place.near * rows + chunk * CHUNK, CHUNK), :] = (
                second_rows[at, :].astype(FLOAT) + total
            ).astype(HALF)

        store_two.start()
        fed.finish()
        for other in (place.near, place.far):
            pl.semaphore_signal(ref.ready, inc=1, device_id={"narrow": other}, device_id_type=MESH)

    store_two = pltpu.make_async_copy(cotans.at[span(place.near * rows, rows), :], ref.out_two, stores.at[2])

    for block in range(blocks):

        attend_back(
            block, min(block + 1, steps), rounds, queries, keys, values, features, grad_merged, merged, logs, dq, dk, dv, bias
        )
        serve()
        if block > 2:
            serve(out_sum, out_swap)
        if block == blocks - 2:
            take_fed()

    grad_query, grad_value = ref.grad_query, ref.grad_value
    finish_attention(queries, grad_merged, logs, dq, dk, dv, grad_query, grad_value)
    serve()
    weight_grad(ref.sum_data[3], whole_one, ref.grad_both)
    in_sum.begin()
    in_swap.begin()
    pl.semaphore_wait(ref.ready, 2)

    scatter = Scatter(
        place,
        lambda at: times_transpose(grad_query[at, :], wq[...]) + times_transpose(grad_value[at, :], wv[...]),
        rows,
        buffers,
        (ref.scatter_sent.at[3], ref.scatter_arrived.at[3]),
    )
    scatter.start()
    serve(out_sum, out_swap)
    serve(in_swap, in_sum)

    for chunk in range(chunks):
        at = span(chunk * CHUNK, CHUNK)
        grad_normed = scatter.chip_sum(chunk) + scatter.take_far(chunk)
        scaled, inverse = normalize(second_rows[at, :].astype(FLOAT))
        mine = span(place.me * rows + chunk * CHUNK, CHUNK)
        cotans[mine, :] = (
            cotans[mine, :].astype(FLOAT) + norm_back(grad_normed, scaled, inverse, ref.gain_one[...])
        ).astype(HALF)
        sums[0:1, :] += jnp.sum(grad_normed * scaled, axis=0, keepdims=True)
        sums[1:2, :] += jnp.sum(grad_normed, axis=0, keepdims=True)
        serve(*exchanges)
        serve()

    store_last = pltpu.make_async_copy(cotans.at[own_at, :], ref.grad_two, stores.at[3])
    store_last.start()
    over_narrow = Everyone("narrow", ref.narrow_all, ref.narrow_sent, ref.narrow_arrived)
    over_wide = Everyone("wide", ref.wide_all, ref.wide_sent, ref.wide_arrived)
    over_narrow.send(sums[...])
    serve(*exchanges)
    sums[...] = over_narrow.total()
    sums[5:7, :] = own_sums[5:7, :]
    over_wide.send(sums[...])
    while min(exchange.stage for exchange in exchanges) < 2 * len(bits) or min(ring.stage for ring in rings) < 14:
        serve(*exchanges)
    ref.small[...] = over_wide.total()
    scatter.finish()
    back.finish()
    for copy in (store_grad, store_two, store_last):
        copy.wait()
    for exchange in [*exchanges, *rings]:
        exchange.finish()


def pieces(members, shape):
    columns = shape[1] if members <= 8 else LANES
    return (2 * members, shape[0] * shape[1] // (2 * members * columns), columns)


def run_layer(members, args):
    rows, width = args.stream_two.shape
    length, heads, hidden = NARROW * rows, args.wq_any.shape[1], args.up_any.shape[1]
    rounds = args.orders.shape[0]
    chunks = rows // CHUNK
    depth = -(-(rounds * (length // GROUP) + args.docs.shape[0]) // LANES) * LANES
    weights = [(width, hidden), (hidden, width), (heads, width), (width, 2 * heads)]
    cut = [pieces(members, shape) for shape in weights]
    args = vars(args)
    in_specs = [IN_SMEM if k == DOCS else ANYWHERE if k.endswith(FROM_HBM) else IN_VMEM for k in args]
    outs = dict(
        out_one=((rows, width), HALF),
        out_two=((rows, width), HALF),
        grad_one=((rows, width), HALF),
        grad_two=((rows, width), HALF),
        small=((8, width), FLOAT),
    )
    out_shape = [jax.ShapeDtypeStruct(*o) for o in outs.values()] + [jax.ShapeDtypeStruct(shape, HALF) for shape in cut]
    out_specs = [ANYWHERE] * 4 + [IN_VMEM] + [ANYWHERE] * len(cut)
    tall = pltpu.VMEM((length, width), HALF)
    slim = pltpu.VMEM((length, heads), HALF)
    gather_sems, scatter_sems = DMA((4, 3 * chunks)), DMA((4, 3 * chunks))
    sum_sems = DMA((4, 2 * (members.bit_length() - 1)))
    ring_sems = DMA((2, 4 * (members - 1)))
    scratch = dict(
        whole_one=tall,
        whole_two=tall,
        cotans=tall,
        grad_rows=tall,
        active=pltpu.VMEM((length, hidden), HALF),
        grad_hidden=pltpu.VMEM((length, hidden), HALF),
        queries=slim,
        keys=slim,
        values=slim,
        merged=slim,
        grad_merged=slim,
        grad_both=pltpu.VMEM((length, 2 * heads), HALF),
        logs=pltpu.VMEM((8, length), FLOAT),
        query_features=pltpu.VMEM((depth, length), HALF),
        key_features=pltpu.VMEM((depth, length), HALF),
        wq=pltpu.VMEM((width, heads), HALF),
        wv=pltpu.VMEM((width, heads), HALF),
        wo=pltpu.VMEM((heads, width), HALF),
        up=pltpu.VMEM((width, hidden), HALF),
        down=pltpu.VMEM((hidden, width), HALF),
        middle=pltpu.VMEM((rows, width), FLOAT),
        first_rows=pltpu.VMEM((rows, width), HALF),
        bias=pltpu.VMEM((max(rounds, band_steps(length)), BLOCK, BLOCK), FLOAT),
        totals=pltpu.VMEM((3 * length, heads), FLOAT),
        sums=pltpu.VMEM((8, width), FLOAT),
        near_out=pltpu.VMEM((2, rows, width), HALF),
        near_in=pltpu.VMEM((2, rows, width), HALF),
        far_out=pltpu.VMEM((rows, width), HALF),
        far_in=pltpu.VMEM((rows, width), HALF),
        narrow_all=pltpu.VMEM((NARROW, 8, width), FLOAT),
        wide_all=pltpu.VMEM((members, 8, width), FLOAT),
        narrow_sent=DMA((NARROW,)),
        narrow_arrived=DMA((NARROW,)),
        wide_sent=DMA((members,)),
        wide_arrived=DMA((members,)),
        loads=DMA((8,)),
        stores=DMA((4,)),
        ready=pltpu.SemaphoreType.REGULAR,
        gather_sent=gather_sems,
        gather_arrived=gather_sems,
        scatter_sent=scatter_sems,
        scatter_arrived=scatter_sems,
        ring_sent=ring_sems,
        ring_arrived=ring_sems,
        ring_kept=DMA((2, 2 * members)),
        sum_sent=sum_sems,
        sum_arrived=sum_sems,
        sum_stored=DMA((4,)),
    )
    sum_buffers = [pltpu.VMEM(shape, HALF) for shape in cut]

    def kernel(*refs):
        count = len(args) + len(outs)
        named = dict(zip([*args, *outs], refs[:count]))
        results, rest = refs[count : count + len(cut)], refs[count + len(cut) :]
        named |= dict(zip(scratch, rest))
        rest = rest[len(scratch) :]
        ref = SimpleNamespace(**named, sum_results=results, sum_data=rest[: len(cut)], sum_landed=rest[len(cut) :])
        ref.grad_query = ref.grad_both.at[:, pl.ds(0, heads)]
        ref.grad_value = ref.grad_both.at[:, pl.ds(heads, heads)]
        layer(members, ref)

    found = pl.pallas_call(
        kernel,
        out_shape=out_shape,
        in_specs=in_specs,
        out_specs=out_specs,
        scratch_shapes=[*scratch.values(), *sum_buffers, *sum_buffers],
        compiler_params=pltpu.CompilerParams(collective_id=0, has_side_effects=True, vmem_limit_bytes=VMEM_LIMIT),
        name=layer.__name__,
    )(*args.values())
    sums = [result.reshape(shape) for result, shape in zip(found[len(outs) :], weights)]
    return SimpleNamespace(**dict(zip(outs, found))), sums


def finish(*refs):
    up, down, out, both, small, *rows = refs[:9]
    grad_up, grad_down, grad_out, grad_query, grad_value, *rest = refs[9:]
    heads = grad_query.shape[1]
    grad_up[...] = up[...].astype(FLOAT)
    grad_down[...] = down[...].astype(FLOAT)
    grad_out[...] = out[...].astype(FLOAT)
    grad_query[...] = both[:, :heads].astype(FLOAT)
    grad_value[...] = both[:, heads:].astype(FLOAT)
    for source, target in zip(rows, rest):
        target[...] = source[...]
    for source, target in zip((0, 1, 2, 3, 5, 6), rest[len(rows) :]):
        target[...] = small[source : source + 1, :]
    counts = rest[-1]
    for index in range(counts.shape[0]):
        counts[index : index + 1, :] = small[4:5, index * LANES : index * LANES + counts.shape[1]].astype(jnp.int32)


def run_finish(grads, small, rows, rounds):
    up, down, out, both = grads
    parts = 4
    vector = jax.ShapeDtypeStruct((1, small.shape[1]), FLOAT)
    taken = [up, down, out, both, small, *rows]
    given = [
        jax.ShapeDtypeStruct(up.shape, FLOAT),
        jax.ShapeDtypeStruct(down.shape, FLOAT),
        jax.ShapeDtypeStruct(out.shape, FLOAT),
        jax.ShapeDtypeStruct((both.shape[0], both.shape[1] // 2), FLOAT),
        jax.ShapeDtypeStruct((both.shape[0], both.shape[1] // 2), FLOAT),
        *[jax.ShapeDtypeStruct(r.shape, r.dtype) for r in rows],
        *[vector] * 6,
        jax.ShapeDtypeStruct((rounds, NB), jnp.int32),
    ]

    def spec(array):
        if array.shape[0] < LANES:
            return pl.BlockSpec(array.shape, lambda i: (0, 0))
        return pl.BlockSpec((array.shape[0] // parts, array.shape[1]), lambda i: (i, 0))

    return pl.pallas_call(
        finish,
        grid=(parts,),
        out_shape=given,
        in_specs=[spec(a) for a in taken],
        out_specs=[spec(a) for a in given],
        compiler_params=pltpu.CompilerParams(vmem_limit_bytes=VMEM_LIMIT),
        name=finish.__name__,
    )(*taken)


def per_device(
    stream_one,
    stream_two,
    attention_gain,
    attention_shift,
    query_proj,
    value_proj,
    output_proj,
    forward_gain,
    forward_shift,
    up_proj,
    up_bias,
    down_proj,
    down_bias,
    bucket_ids,
    sort_orders,
    doc_lengths,
    cotan_one,
    cotan_two,
):
    members = lax.axis_size("wide")
    row = lambda vector: vector.reshape(1, -1)
    found, grads = run_layer(
        members,
        SimpleNamespace(
            stream_one_any=stream_one,
            stream_two=stream_two,
            gain_one=row(attention_gain),
            shift_one=row(attention_shift),
            wq_any=query_proj,
            wv_any=value_proj,
            wo_any=output_proj,
            gain_two=row(forward_gain),
            shift_two=row(forward_shift),
            up_any=up_proj,
            up_bias=row(up_bias),
            down_any=down_proj,
            down_bias=row(down_bias),
            buckets=bucket_ids.T,
            orders=sort_orders[0],
            docs=doc_lengths[0],
            cotan_one_any=cotan_one,
            cotan_two_any=cotan_two,
        ),
    )
    rows = [found.out_one, found.out_two, found.grad_one, found.grad_two]
    grad_up, grad_down, grad_out, grad_query, grad_value, *rest = run_finish(
        grads, found.small, rows, sort_orders.shape[1]
    )
    gain_one, shift_one, gain_two, shift_two, bias_up, bias_down = [vector.reshape(-1) for vector in rest[4:10]]
    return (
        *rest[:4],
        gain_one,
        shift_one,
        grad_query,
        grad_value,
        grad_out,
        gain_two,
        shift_two,
        grad_up,
        bias_up,
        grad_down,
        bias_down,
        rest[10],
    )


def solution(mesh):
    rows = P(("wide", "narrow"), None)
    columns = P(None, "narrow")
    return jax.shard_map(
        per_device,
        mesh=mesh,
        in_specs=(
            rows,
            rows,
            P(),
            P(),
            columns,
            columns,
            P("narrow", None),
            P(),
            P(),
            columns,
            P("narrow"),
            P("narrow", None),
            P(),
            rows,
            P("wide", None, None),
            P("wide", None),
            rows,
            rows,
        ),
        out_specs=(
            rows,
            rows,
            rows,
            rows,
            P(),
            P(),
            columns,
            columns,
            P("narrow", None),
            P(),
            P(),
            columns,
            P("narrow"),
            P("narrow", None),
            P(),
            P(),
        ),
        check_vma=False,
    )
```

```python
import math
from types import SimpleNamespace

import jax
import jax.numpy as jnp
from jax import lax
from jax.experimental import pallas as pl
from jax.experimental.pallas import tpu as pltpu
from jax.sharding import PartitionSpec as P

HD = 128
GROUP = 64
NB = 24
MOST = 768
BLOCK = 256
LANES = 128
CHUNK = 128
NARROW = 4
VMEM_LIMIT = 60 << 20

FLOAT = jnp.float32
HALF = jnp.bfloat16
NEG = -1e30
EXP_SCALE = math.log2(math.e) / math.sqrt(HD)
FACTOR = 1.0 / math.sqrt(HD)
MESH = pl.DeviceIdType.MESH
IN_VMEM = pl.BlockSpec(memory_space=pltpu.VMEM)
IN_SMEM = pl.BlockSpec(memory_space=pltpu.SMEM)
ANYWHERE = pl.BlockSpec(memory_space=pl.ANY)
DMA = pltpu.SemaphoreType.DMA
WIDE = "wide"
DOCS = "docs"
FROM_HBM = "_any"


def normalize(inputs):
    center = inputs - jnp.mean(inputs, axis=-1, keepdims=True)
    inverse = lax.rsqrt(jnp.mean(center * center, axis=-1, keepdims=True) + 1e-05)
    return (center * inverse, inverse)


def norm_back(grad_out, scaled, inverse, gain):
    spread = grad_out * gain
    return inverse * (
        spread
        - jnp.mean(spread, axis=-1, keepdims=True)
        - scaled * jnp.mean(spread * scaled, axis=-1, keepdims=True)
    )


def contract_rows(left, right):
    return lax.dot_general(left, right, (((0,), (0,)), ((), ())), preferred_element_type=FLOAT)


def times_transpose(left, right):
    return lax.dot_general(left, right, (((1,), (1,)), ((), ())), preferred_element_type=FLOAT)


def times(left, right):
    return jnp.dot(left, right, preferred_element_type=FLOAT)


def column_sums(rows):
    return times(jnp.ones((8, rows.shape[0]), rows.dtype), rows)[0:1]


class Place:
    def __init__(self):
        index = lax.axis_index("narrow")
        core, chip = lax.rem(index, 2), lax.div(index, 2)
        self.me = index
        self.near = 2 * chip + 1 - core
        self.far = 2 * (1 - chip) + core
        self.cross = 2 * (1 - chip) + 1 - core


def span(start, size):
    return pl.ds(pl.multiple_of(start, size), size)


def remote(source, target, sent, arrived, other):
    return pltpu.make_async_remote_copy(
        src_ref=source,
        dst_ref=target,
        send_sem=sent,
        recv_sem=arrived,
        device_id={"narrow": other},
        device_id_type=MESH,
    )


class Gather:
    def __init__(self, place, whole, rows, sems):
        self.place, self.whole, self.rows = place, whole, rows
        self.sent, self.arrived = sems
        self.chunks = rows // CHUNK

    def at(self, owner, chunk):
        return self.whole.at[span(owner * self.rows + chunk * CHUNK, CHUNK), :]

    def copy(self, lane, owner, chunk, other):
        index = lane * self.chunks + chunk
        piece = self.at(owner, chunk)
        return remote(piece, piece, self.sent.at[index], self.arrived.at[index], other)

    def to_far(self, chunk):
        return self.copy(0, self.place.me, chunk, self.place.far)

    def to_near(self, chunk):
        return self.copy(1, self.place.me, chunk, self.place.near)

    def onward(self, chunk):
        return self.copy(2, self.place.far, chunk, self.place.near)

    def send(self, chunk):
        self.to_far(chunk).start()
        self.to_near(chunk).start()

    def take_near(self, chunk):
        self.to_near(chunk).wait_recv()

    def take_far(self, chunk):
        self.to_far(chunk).wait_recv()
        self.onward(chunk).start()

    def take_cross(self, chunk):
        self.onward(chunk).wait_recv()

    def finish(self):
        @pl.loop(0, self.chunks)
        def _(chunk):
            self.to_far(chunk).wait_send()
            self.to_near(chunk).wait_send()
            self.onward(chunk).wait_send()


class Scatter:
    def __init__(self, place, term, rows, buffers, sems):
        self.place, self.term, self.rows = place, term, rows
        self.near_out, self.near_in, self.far_out, self.far_in = buffers
        self.sent, self.arrived = sems
        self.chunks = rows // CHUNK

    def to_near(self, part, chunk):
        index = part * self.chunks + chunk
        at = span(chunk * CHUNK, CHUNK)
        return remote(
            self.near_out.at[part, at, :],
            self.near_in.at[part, at, :],
            self.sent.at[index],
            self.arrived.at[index],
            self.place.near,
        )

    def to_far(self, chunk):
        index = 2 * self.chunks + chunk
        at = span(chunk * CHUNK, CHUNK)
        return remote(
            self.far_out.at[at, :], self.far_in.at[at, :], self.sent.at[index], self.arrived.at[index], self.place.far
        )

    def part(self, owner, chunk):
        return self.term(span(owner * self.rows + chunk * CHUNK, CHUNK))

    def start(self, between=lambda: None):
        @pl.loop(0, self.chunks)
        def _(chunk):
            self.near_out[0, span(chunk * CHUNK, CHUNK), :] = self.part(self.place.cross, chunk).astype(HALF)
            self.to_near(0, chunk).start()

        between()

        @pl.loop(0, self.chunks)
        def _(chunk):
            at = span(chunk * CHUNK, CHUNK)
            own = self.part(self.place.far, chunk)
            self.to_near(0, chunk).wait_recv()
            self.far_out[at, :] = (own + self.near_in[0, at, :].astype(FLOAT)).astype(HALF)
            self.to_far(chunk).start()

        between()

        @pl.loop(0, self.chunks)
        def _(chunk):
            self.near_out[1, span(chunk * CHUNK, CHUNK), :] = self.part(self.place.near, chunk).astype(HALF)
            self.to_near(1, chunk).start()

    def chip_sum(self, chunk):
        own = self.part(self.place.me, chunk)
        self.to_near(1, chunk).wait_recv()
        return own + self.near_in[1, span(chunk * CHUNK, CHUNK), :].astype(FLOAT)

    def take_far(self, chunk):
        self.to_far(chunk).wait_recv()
        return self.far_in[span(chunk * CHUNK, CHUNK), :].astype(FLOAT)

    def finish(self):
        @pl.loop(0, self.chunks)
        def _(chunk):
            self.to_near(0, chunk).wait_send()
            self.to_near(1, chunk).wait_send()
            self.to_far(chunk).wait_send()


def pair_features(orders, docs, query_features, key_features, found):
    rounds, length = orders.shape
    groups = length // GROUP
    high_count = length // LANES
    high_rows = -(-high_count // 8) * 8
    count = docs.shape[0]
    depth = query_features.shape[0]
    lane = lax.broadcasted_iota(jnp.int32, (LANES, length), 1)
    low_at = lax.broadcasted_iota(jnp.int32, (LANES, length), 0)
    high_at = lax.broadcasted_iota(jnp.int32, (high_rows, length), 0)
    group_at = lax.broadcasted_iota(jnp.int32, (groups, LANES), 0).astype(FLOAT)
    sorted_group = lax.shift_right_logical(lane, int(math.log2(GROUP))).astype(FLOAT)

    @pl.loop(0, rounds)
    def _(index):
        row = orders[pl.ds(index, 1), :]
        high = jnp.where(high_at == lax.shift_right_logical(row, int(math.log2(LANES))), 1.0, 0.0)
        low = jnp.where(low_at == (row & (LANES - 1)), sorted_group, 0.0)
        found[index, :high_rows, :LANES] = times_transpose(high.astype(HALF), low.astype(HALF))
    place = lax.broadcasted_iota(jnp.int32, (count, LANES), 1)
    which = lax.broadcasted_iota(jnp.int32, (count, LANES), 0)
    begins = jnp.zeros((count, LANES), jnp.int32)
    ends = jnp.zeros((count, LANES), jnp.int32)
    begin = jnp.int32(0)
    for doc in range(count):
        end = begin + docs[doc]
        begins = jnp.where(which == doc, begin, begins)
        ends = jnp.where(which == doc, end, ends)
        begin = end
    rest = jnp.zeros((depth - rounds * groups - count, LANES), FLOAT)
    for block in range(high_count):
        mine, window = [], []
        for index in range(rounds):
            own = found[index, block : block + 1, :LANES]
            after = jnp.where(own == groups - 1.0, 0.0, own + 1.0)
            here = group_at == own
            mine.append(jnp.where(here, 1.0, 0.0))
            window.append(jnp.where(here | (group_at == after), 1.0, 0.0))
        at = place + block * LANES
        same = jnp.where((at >= begins) & (at < ends), 1.0, 0.0)
        lanes = slice(block * LANES, (block + 1) * LANES)
        query_features[:, lanes] = jnp.concatenate([*mine, same * (2.0 * rounds), rest], axis=0).astype(HALF)
        key_features[:, lanes] = jnp.concatenate([*window, same, rest], axis=0).astype(HALF)


def in_turn(place, step):
    flip_core, flip_chip = lax.rem(step, 2), lax.div(step, 2)
    core, chip = lax.rem(place.me, 2), lax.div(place.me, 2)
    core = core + flip_core * (1 - 2 * core)
    chip = chip + flip_chip * (1 - 2 * chip)
    return 2 * chip + core


def by_arrival(gather, act, after=None):
    place, rows = gather.place, gather.rows
    act(span(place.me * rows, rows))

    @pl.loop(0, gather.chunks)
    def _(chunk):
        gather.take_near(chunk)

    act(span(place.near * rows, rows))
    by_chunk(gather, act, after)


def by_chunk(gather, act, after=None):
    place, rows = gather.place, gather.rows

    @pl.loop(0, gather.chunks)
    def _(chunk):
        gather.take_far(chunk)
        if after is not None:
            pl.when(chunk == gather.chunks - 1)(after)
        act(span(place.far * rows + chunk * CHUNK, CHUNK))
        gather.take_cross(chunk)
        act(span(place.cross * rows + chunk * CHUNK, CHUNK))


def pair_bias(query_features, key_features, rounds, diagonal):
    counts = jnp.maximum(contract_rows(key_features, query_features) - 2.0 * rounds, 0.0)
    bias = jnp.where(counts > 0.0, jnp.log2(counts), NEG)
    if diagonal:
        key_at = lax.broadcasted_iota(jnp.int32, bias.shape, 0)
        query_at = lax.broadcasted_iota(jnp.int32, bias.shape, 1)
        bias = jnp.where(key_at < query_at, bias, NEG)
    return bias


def band_steps(length):
    return min(-(-(MOST - 1) // BLOCK), length // BLOCK - 1) + 1


def block_biases(block, steps, features, rounds, bias):
    query_features, key_features = features
    at = span(block * BLOCK, BLOCK)
    for step in range(steps):
        bias[step] = pair_bias(
            query_features[:, at], key_features[:, span((block - step) * BLOCK, BLOCK)], rounds, step == 0
        )


def attend(block, steps, rounds, queries, keys, values, features, merged, logs, bias, scores):
    at = span(block * BLOCK, BLOCK)
    heads = queries.shape[1] // HD
    block_biases(block, steps, features, rounds, bias)
    for head in range(heads):
        part = slice(head * HD, (head + 1) * HD)
        query = queries[at, part]
        peak = jnp.full((1, BLOCK), 2 * NEG, FLOAT)
        for step in range(steps):
            key_at = span((block - step) * BLOCK, BLOCK)
            score = times_transpose(keys[key_at, part], query) * EXP_SCALE + bias[step]
            scores[span((head * steps + step) * BLOCK, BLOCK), :] = score
            peak = jnp.maximum(peak, jnp.max(score, axis=0, keepdims=True))
        alone = peak < 0.5 * NEG
        peak = jnp.where(alone, 0.0, peak)
        total = jnp.zeros((1, BLOCK), FLOAT)
        mixed = jnp.zeros((HD, BLOCK), FLOAT)
        for step in range(steps):
            key_at = span((block - step) * BLOCK, BLOCK)
            powers = jnp.exp2(scores[span((head * steps + step) * BLOCK, BLOCK), :] - peak)
            total = total + jnp.sum(powers, axis=0, keepdims=True)
            mixed = mixed + contract_rows(values[key_at, part], powers.astype(HALF))
        total = jnp.where(alone, 1.0, total)
        mixed = jnp.where(alone, values[at, part].astype(FLOAT).T, mixed / total)
        merged[at, part] = mixed.T.astype(HALF)
        logs[head : head + 1, at] = jnp.where(alone, -NEG, peak + jnp.log2(total))


def attend_back(block, steps, rounds, queries, keys, values, features, grads, merged, logs, dq, dk, dv, bias):
    at = span(block * BLOCK, BLOCK)
    heads = queries.shape[1] // HD
    block_biases(block, steps, features, rounds, bias)
    ones = jnp.ones((8, HD), HALF)

    @pl.loop(0, heads)
    def _(head):
        part = span(head * HD, HD)
        query, grad = queries[at, part], grads[at, part]
        log_sum = logs[pl.ds(head, 1), at]
        product = grad.astype(FLOAT) * merged[at, part].astype(FLOAT)
        coarse = product.astype(HALF)
        fine = (product - coarse.astype(FLOAT)).astype(HALF)
        along = (times_transpose(ones, coarse) + times_transpose(ones, fine))[0:1]
        grad_query = jnp.zeros((HD, BLOCK), FLOAT)
        for step in range(steps):
            key_at = span((block - step) * BLOCK, BLOCK)
            key = keys[key_at, part]
            weights = jnp.exp2(times_transpose(key, query) * EXP_SCALE + bias[step] - log_sum)
            grad_probs = times_transpose(values[key_at, part], grad)
            grad_scores = (weights * (grad_probs - along)).astype(HALF)
            grad_value = times(weights.astype(HALF), grad)
            grad_key = times(grad_scores, query)
            if step == 0:
                dv[key_at, part] = grad_value
                dk[key_at, part] = grad_key
            else:
                dv[key_at, part] += grad_value
                dk[key_at, part] += grad_key
            grad_query = grad_query + contract_rows(key, grad_scores)
        dq[at, part] = grad_query.T


def finish_attention(queries, grads, logs, dq, dk, dv, grad_query, grad_value):
    length, width = queries.shape

    @pl.loop(0, length // BLOCK)
    def _(block):
        at = span(block * BLOCK, BLOCK)
        alone = jnp.where(logs[:, at] == -NEG, 1.0, 0.0).T
        for head in range(width // HD):
            part = slice(head * HD, (head + 1) * HD)
            grad_value[at, part] = (dv[at, part] + alone[:, head : head + 1] * grads[at, part].astype(FLOAT)).astype(HALF)
            query = queries[at, part].astype(FLOAT)
            key_scale = lax.rsqrt(jnp.sum(query * query, axis=-1, keepdims=True) + 1e-06)
            unit = query * key_scale
            grad_key = dk[at, part] * FACTOR
            key_along = jnp.sum(grad_key * unit, axis=-1, keepdims=True)
            grad_query[at, part] = (dq[at, part] * FACTOR + key_scale * (grad_key - unit * key_along)).astype(HALF)


def gelu_and_slope(hidden):
    square = hidden * hidden
    bend = jnp.tanh(math.sqrt(2.0 / math.pi) * hidden * (1.0 + 0.044715 * square))
    half_more = 0.5 + 0.5 * bend
    slope = half_more + 0.5 * hidden * (1.0 - bend * bend) * (
        math.sqrt(2.0 / math.pi) * (1.0 + 3.0 * 0.044715 * square)
    )
    return hidden * half_more, slope


def weight_grad(result, left, right, rows=None, add=False):
    width = 256
    height = result.shape[1] * result.shape[2] // right.shape[1]
    pieces = width // height
    rows = slice(None) if rows is None else rows

    @pl.loop(0, left.shape[1] // width)
    def _(index):
        block = contract_rows(left[rows, span(index * width, width)], right[rows, :])
        at = pl.ds(index * pieces, pieces)
        block = block.reshape(pieces, *result.shape[1:])
        if add:
            block = block + result[at].astype(FLOAT)
        result[at] = block.astype(result.dtype)


def ring_place(members, index):
    column, row = lax.rem(index, 2), lax.div(index, 2)
    return row + column * (members - 1 - 2 * row)


def ring_member(members, place):
    back = lax.div(place, members // 2)
    return 2 * place + back * (2 * (members - 1 - place) + 1 - 2 * place)


class Ring:
    def __init__(self, members, data, landed, result, sent, arrived, kept):
        self.members, self.data, self.landed, self.result = members, data, landed, result
        self.sent, self.arrived, self.kept, self.stage = sent, arrived, kept, 0
        self.here = ring_place(members, lax.axis_index("wide"))
        self.neighbours = (
            ring_member(members, lax.rem(self.here + 1, members)),
            ring_member(members, lax.rem(self.here + members - 1, members)),
        )

    def piece(self, direction, step):
        if direction == 0:
            return 2 * lax.rem(self.here - step + 2 * self.members, self.members)
        return 2 * lax.rem(self.here + step, self.members) + 1

    def copy(self, direction, step, at, gathering, fresh):
        index = direction * 2 * (self.members - 1) + step
        source = self.landed if gathering and not fresh else self.data
        return pltpu.make_async_remote_copy(
            src_ref=source.at[at],
            dst_ref=self.landed.at[at],
            send_sem=self.sent.at[index],
            recv_sem=self.arrived.at[index],
            device_id={"wide": self.neighbours[direction]},
            device_id_type=MESH,
        )

    def outgoing(self, direction, step, gathering=False, fresh=False):
        return self.copy(direction, step, self.piece(direction, step), gathering, fresh)

    def incoming(self, direction, step, gathering=False):
        return self.copy(direction, step, self.piece(direction, step + 1), gathering, False)

    def begin(self):
        for direction in range(2):
            self.outgoing(direction, 0).start()

    def add(self, direction, step):
        self.incoming(direction, step).wait_recv()
        at = self.piece(direction, step + 1)
        height = min(16, self.data.shape[1])

        @pl.loop(0, self.data.shape[1] // height)
        def _(index):
            rows = span(index * height, height)
            self.data[at, rows] = (
                self.data[at, rows].astype(FLOAT) + self.landed[at, rows].astype(FLOAT)
            ).astype(HALF)

        return at

    def keep(self, direction, step):
        at = self.piece(direction, step)
        source = self.data if isinstance(step, int) and step == self.members - 1 else self.landed
        return pltpu.make_async_copy(
            source.at[at], self.result.at[at], self.kept.at[direction * self.members + step - (self.members - 1)]
        )

    def advance(self):
        stage, last = self.stage, self.members - 1
        if stage == 14:
            return
        self.stage = stage + 1
        low, high = stage * 2 * last // 14, (stage + 1) * 2 * last // 14

        def repeat(begin, end, act):
            if end == begin + 1:
                act(begin)
            elif end > begin:
                pl.loop(begin, end)(act)

        def reduce(step):
            for direction in range(2):
                self.add(direction, step)
                self.outgoing(direction, step + 1).start()

        def forward(step):
            for direction in range(2):
                self.incoming(direction, step, True).wait_recv()
                self.outgoing(direction, step + 1, True).start()
                self.keep(direction, step + 1).start()

        repeat(low, min(high, last - 1), reduce)
        if low <= last - 1 < high:
            for direction in range(2):
                self.add(direction, last - 1)
                self.outgoing(direction, last, True, True).start()
                self.keep(direction, last).start()
        repeat(max(low, last), min(high, 2 * last - 1), forward)
        if low <= 2 * last - 1 < high:
            for direction in range(2):
                self.incoming(direction, 2 * last - 1, True).wait_recv()
                self.keep(direction, 2 * last).start()

    def finish(self):
        last = self.members - 1
        for direction in range(2):
            self.keep(direction, last).wait()
            self.outgoing(direction, last, True, True).wait_send()

        @pl.loop(0, last)
        def _(step):
            for direction in range(2):
                self.outgoing(direction, step).wait_send()

        @pl.loop(last + 1, 2 * last)
        def _(step):
            for direction in range(2):
                self.outgoing(direction, step, True).wait_send()
                self.keep(direction, step).wait()

        for direction in range(2):
            self.keep(direction, 2 * last).wait()


class Exchange:
    def __init__(self, members, data, landed, result, first, unit, bits, sems, stored):
        self.members, self.data, self.landed, self.result = members, data, landed, result
        self.first, self.unit, self.bits = first, unit, bits
        self.sent, self.arrived, self.stored, self.stage = *sems, stored, 0
        self.wide = lax.axis_index("wide")

    def bit(self, step):
        return lax.rem(lax.div(self.wide, 1 << self.bits[step]), 2)

    def size(self, step):
        return self.unit * (self.members >> (step + 1))

    def part(self, step, kept):
        start = self.first
        for before in range(step):
            start = start + self.bit(before) * self.size(before)
        bit = self.bit(step)
        return pl.ds(start + (bit if kept else 1 - bit) * self.size(step), self.size(step))

    def landing(self, step):
        return pl.ds(self.first + self.unit * self.members - 2 * self.size(step), self.size(step))

    def copy(self, step, gathering):
        index = step + gathering * len(self.bits)
        at = self.part(step, gathering)
        source = self.result if gathering and step < len(self.bits) - 1 else self.data
        return pltpu.make_async_remote_copy(
            src_ref=source.at[at],
            dst_ref=self.result.at[at] if gathering else self.landed.at[self.landing(step)],
            send_sem=self.sent.at[index],
            recv_sem=self.arrived.at[index],
            device_id={"wide": self.wide + (1 - 2 * self.bit(step)) * (1 << self.bits[step])},
            device_id_type=MESH,
        )

    def begin(self):
        self.copy(0, False).start()

    def advance(self):
        count, stage = len(self.bits), self.stage
        if stage == 2 * count:
            return
        self.stage = stage + 1
        if stage < count:
            self.copy(stage, False).wait_recv()
            kept, landed = self.part(stage, True), self.landing(stage)

            @pl.loop(0, self.size(stage))
            def _(index):
                at = kept.start + index
                self.data[at] = (
                    self.data[at].astype(FLOAT) + self.landed[landed.start + index].astype(FLOAT)
                ).astype(HALF)

        else:
            self.copy(2 * count - 1 - stage, True).wait_recv()
        if stage < count - 1:
            self.copy(stage + 1, False).start()
            return
        if stage == count - 1:
            self.store().start()
        if stage == count:
            self.store().wait()
        if stage < 2 * count - 1:
            self.copy(2 * count - 2 - stage, True).start()

    def store(self):
        at = self.part(len(self.bits) - 1, True)
        return pltpu.make_async_copy(self.data.at[at], self.result.at[at], self.stored)

    def finish(self):
        for step in range(len(self.bits)):
            self.copy(step, False).wait_send()
            self.copy(step, True).wait_send()


class Everyone:
    def __init__(self, axis, slots, sent, arrived):
        self.axis, self.slots, self.sent, self.arrived = axis, slots, sent, arrived
        self.me, self.members = lax.axis_index(axis), slots.shape[0]

    def copy(self, step):
        mine = self.slots.at[self.me]
        return pltpu.make_async_remote_copy(
            src_ref=mine,
            dst_ref=mine,
            send_sem=self.sent.at[step],
            recv_sem=self.arrived.at[step],
            device_id={self.axis: lax.rem(self.me + step, self.members)},
            device_id_type=MESH,
        )

    def send(self, value):
        self.slots[self.me] = value

        @pl.loop(1, self.members)
        def _(step):
            self.copy(step).start()

    def total(self):
        @pl.loop(1, self.members)
        def _(step):
            self.copy(step).wait()

        return lax.fori_loop(1, self.members, lambda index, total: total + self.slots[index], self.slots[0])


def advance(*exchanges):
    for exchange in exchanges:
        exchange.advance()


def greet_all(members):
    barrier = pltpu.get_barrier_semaphore()
    narrow, wide = lax.axis_index("narrow"), lax.axis_index("wide")

    @pl.loop(1, NARROW)
    def _(step):
        pl.semaphore_signal(
            barrier, inc=1, device_id={"narrow": lax.rem(narrow + step, NARROW)}, device_id_type=MESH
        )

    @pl.loop(1, members)
    def _(step):
        pl.semaphore_signal(barrier, inc=1, device_id={"wide": lax.rem(wide + step, members)}, device_id_type=MESH)

    return lambda: pl.semaphore_wait(barrier, NARROW - 1 + members - 1)


def layer(members, ref):
    place = Place()
    second_rows = ref.stream_two
    rows, width = second_rows.shape
    orders, docs = ref.orders, ref.docs
    rounds, length = orders.shape
    heads = ref.wq.shape[1]
    chunks = rows // CHUNK
    whole_one, whole_two, cotans, grad_rows = (ref.whole_one, ref.whole_two, ref.cotans, ref.grad_rows)
    queries, keys, values, merged, logs = (ref.queries, ref.keys, ref.values, ref.merged, ref.logs)
    features = (ref.query_features, ref.key_features)
    wq, wv, wo, up, down = (ref.wq, ref.wv, ref.wo, ref.up, ref.down)
    active, grad_hidden, middle, first_rows = (ref.active, ref.grad_hidden, ref.middle, ref.first_rows)
    grad_merged, bias, sums = ref.grad_merged, ref.bias, ref.sums
    dq, dk, dv = (ref.totals.at[pl.ds(i * length, length), :] for i in range(3))
    own_at, far_at = span(place.me * rows, rows), span(place.far * rows, rows)
    loads, stores = ref.loads, ref.stores

    def load(index, source, target):
        copy = pltpu.make_async_copy(source, target, loads.at[index])
        copy.start()
        return copy

    meet = greet_all(members)
    load_wq, load_wv = load(0, ref.wq_any, wq), load(1, ref.wv_any, wv)
    load_cotan = load(2, ref.cotan_two_any, cotans.at[own_at, :])
    load_wo, load_first = load(3, ref.wo_any, wo), load(4, ref.stream_one_any, first_rows)
    load_down, load_up = load(5, ref.down_any, down), load(6, ref.up_any, up)

    up_ring, down_ring = rings = [
        Ring(
            members, ref.sum_data[i], ref.sum_landed[i], ref.sum_results[i], ref.ring_sent.at[i], ref.ring_arrived.at[i],
            ref.ring_kept.at[i],
        )
        for i in range(2)
    ]
    bits = list(range(members.bit_length() - 1))
    swapped = bits[1::-1] + bits[2:]
    lanes = ((2, 0, bits), (2, members, swapped), (3, 0, bits), (3, members, swapped))
    out_sum, out_swap, in_sum, in_swap = exchanges = [
        Exchange(
            members, ref.sum_data[array], ref.sum_landed[array], ref.sum_results[array], first, 1, order,
            (ref.sum_sent.at[lane], ref.sum_arrived.at[lane]), ref.sum_stored.at[lane],
        )
        for lane, (array, first, order) in enumerate(lanes)
    ]
    queue = [up_ring, down_ring]

    def serve(*more):
        ring = queue.pop(0)
        queue.append(ring)
        advance(ring, *more)

    gather = Gather(place, whole_one, rows, (ref.gather_sent.at[0], ref.gather_arrived.at[0]))

    @pl.loop(0, chunks)
    def _(chunk):
        scaled, _ = normalize(second_rows[span(chunk * CHUNK, CHUNK), :].astype(FLOAT))
        normed = (scaled * ref.gain_one[...] + ref.shift_one[...]).astype(HALF)
        whole_one[span(place.me * rows + chunk * CHUNK, CHUNK), :] = normed

    meet()

    @pl.loop(0, chunks)
    def _(chunk):
        gather.send(chunk)

    pair_features(orders, docs, *features, bias)
    level = lax.broadcasted_iota(jnp.int32, (LANES, rows), 0)
    counted = jnp.ones((8, rows), HALF)
    sums[...] = jnp.zeros_like(sums)
    for index in range(rounds):
        found = jnp.where(level == ref.buckets[index : index + 1, :], 1.0, 0.0).astype(HALF)
        sums[4:5, index * LANES : (index + 1) * LANES] = times_transpose(counted, found)[0:1]
    load_wq.wait()
    load_wv.wait()

    def project(at):
        query = times(whole_one[at, :], wq[...]).astype(HALF)
        queries[at, :] = query
        for head in range(heads // HD):
            part = query[:, head * HD : (head + 1) * HD].astype(FLOAT)
            scale = lax.rsqrt(jnp.sum(part * part, axis=-1, keepdims=True) + 1e-06)
            keys[at, head * HD : (head + 1) * HD] = (part * scale).astype(HALF)
        values[at, :] = times(whole_one[at, :], wv[...]).astype(HALF)

    load_cotan.wait()
    spread = Gather(place, cotans, rows, (ref.gather_sent.at[1], ref.gather_arrived.at[1]))

    def send_cotangents():
        @pl.loop(0, chunks)
        def _(chunk):
            spread.send(chunk)

    by_arrival(gather, project, send_cotangents)
    gather.finish()

    steps = band_steps(length)
    blocks = length // BLOCK

    def forward(block, count):
        attend(block, count, rounds, queries, keys, values, features, merged, logs, bias, ref.totals)

    for block in range(steps - 1):
        forward(block, block + 1)

    @pl.loop(steps - 1, blocks)
    def _(block):
        forward(block, steps)

    buffers = (ref.near_out, ref.near_in, ref.far_out, ref.far_in)
    load_wo.wait()
    scatter = Scatter(
        place, lambda at: times(merged[at, :], wo[...]), rows, buffers, (ref.scatter_sent.at[0], ref.scatter_arrived.at[0])
    )
    scatter.start()
    load_first.wait()

    @pl.loop(0, chunks)
    def _(chunk):
        at = span(chunk * CHUNK, CHUNK)
        middle[at, :] = first_rows[at, :].astype(FLOAT) + scatter.chip_sum(chunk)

    @pl.loop(0, chunks)
    def _(chunk):
        spread.take_near(chunk)
        spread.take_far(chunk)

    load_down.wait()
    half_width = width // 2

    def grad_active(owner):
        @pl.loop(0, 2)
        def _(half):
            at = span(half * half_width, half_width)
            grad_hidden[span(owner * rows, rows), at] = times_transpose(
                cotans[span(owner * rows, rows), :], down[at, :]
            ).astype(HALF)

    @pl.loop(0, NARROW)
    def _(step):
        @pl.when(step == NARROW - 1)
        def _():
            @pl.loop(0, chunks)
            def _(chunk):
                spread.take_cross(chunk)

        grad_active(in_turn(place, step))

    gather = Gather(place, whole_two, rows, (ref.gather_sent.at[2], ref.gather_arrived.at[2]))
    load_up.wait()

    @pl.loop(0, chunks)
    def _(chunk):
        at = span(chunk * CHUNK, CHUNK)
        value = middle[at, :] + scatter.take_far(chunk)
        middle[at, :] = value
        first_rows[at, :] = value.astype(HALF)
        scaled, _ = normalize(value)
        whole_two[span(place.me * rows + chunk * CHUNK, CHUNK), :] = (
            scaled * ref.gain_two[...] + ref.shift_two[...]
        ).astype(HALF)
        gather.send(chunk)

    store_one = pltpu.make_async_copy(first_rows, ref.out_one, stores.at[0])
    store_one.start()

    def feed(row_at):
        @pl.loop(0, 2)
        def _(half):
            at = span(half * half_width, half_width)
            value, slope = gelu_and_slope(times(whole_two[row_at, :], up[:, at]) + ref.up_bias[:, at])
            active[row_at, at] = value.astype(HALF)
            grad_hidden[row_at, at] = (grad_hidden[row_at, at].astype(FLOAT) * slope).astype(HALF)

    chip = lax.div(place.me, 2)
    here, there = span(chip * 2 * rows, 2 * rows), span((1 - chip) * 2 * rows, 2 * rows)
    feed(span(place.me * rows, rows))

    @pl.loop(0, chunks)
    def _(chunk):
        gather.take_near(chunk)

    feed(span(place.near * rows, rows))
    weight_grad(ref.sum_data[1], active, cotans, here)
    weight_grad(ref.sum_data[0], whole_two, grad_hidden, here)
    by_chunk(gather, feed)
    scatter.finish()

    store_one.wait()
    load_cotan_one = load(7, ref.cotan_one_any, first_rows)
    scatter = Scatter(
        place,
        lambda at: times_transpose(grad_hidden[at, :], up[...]),
        rows,
        buffers,
        (ref.scatter_sent.at[1], ref.scatter_arrived.at[1]),
    )

    weight_grad(ref.sum_data[1], active, cotans, there, True)
    down_ring.begin()
    scatter.start()
    weight_grad(ref.sum_data[0], whole_two, grad_hidden, there, True)
    up_ring.begin()
    queue.reverse()
    back = Gather(place, grad_rows, rows, (ref.gather_sent.at[3], ref.gather_arrived.at[3]))
    load_cotan_one.wait()

    for chunk in range(chunks):
        at = span(chunk * CHUNK, CHUNK)
        grad_normed = scatter.chip_sum(chunk) + scatter.take_far(chunk)
        scaled, inverse = normalize(middle[at, :])
        grad = first_rows[at, :].astype(FLOAT) + norm_back(grad_normed, scaled, inverse, ref.gain_two[...])
        grad_rows[span(place.me * rows + chunk * CHUNK, CHUNK), :] = grad.astype(HALF)
        back.send(chunk)
        sums[2:3, :] += jnp.sum(grad_normed * scaled, axis=0, keepdims=True)
        sums[3:4, :] += jnp.sum(grad_normed, axis=0, keepdims=True)
        serve()
        serve()

    def merge_back(at):
        grad_merged[at, :] = times_transpose(grad_rows[at, :], wo[...]).astype(HALF)

    store_grad = pltpu.make_async_copy(grad_rows.at[own_at, :], ref.grad_one, stores.at[1])
    store_grad.start()
    own_sums = ref.wide_all.at[lax.axis_index(WIDE)]
    own_sums[5:6, :] = column_sums(grad_hidden[...])
    own_sums[6:7, :] = column_sums(cotans[...])
    scatter.finish()
    gather.finish()
    spread.finish()

    merge_back(span(place.me * rows, rows))
    serve()

    @pl.loop(0, chunks)
    def _(chunk):
        back.take_near(chunk)

    merge_back(span(place.near * rows, rows))
    serve()
    for chunk in range(chunks):
        back.take_far(chunk)
        merge_back(span(place.far * rows + chunk * CHUNK, CHUNK))
        back.take_cross(chunk)
        merge_back(span(place.cross * rows + chunk * CHUNK, CHUNK))
        serve()
    serve()
    weight_grad(ref.sum_data[2], merged, grad_rows)
    out_sum.begin()
    out_swap.begin()
    serve()

    fed = Scatter(
        place, lambda at: times(active[at, :], down[...]), rows, buffers, (ref.scatter_sent.at[2], ref.scatter_arrived.at[2])
    )
    fed.start()
    serve()

    def take_fed():
        @pl.loop(0, chunks)
        def _(chunk):
            at = span(chunk * CHUNK, CHUNK)
            total = fed.chip_sum(chunk) + fed.take_far(chunk) + ref.down_bias[...]
            cotans[span(place.near * rows + chunk * CHUNK, CHUNK), :] = (
                second_rows[at, :].astype(FLOAT) + total
            ).astype(HALF)

        store_two.start()
        fed.finish()
        for other in (place.near, place.far):
            pl.semaphore_signal(ref.ready, inc=1, device_id={"narrow": other}, device_id_type=MESH)

    store_two = pltpu.make_async_copy(cotans.at[span(place.near * rows, rows), :], ref.out_two, stores.at[2])

    for block in range(blocks):

        attend_back(
            block, min(block + 1, steps), rounds, queries, keys, values, features, grad_merged, merged, logs, dq, dk, dv, bias
        )
        serve()
        if block > 3:
            serve(out_sum, out_swap)
        if block == blocks - 2:
            take_fed()

    grad_query, grad_value = ref.grad_query, ref.grad_value
    finish_attention(queries, grad_merged, logs, dq, dk, dv, grad_query, grad_value)
    serve()
    weight_grad(ref.sum_data[3], whole_one, ref.grad_both)
    in_sum.begin()
    in_swap.begin()
    pl.semaphore_wait(ref.ready, 2)

    scatter = Scatter(
        place,
        lambda at: times_transpose(grad_query[at, :], wq[...]) + times_transpose(grad_value[at, :], wv[...]),
        rows,
        buffers,
        (ref.scatter_sent.at[3], ref.scatter_arrived.at[3]),
    )
    scatter.start()
    serve(out_sum, out_swap)
    serve()

    for chunk in range(chunks):
        at = span(chunk * CHUNK, CHUNK)
        grad_normed = scatter.chip_sum(chunk) + scatter.take_far(chunk)
        scaled, inverse = normalize(second_rows[at, :].astype(FLOAT))
        mine = span(place.me * rows + chunk * CHUNK, CHUNK)
        cotans[mine, :] = (
            cotans[mine, :].astype(FLOAT) + norm_back(grad_normed, scaled, inverse, ref.gain_one[...])
        ).astype(HALF)
        sums[0:1, :] += jnp.sum(grad_normed * scaled, axis=0, keepdims=True)
        sums[1:2, :] += jnp.sum(grad_normed, axis=0, keepdims=True)
        serve(in_swap, in_sum)
        serve(out_swap, out_sum)

    store_last = pltpu.make_async_copy(cotans.at[own_at, :], ref.grad_two, stores.at[3])
    store_last.start()
    over_narrow = Everyone("narrow", ref.narrow_all, ref.narrow_sent, ref.narrow_arrived)
    over_wide = Everyone("wide", ref.wide_all, ref.wide_sent, ref.wide_arrived)
    over_narrow.send(sums[...])
    serve(*exchanges)
    sums[...] = over_narrow.total()
    sums[5:7, :] = own_sums[5:7, :]
    over_wide.send(sums[...])
    while min(exchange.stage for exchange in exchanges) < 2 * len(bits) or min(ring.stage for ring in rings) < 14:
        serve(*exchanges)
    ref.small[...] = over_wide.total()
    scatter.finish()
    back.finish()
    for copy in (store_grad, store_two, store_last):
        copy.wait()
    for exchange in [*exchanges, *rings]:
        exchange.finish()


def pieces(members, shape):
    columns = shape[1] if members <= 8 else LANES
    return (2 * members, shape[0] * shape[1] // (2 * members * columns), columns)


def run_layer(members, args):
    rows, width = args.stream_two.shape
    length, heads, hidden = NARROW * rows, args.wq_any.shape[1], args.up_any.shape[1]
    rounds = args.orders.shape[0]
    chunks = rows // CHUNK
    depth = -(-(rounds * (length // GROUP) + args.docs.shape[0]) // LANES) * LANES
    weights = [(width, hidden), (hidden, width), (heads, width), (width, 2 * heads)]
    cut = [pieces(members, shape) for shape in weights]
    args = vars(args)
    in_specs = [IN_SMEM if k == DOCS else ANYWHERE if k.endswith(FROM_HBM) else IN_VMEM for k in args]
    outs = dict(
        out_one=((rows, width), HALF),
        out_two=((rows, width), HALF),
        grad_one=((rows, width), HALF),
        grad_two=((rows, width), HALF),
        small=((8, width), FLOAT),
    )
    out_shape = [jax.ShapeDtypeStruct(*o) for o in outs.values()] + [jax.ShapeDtypeStruct(shape, HALF) for shape in cut]
    out_specs = [ANYWHERE] * 4 + [IN_VMEM] + [ANYWHERE] * len(cut)
    tall = pltpu.VMEM((length, width), HALF)
    slim = pltpu.VMEM((length, heads), HALF)
    gather_sems, scatter_sems = DMA((4, 3 * chunks)), DMA((4, 3 * chunks))
    sum_sems = DMA((4, 2 * (members.bit_length() - 1)))
    ring_sems = DMA((2, 4 * (members - 1)))
    scratch = dict(
        whole_one=tall,
        whole_two=tall,
        cotans=tall,
        grad_rows=tall,
        active=pltpu.VMEM((length, hidden), HALF),
        grad_hidden=pltpu.VMEM((length, hidden), HALF),
        queries=slim,
        keys=slim,
        values=slim,
        merged=slim,
        grad_merged=slim,
        grad_both=pltpu.VMEM((length, 2 * heads), HALF),
        logs=pltpu.VMEM((8, length), FLOAT),
        query_features=pltpu.VMEM((depth, length), HALF),
        key_features=pltpu.VMEM((depth, length), HALF),
        wq=pltpu.VMEM((width, heads), HALF),
        wv=pltpu.VMEM((width, heads), HALF),
        wo=pltpu.VMEM((heads, width), HALF),
        up=pltpu.VMEM((width, hidden), HALF),
        down=pltpu.VMEM((hidden, width), HALF),
        middle=pltpu.VMEM((rows, width), FLOAT),
        first_rows=pltpu.VMEM((rows, width), HALF),
        bias=pltpu.VMEM((max(rounds, band_steps(length)), BLOCK, BLOCK), FLOAT),
        totals=pltpu.VMEM((3 * length, heads), FLOAT),
        sums=pltpu.VMEM((8, width), FLOAT),
        near_out=pltpu.VMEM((2, rows, width), HALF),
        near_in=pltpu.VMEM((2, rows, width), HALF),
        far_out=pltpu.VMEM((rows, width), HALF),
        far_in=pltpu.VMEM((rows, width), HALF),
        narrow_all=pltpu.VMEM((NARROW, 8, width), FLOAT),
        wide_all=pltpu.VMEM((members, 8, width), FLOAT),
        narrow_sent=DMA((NARROW,)),
        narrow_arrived=DMA((NARROW,)),
        wide_sent=DMA((members,)),
        wide_arrived=DMA((members,)),
        loads=DMA((8,)),
        stores=DMA((4,)),
        ready=pltpu.SemaphoreType.REGULAR,
        gather_sent=gather_sems,
        gather_arrived=gather_sems,
        scatter_sent=scatter_sems,
        scatter_arrived=scatter_sems,
        ring_sent=ring_sems,
        ring_arrived=ring_sems,
        ring_kept=DMA((2, 2 * members)),
        sum_sent=sum_sems,
        sum_arrived=sum_sems,
        sum_stored=DMA((4,)),
    )
    sum_buffers = [pltpu.VMEM(shape, HALF) for shape in cut]

    def kernel(*refs):
        count = len(args) + len(outs)
        named = dict(zip([*args, *outs], refs[:count]))
        results, rest = refs[count : count + len(cut)], refs[count + len(cut) :]
        named |= dict(zip(scratch, rest))
        rest = rest[len(scratch) :]
        ref = SimpleNamespace(**named, sum_results=results, sum_data=rest[: len(cut)], sum_landed=rest[len(cut) :])
        ref.grad_query = ref.grad_both.at[:, pl.ds(0, heads)]
        ref.grad_value = ref.grad_both.at[:, pl.ds(heads, heads)]
        layer(members, ref)

    found = pl.pallas_call(
        kernel,
        out_shape=out_shape,
        in_specs=in_specs,
        out_specs=out_specs,
        scratch_shapes=[*scratch.values(), *sum_buffers, *sum_buffers],
        compiler_params=pltpu.CompilerParams(collective_id=0, has_side_effects=True, vmem_limit_bytes=VMEM_LIMIT),
        name=layer.__name__,
    )(*args.values())
    sums = [result.reshape(shape) for result, shape in zip(found[len(outs) :], weights)]
    return SimpleNamespace(**dict(zip(outs, found))), sums


def finish(*refs):
    up, down, out, both, small, *rows = refs[:9]
    grad_up, grad_down, grad_out, grad_query, grad_value, *rest = refs[9:]
    heads = grad_query.shape[1]
    grad_up[...] = up[...].astype(FLOAT)
    grad_down[...] = down[...].astype(FLOAT)
    grad_out[...] = out[...].astype(FLOAT)
    grad_query[...] = both[:, :heads].astype(FLOAT)
    grad_value[...] = both[:, heads:].astype(FLOAT)
    for source, target in zip(rows, rest):
        target[...] = source[...]
    for source, target in zip((0, 1, 2, 3, 5, 6), rest[len(rows) :]):
        target[...] = small[source : source + 1, :]
    counts = rest[-1]
    for index in range(counts.shape[0]):
        counts[index : index + 1, :] = small[4:5, index * LANES : index * LANES + counts.shape[1]].astype(jnp.int32)


def run_finish(grads, small, rows, rounds):
    up, down, out, both = grads
    parts = 2
    vector = jax.ShapeDtypeStruct((1, small.shape[1]), FLOAT)
    taken = [up, down, out, both, small, *rows]
    given = [
        jax.ShapeDtypeStruct(up.shape, FLOAT),
        jax.ShapeDtypeStruct(down.shape, FLOAT),
        jax.ShapeDtypeStruct(out.shape, FLOAT),
        jax.ShapeDtypeStruct((both.shape[0], both.shape[1] // 2), FLOAT),
        jax.ShapeDtypeStruct((both.shape[0], both.shape[1] // 2), FLOAT),
        *[jax.ShapeDtypeStruct(r.shape, r.dtype) for r in rows],
        *[vector] * 6,
        jax.ShapeDtypeStruct((rounds, NB), jnp.int32),
    ]

    def spec(array):
        if array.shape[0] < LANES:
            return pl.BlockSpec(array.shape, lambda i: (0, 0))
        return pl.BlockSpec((array.shape[0] // parts, array.shape[1]), lambda i: (i, 0))

    return pl.pallas_call(
        finish,
        grid=(parts,),
        out_shape=given,
        in_specs=[spec(a) for a in taken],
        out_specs=[spec(a) for a in given],
        compiler_params=pltpu.CompilerParams(vmem_limit_bytes=VMEM_LIMIT),
        name=finish.__name__,
    )(*taken)


def per_device(
    stream_one,
    stream_two,
    attention_gain,
    attention_shift,
    query_proj,
    value_proj,
    output_proj,
    forward_gain,
    forward_shift,
    up_proj,
    up_bias,
    down_proj,
    down_bias,
    bucket_ids,
    sort_orders,
    doc_lengths,
    cotan_one,
    cotan_two,
):
    members = lax.axis_size("wide")
    row = lambda vector: vector.reshape(1, -1)
    found, grads = run_layer(
        members,
        SimpleNamespace(
            stream_one_any=stream_one,
            stream_two=stream_two,
            gain_one=row(attention_gain),
            shift_one=row(attention_shift),
            wq_any=query_proj,
            wv_any=value_proj,
            wo_any=output_proj,
            gain_two=row(forward_gain),
            shift_two=row(forward_shift),
            up_any=up_proj,
            up_bias=row(up_bias),
            down_any=down_proj,
            down_bias=row(down_bias),
            buckets=bucket_ids.T,
            orders=sort_orders[0],
            docs=doc_lengths[0],
            cotan_one_any=cotan_one,
            cotan_two_any=cotan_two,
        ),
    )
    rows = [found.out_one, found.out_two, found.grad_one, found.grad_two]
    grad_up, grad_down, grad_out, grad_query, grad_value, *rest = run_finish(
        grads, found.small, rows, sort_orders.shape[1]
    )
    gain_one, shift_one, gain_two, shift_two, bias_up, bias_down = [vector.reshape(-1) for vector in rest[4:10]]
    return (
        *rest[:4],
        gain_one,
        shift_one,
        grad_query,
        grad_value,
        grad_out,
        gain_two,
        shift_two,
        grad_up,
        bias_up,
        grad_down,
        bias_down,
        rest[10],
    )


def solution(mesh):
    rows = P(("wide", "narrow"), None)
    columns = P(None, "narrow")
    return jax.shard_map(
        per_device,
        mesh=mesh,
        in_specs=(
            rows,
            rows,
            P(),
            P(),
            columns,
            columns,
            P("narrow", None),
            P(),
            P(),
            columns,
            P("narrow"),
            P("narrow", None),
            P(),
            rows,
            P("wide", None, None),
            P("wide", None),
            rows,
            rows,
        ),
        out_specs=(
            rows,
            rows,
            rows,
            rows,
            P(),
            P(),
            columns,
            columns,
            P("narrow", None),
            P(),
            P(),
            columns,
            P("narrow"),
            P("narrow", None),
            P(),
            P(),
        ),
        check_vma=False,
    )
```
